32 devices in a mesh: ctx: 8 (over y, x, core), fsdp: 4 (over z).
Axes of the slice: x: 2, y: 2, z: 4, core: 2. Of those that a mesh axis runs over, the one named last changes fastest.
Arguments:
- inputs: bfloat16 [4, 1024, 2048], P('fsdp', 'ctx'), may hold values from -6 to 6
- gain: bfloat16 [2048], P('fsdp'), may hold values from 0.5 to 1.5
- bias: bfloat16 [2048], P('fsdp'), may hold values from -3 to 3
- in_weight: bfloat16 [2048, 17408], P('fsdp'), may hold values from -0.125 to 0.125
- out_weight: bfloat16 [7680, 2048], P('fsdp'), may hold values from -0.5524272 to 0.5524272
- grad_out: bfloat16 [4, 1024, 2048], P('fsdp', 'ctx'), may hold values from -6 to 6
- lengths: int32 [4, 4], P('fsdp'), may hold values from 1 to 512, 1024 in all within a row
- order: int32 [4, 16], P('fsdp'), may hold values from 0 to 15, each once within a row
Outputs:
- result: bfloat16 [4, 1024, 2048], P('fsdp', 'ctx')
- grad_in: bfloat16 [4, 1024, 2048], P('fsdp', 'ctx')
- in_weight_grad: float32 [2048, 17408], P('fsdp')
- out_weight_grad: float32 [7680, 2048], P('fsdp')
- gain_grad: float32 [2048], P('fsdp')
- bias_grad: float32 [2048], P('fsdp')
The draws below stay inside these ranges and needn't reach their ends.
Inputs may be any that keep to these rules, and one draw needn't show every extreme that they name: Each row holds 4 lengths summing to 1024, the largest exactly 512. `order`: each row names every block of the batch once.
All inputs are finite; a program needn't handle non-finite values.
Results may differ from the reference program's by a relative error of at most 0.012.
Values may be sent and summed in bfloat16 or wider, within the bound.
A program may use at most 576 MiB of HBM per device.

```python
import math
import jax
import jax.numpy as jnp
import numpy as np
from jax import lax

D = 2048
HEADS = 32
HEAD = 64
ROT = 16
FF = 5632
SEQS = 4
BLOCK = 64
BLOCKS = 16
GROUP_TOK = 1024
LONGEST = 512
BATCHES = 4


def draw_out_weight(key, part):
    row_ids = jnp.arange(D + FF, dtype=jnp.int32)
    scales = jnp.where(row_ids < D, 6.0 / math.sqrt(D), 1.0 / math.sqrt(FF)).astype(jnp.float32)
    normal_values = jnp.clip(jax.random.normal(key, (D + FF, D), jnp.float32), -4.0, 4.0)
    return (normal_values * scales[:, None]).astype(jnp.bfloat16)


def block_scale(own_key, extent, pieces, smallest, top_value):
    def one(dim, parts):
        heights = jax.random.uniform(jax.random.fold_in(jax.random.fold_in(own_key, 6), dim), (parts,), jnp.float32, smallest / len(pieces), top_value / len(pieces))
        return jnp.repeat(jnp.exp(heights), extent[dim] // parts).reshape((-1,) + (1,) * (len(extent) - dim - 1))

    loudness = one(*pieces[0])
    for cut in pieces[1:]:
        loudness = loudness * one(*cut)
    return loudness


def split_up(amount, total, most, slope):
    weights = [(1 << 20) // math.isqrt(grade ** slope) + 1 for grade in range(2, amount + 1)]
    rest, counts = total - most - (amount - 1), [1] * (amount - 1)
    while rest > 0:
        candidates = [i for i in range(amount - 1) if counts[i] < most]
        pool, budget = sum([weights[i] for i in candidates]), rest
        for i in candidates:
            addition = min(most - counts[i], max(1, budget * weights[i] // pool), rest)
            counts[i] = counts[i] + addition
            rest = rest - addition
    return np.array([most] + counts)


def ragged_sizes(own_key, amount, total, limit, skew):
    if amount == 2:
        one = jax.random.randint(own_key, (), max(1, total - limit), min(limit, total - 1) + 1)
        return jnp.stack([one, total - one])
    tallies = jnp.asarray(split_up(amount, total, limit, skew), jnp.int32)
    twos = (amount - 1) // 2
    source_of, sink = tallies[1:1 + 2 * twos:2], tallies[2:2 + 2 * twos:2]
    room = jnp.minimum(source_of - 1, limit - sink)
    shifted = jax.random.randint(jax.random.fold_in(own_key, 1), (twos,), 0, 1 << 20) % (room + 1)
    tallies = tallies.at[1:1 + 2 * twos:2].set(source_of - shifted).at[2:2 + 2 * twos:2].set(sink + shifted)
    return tallies[jax.random.permutation(jax.random.fold_in(own_key, 2), amount)]


def bell_draw(stream_key, dims, scale, limit, split=(), kind=jnp.bfloat16):
    values = jax.random.normal(stream_key, dims, jnp.float32) * scale
    if len(split) > 0:
        values = block_scale(stream_key, dims, split, -0.22, 0.18) * values
    return jnp.clip(values, min=-limit, max=limit).astype(kind)


def setup_inputs(seed: int = 0) -> dict:
    splits = jax.random.split(jax.random.key(seed), 9)
    return {
        "inputs": bell_draw(splits[0], (BATCHES, GROUP_TOK, D), 1.0, 6.0, ((0, 4), (1, 8))),
        "gain": jnp.clip(1.0 + 0.1 * jax.random.normal(splits[1], (D,), jnp.float32), 0.5, 1.5).astype(jnp.bfloat16),
        "bias": bell_draw(splits[2], (D,), 0.5, 3.0, ((0, 4),)),
        "in_weight": bell_draw(splits[3], (D, 3 * D + 2 * FF), D ** -0.5, 0.125, ((0, 4),)),
        "out_weight": draw_out_weight(jax.random.fold_in(splits[8], 71), 0),
        "grad_out": bell_draw(splits[5], (BATCHES, GROUP_TOK, D), 1.0, 6.0, ((0, 4), (1, 8))),
        "lengths": jax.vmap(lambda own: ragged_sizes(own, SEQS, GROUP_TOK, LONGEST, 2))(jax.random.split(splits[6], BATCHES)).reshape((BATCHES, SEQS)).astype(jnp.int32),
        "order": jax.vmap(lambda own: jax.random.permutation(own, BLOCKS))(jax.random.split(splits[7], BATCHES)).reshape((BATCHES, BLOCKS)).astype(jnp.int32),
    }


@jax.custom_vjp
def low(v):
    return lax.optimization_barrier(v.astype(jnp.bfloat16)).astype(jnp.float32)

@jax.custom_vjp
def low_back(v):
    return v

def low_keep(v):
    return (low(v), None)

def low_pass(kept, grad):
    return (grad,)

def back_keep(v):
    return (v, None)

def back_low(kept, grad):
    return (low(grad),)
low.defvjp(low_keep, low_pass)
low_back.defvjp(back_keep, back_low)

def hi_dot(left, right):
    return jnp.dot(left, right, precision=lax.Precision.HIGHEST, preferred_element_type=jnp.float32)

def places_of(index, length_row, order_row):
    count = order_row.shape[0]
    hit = (index // BLOCK)[:, None] == jnp.arange(count, dtype=jnp.int32)[None, :]
    block_id = lax.optimization_barrier(jnp.sum(jnp.where(hit, order_row[None, :], 0), axis=1)).astype(jnp.int32)
    place = (block_id * BLOCK + index % BLOCK).astype(jnp.int32)
    ends = jnp.cumsum(length_row).astype(jnp.int32)
    starts = (ends - length_row).astype(jnp.int32)
    inside = (place[:, None] >= starts[None, :]) & (place[:, None] < ends[None, :])
    docs = lax.optimization_barrier(jnp.sum(jnp.where(inside, jnp.arange(length_row.shape[0], dtype=jnp.int32)[None, :], 0), axis=1)).astype(jnp.int32)
    first = lax.optimization_barrier(jnp.sum(jnp.where(inside, starts[None, :], 0), axis=1)).astype(jnp.int32)
    return (place, docs, (place - first).astype(jnp.int32))

def rotate(values, positions, sign):
    half = ROT // 2
    freq = 10000.0 ** (-2.0 * jnp.arange(half, dtype=jnp.float32) / ROT)
    angle = positions.astype(jnp.float32)[:, None] * freq[None, :]
    cosine = jnp.cos(angle)[:, None, :]
    sine = sign * jnp.sin(angle)[:, None, :]
    first = values[..., :half]
    second = values[..., half:ROT]
    return jnp.concatenate([first * cosine - second * sine, second * cosine + first * sine, values[..., ROT:]], axis=-1)

def forward(inputs, gain, bias, in_weight, out_weight, places, docs, turns):
    width = inputs.shape[1]
    group = inputs.shape[0]
    centre = lax.optimization_barrier(jnp.mean(inputs, axis=1, keepdims=True))
    centred = inputs - centre
    spread = lax.optimization_barrier(jnp.mean(centred * centred, axis=1, keepdims=True))
    normed = centred * lax.rsqrt(spread + 1e-05)
    hidden_in = low(normed * gain + bias)
    joint = low_back(hi_dot(hidden_in, in_weight))
    shape = (group, HEADS, HEAD)
    queries = low(rotate(joint[:, :width].reshape(shape), turns, 1.0))
    keys = low(rotate(joint[:, width:2 * width].reshape(shape), turns, 1.0))
    values = low(joint[:, 2 * width:3 * width].reshape(shape))
    gate = joint[:, 3 * width:3 * width + FF]
    upward = joint[:, 3 * width + FF:]
    scale = HEAD ** (-0.5)
    qblock = math.gcd(group, 512)

    def attend(item):
        query_block, query_place, query_doc = item
        scores = low_back(jnp.einsum('qhd,khd->hqk', query_block, keys, precision=lax.Precision.HIGHEST) * scale)
        allowed = (query_doc[:, None] == docs[None, :]) & (places[None, :] <= query_place[:, None])
        weights = jnp.where(allowed[None], jnp.exp(scores), 0.0)
        totals = lax.optimization_barrier(jnp.sum(weights, axis=2))
        numer = low_back(jnp.einsum('hqk,khd->qhd', low(weights), values, precision=lax.Precision.HIGHEST))
        return numer / jnp.transpose(totals)[:, :, None]
    blocks = (queries.reshape(group // qblock, qblock, HEADS, HEAD), places.reshape(group // qblock, qblock), docs.reshape(group // qblock, qblock))
    attended = lax.map(jax.checkpoint(attend), blocks).reshape(group, width)
    activated = gate * jax.nn.sigmoid(gate) * upward
    mixed_in = jnp.concatenate([low(low_back(attended)), low(low_back(activated))], axis=1)
    return inputs + hi_dot(mixed_in, out_weight)

def reference(inputs, gain, bias, in_weight, out_weight, grad_out, lengths, order):
    params = (gain.astype(jnp.float32), bias.astype(jnp.float32), in_weight.astype(jnp.float32), out_weight.astype(jnp.float32))
    group = inputs.shape[1]

    def one_batch(carry, item):
        batch_in, batch_grad, length_row, order_row = item
        places, docs, turns = places_of(jnp.arange(group, dtype=jnp.int32), length_row, order_row)

        def layer(values_in, gain_value, bias_value, in_matrix, out_matrix):
            return forward(values_in, gain_value, bias_value, in_matrix, out_matrix, places, docs, turns)
        output, pull = jax.vjp(layer, batch_in.astype(jnp.float32), params[0], params[1], params[2], params[3])
        grads = pull(batch_grad.astype(jnp.float32))
        summed = tuple((total + part for total, part in zip(carry, grads[1:])))
        return (summed, (output.astype(jnp.bfloat16), grads[0].astype(jnp.bfloat16)))
    start = tuple((jnp.zeros(p.shape, jnp.float32) for p in params))
    totals, (outputs, grads_in) = lax.scan(one_batch, start, (inputs, grad_out, lengths, order))
    return (outputs, grads_in, totals[2], totals[3], totals[0], totals[1])
```

```python
import functools
import math

import jax
import jax.numpy as jnp
from jax import lax
from jax.experimental import pallas as pl
from jax.experimental.pallas import tpu as pltpu
from jax.sharding import PartitionSpec as P

HEADS = 32
HEAD = 64
ROT = 16
FF = 5632
BLOCK = 64
BF16 = jnp.bfloat16
F32 = jnp.float32
UNIT = 16


def places_of(index, length_row, order_row):
    count = order_row.shape[0]
    hit = (index // BLOCK)[:, None] == jnp.arange(count, dtype=jnp.int32)[None, :]
    block_id = jnp.sum(jnp.where(hit, order_row[None, :], 0), axis=1)
    place = block_id * BLOCK + index % BLOCK
    ends = jnp.cumsum(length_row)
    starts = ends - length_row
    inside = (place[:, None] >= starts[None, :]) & (place[:, None] < ends[None, :])
    docs = jnp.sum(
        jnp.where(inside, jnp.arange(length_row.shape[0], dtype=jnp.int32)[None, :], 0), axis=1
    )
    first = jnp.sum(jnp.where(inside, starts[None, :], 0), axis=1)
    return (place, docs, place - first)


def rotate(values, positions, sign):
    half = ROT // 2
    freq = 10000.0 ** (-2.0 * jnp.arange(half, dtype=jnp.float32) / ROT)
    angle = positions.astype(jnp.float32)[:, None] * freq[None, :]
    cosine = jnp.cos(angle)[:, None, :]
    sine = sign * jnp.sin(angle)[:, None, :]
    first = values[..., :half]
    second = values[..., half:ROT]
    return jnp.concatenate(
        [first * cosine - second * sine, second * cosine + first * sine, values[..., ROT:]], axis=-1
    )


def rounded(values):
    return lax.optimization_barrier(values.astype(jnp.bfloat16)).astype(jnp.float32)


def transposed_dot(left, right):
    return lax.dot_general(
        left, right, (((0,), (0,)), ((), ())), preferred_element_type=jnp.float32
    )


def against_rows(left, right):
    return lax.dot_general(
        left, right, (((1,), (1,)), ((), ())), preferred_element_type=jnp.float32
    )


def body(inputs, gain, bias, in_weight, out_weight, grad_out, lengths, order):
    rows = inputs.shape[1]
    width = inputs.shape[2]
    length_row = lengths[0]
    order_row = order[0]
    local_index = lax.axis_index("ctx") * rows + jnp.arange(rows, dtype=jnp.int32)
    query_place, query_doc, query_turn = places_of(local_index, length_row, order_row)
    scale = HEAD ** (-0.5)
    head_shape = (rows, HEADS, HEAD)
    values_in = inputs[0].astype(jnp.float32)
    centred = values_in - jnp.mean(values_in, axis=1, keepdims=True)
    inverse_std = lax.rsqrt(jnp.mean(centred * centred, axis=1, keepdims=True) + 1e-05)
    normed = centred * inverse_std
    weight_piece = lax.all_gather(in_weight, "fsdp", axis=0, tiled=True)
    gain_piece = lax.all_gather(gain, "fsdp", axis=0, tiled=True)
    bias_piece = lax.all_gather(bias, "fsdp", axis=0, tiled=True)
    count = weight_piece.shape[0]
    columns = normed
    hidden_piece = (
        columns * gain_piece.astype(jnp.float32) + bias_piece.astype(jnp.float32)
    ).astype(jnp.bfloat16)
    joint_sum = jnp.dot(hidden_piece, weight_piece, preferred_element_type=jnp.float32)
    gain_full = gain_piece.astype(jnp.float32)
    joint, hidden_in, gain_full = (joint_sum, hidden_piece, gain_full)
    queries = rotate(joint[:, :width].reshape(head_shape), query_turn, 1.0).astype(jnp.bfloat16)
    keys = (
        rotate(joint[:, width : 2 * width].reshape(head_shape), query_turn, 1.0)
        .astype(jnp.bfloat16)
        .reshape(rows, width)
    )
    values = joint[:, 2 * width : 3 * width].astype(jnp.bfloat16)
    gate = joint[:, 3 * width : 3 * width + FF]
    upward = joint[:, 3 * width + FF :]

    def exp_scores(key_block, start, count):
        key_place, key_doc, unused_turn = places_of(
            start + jnp.arange(count, dtype=jnp.int32), length_row, order_row
        )
        scores = (
            jnp.einsum(
                "qhd,khd->hqk",
                queries,
                key_block.reshape(count, HEADS, HEAD),
                preferred_element_type=jnp.float32,
            )
            * scale
        )
        allowed = (query_doc[:, None] == key_doc[None, :]) & (
            key_place[None, :] <= query_place[:, None]
        )
        return jnp.where(allowed[None], jnp.exp(scores), 0.0)

    empty_attention = (jnp.zeros(head_shape, jnp.float32), jnp.zeros((HEADS, rows), jnp.float32))
    key_piece = lax.all_gather(keys, "ctx", axis=0, tiled=True)
    value_piece = lax.all_gather(values, "ctx", axis=0, tiled=True)
    count = key_piece.shape[0]
    block_rows = math.gcd(count, 512)

    def add_block(j, state):
        numer, totals = state
        offset = j * block_rows
        key_block = lax.dynamic_slice_in_dim(key_piece, offset, block_rows, 0)
        value_block = lax.dynamic_slice_in_dim(value_piece, offset, block_rows, 0)
        weights = exp_scores(key_block, offset, block_rows)
        totals = totals + jnp.sum(weights, axis=2)
        numer = numer + jnp.einsum(
            "hqk,khd->qhd",
            weights.astype(jnp.bfloat16),
            value_block.reshape(block_rows, HEADS, HEAD),
            preferred_element_type=jnp.float32,
        )
        return (numer, totals)

    numer, totals = lax.fori_loop(0, count // block_rows, add_block, empty_attention)
    attended = numer / jnp.transpose(totals)[:, :, None]
    sigmoid_gate = jax.nn.sigmoid(gate)
    activated = gate * sigmoid_gate * upward
    mixed_in = jnp.concatenate(
        [attended.reshape(rows, width).astype(jnp.bfloat16), activated.astype(jnp.bfloat16)], axis=1
    )
    columns = mixed_in
    mixed = jnp.dot(
        columns,
        lax.all_gather(out_weight, "fsdp", axis=0, tiled=True),
        preferred_element_type=jnp.float32,
    )
    result = (values_in + mixed).astype(jnp.bfloat16)
    grad_rows = grad_out[0]
    grad_mixed = against_rows(grad_rows, lax.all_gather(out_weight, "fsdp", axis=0, tiled=True))
    grad_att = grad_mixed[:, :width].astype(jnp.bfloat16).reshape(head_shape)
    grad_act = rounded(grad_mixed[:, width:])
    grad_gate = grad_act * upward * sigmoid_gate * (1.0 + gate * (1.0 - sigmoid_gate))
    grad_up = grad_act * gate * sigmoid_gate
    delta = jnp.transpose(jnp.sum(grad_att.astype(jnp.float32) * attended, axis=2))
    grad_numer = (grad_att.astype(jnp.float32) / jnp.transpose(totals)[:, :, None]).astype(
        jnp.bfloat16
    )
    ratio = delta / totals
    keys_all, values_all = (
        lax.all_gather(keys, "ctx", axis=0, tiled=True),
        lax.all_gather(values, "ctx", axis=0, tiled=True),
    )
    group = keys_all.shape[0]

    def score_grads(key_block, value_block, start, count):
        weights = exp_scores(key_block, start, count)
        pushed = jnp.einsum(
            "qhd,khd->hqk",
            grad_numer,
            value_block.reshape(count, HEADS, HEAD),
            preferred_element_type=jnp.float32,
        )
        return (weights, (weights * (pushed - ratio[:, :, None])).astype(jnp.bfloat16))

    query_rows = math.gcd(group, 512)

    def query_block_grad(j, total):
        offset = j * query_rows
        key_block = lax.dynamic_slice_in_dim(keys_all, offset, query_rows, 0)
        value_block = lax.dynamic_slice_in_dim(values_all, offset, query_rows, 0)
        unused_weights, grad_scores = score_grads(key_block, value_block, offset, query_rows)
        return total + jnp.einsum(
            "hqk,khd->qhd",
            grad_scores,
            key_block.reshape(query_rows, HEADS, HEAD),
            preferred_element_type=jnp.float32,
        )

    grad_query = (
        lax.fori_loop(0, group // query_rows, query_block_grad, jnp.zeros(head_shape, jnp.float32))
        * scale
    )
    key_block_rows = math.gcd(rows * lax.axis_size("ctx"), 512)

    def key_block_grad(j, terms):
        offset = j * key_block_rows
        key_block = lax.dynamic_slice_in_dim(keys_all, offset, key_block_rows, 0)
        value_block = lax.dynamic_slice_in_dim(values_all, offset, key_block_rows, 0)
        weights, grad_scores = score_grads(key_block, value_block, offset, key_block_rows)
        key_part = (
            jnp.einsum("hqk,qhd->khd", grad_scores, queries, preferred_element_type=jnp.float32)
            * scale
        )
        value_part = jnp.einsum(
            "hqk,qhd->khd",
            weights.astype(jnp.bfloat16),
            grad_numer,
            preferred_element_type=jnp.float32,
        )
        block_terms = jnp.concatenate(
            [key_part.reshape(key_block_rows, width), value_part.reshape(key_block_rows, width)],
            axis=1,
        )
        return lax.dynamic_update_slice_in_dim(terms, block_terms, j * key_block_rows, 0)

    key_value_grad = lax.psum_scatter(
        lax.fori_loop(
            0,
            rows * lax.axis_size("ctx") // key_block_rows,
            key_block_grad,
            jnp.zeros((rows * lax.axis_size("ctx"), 2 * width), jnp.float32),
        ).astype(jnp.bfloat16),
        "ctx",
        scatter_dimension=0,
        tiled=True,
    ).astype(jnp.float32)
    grad_key = rotate(key_value_grad[:, :width].reshape(head_shape), query_turn, -1.0).reshape(
        rows, width
    )
    grad_query = rotate(grad_query, query_turn, -1.0).reshape(rows, width)
    grad_joint = jnp.concatenate(
        [
            grad_query.astype(jnp.bfloat16),
            grad_key.astype(jnp.bfloat16),
            key_value_grad[:, width:].astype(jnp.bfloat16),
            grad_gate.astype(jnp.bfloat16),
            grad_up.astype(jnp.bfloat16),
        ],
        axis=1,
    )
    grad_hidden = against_rows(grad_joint, lax.all_gather(in_weight, "fsdp", axis=0, tiled=True))
    grad_normed = grad_hidden * gain_full[None, :]
    grad_inputs = inverse_std * (
        grad_normed
        - jnp.mean(grad_normed, axis=1, keepdims=True)
        - normed * jnp.mean(grad_normed * normed, axis=1, keepdims=True)
    )
    grad_in = (grad_rows.astype(jnp.float32) + grad_inputs).astype(jnp.bfloat16)
    norm_terms = jnp.stack([jnp.sum(grad_hidden * normed, axis=0), jnp.sum(grad_hidden, axis=0)])
    norm_totals = lax.psum(norm_terms, ("ctx", "fsdp"))
    shards = lax.axis_size("fsdp")
    share = width // shards
    gain_grad = lax.dynamic_slice_in_dim(norm_totals[0], lax.axis_index("fsdp") * share, share, 0)
    bias_grad = lax.dynamic_slice_in_dim(norm_totals[1], lax.axis_index("fsdp") * share, share, 0)

    def column_terms(source, partner):
        return transposed_dot(source, partner)

    parts = lax.axis_size("ctx")

    def reorder(matrix):
        columns = matrix.shape[1]
        return (
            matrix.reshape(rows, shards, parts, columns // (shards * parts))
            .transpose(0, 2, 1, 3)
            .reshape(rows, columns)
        )

    in_piece = lax.psum_scatter(
        column_terms(reorder(hidden_in), grad_joint),
        ("ctx", "fsdp"),
        scatter_dimension=0,
        tiled=True,
    )
    out_piece = lax.psum_scatter(
        column_terms(reorder(mixed_in), grad_rows), ("ctx", "fsdp"), scatter_dimension=0, tiled=True
    )
    in_weight_grad, out_weight_grad = (
        lax.all_gather(in_piece.astype(jnp.bfloat16), "ctx", axis=0, tiled=True).astype(
            in_piece.dtype
        ),
        lax.all_gather(out_piece.astype(jnp.bfloat16), "ctx", axis=0, tiled=True).astype(
            out_piece.dtype
        ),
    )
    return (result[None], grad_in[None], in_weight_grad, out_weight_grad, gain_grad, bias_grad)


def flip(index, bit):
    return index + bit - 2 * bit * ((index // bit) % 2)


class Copies:
    def __init__(self, sems):
        self.sems = sems
        self.used = 0
        self.open = []

    def send(self, src, dst, recv_sem, target, when=None):
        copy = pltpu.make_async_remote_copy(
            src_ref=src,
            dst_ref=dst,
            send_sem=self.sems.at[self.used],
            recv_sem=recv_sem,
            device_id=target,
            device_id_type=pl.DeviceIdType.MESH,
        )
        self.used += 1
        self.open.append((copy.wait_send, when))
        if when is None:
            copy.start()
        else:
            pl.when(when)(copy.start)

    def local(self, src, dst):
        copy = pltpu.make_async_copy(src, dst, self.sems.at[self.used])
        self.used += 1
        copy.start()
        self.open.append((copy.wait, None))

    def finish(self):
        for done, when in self.open:
            if when is None:
                done()
            else:
                pl.when(when)(done)


def arrived(ref, recv_sem):
    pltpu.make_async_copy(ref, ref, recv_sem).wait()


def owner_of_unit(unit, att_units, ff_units, heads):
    first = heads * att_units
    is_att = (unit < first).astype(jnp.int32) if hasattr(unit, "astype") else int(unit < first)
    return is_att * (unit // att_units) + (1 - is_att) * ((unit - first) // ff_units)


def gather_kernel(
    sizes,
    x_ref, go_ref, gain_ref, bias_ref, table_ref, win_ref, wout_ref,
    go_all, hid_all, win_all, wout_all, table_all,
    gain_buf, bias_buf, hid_own, send_sems, block_sems, small_sems, win_sems, wout_sems,
):
    C, F = sizes
    c = lax.axis_index("ctx")
    f = lax.axis_index("fsdp")
    x_nbr, y_nbr, core = flip(c, 2), flip(c, 4), flip(c, 1)
    diag = flip(x_nbr, 4)
    copies = Copies(send_sems)
    here = {"ctx": c, "fsdp": f}

    def at_ctx(other):
        return {"ctx": other, "fsdp": f}

    def at_f(other):
        return {"ctx": c, "fsdp": other}

    barrier = pltpu.get_barrier_semaphore()
    others = [lax.rem(f + s, F) for s in range(1, F)]
    for peer in [at_ctx(x_nbr), at_ctx(y_nbr), at_ctx(core)] + [at_f(o) for o in others]:
        pl.semaphore_signal(barrier, inc=1, device_id=peer, device_id_type=pl.DeviceIdType.MESH)
    pl.semaphore_wait(barrier, 3 + F - 1)

    for i, o in enumerate(others):
        copies.send(gain_ref, gain_buf.at[f], small_sems.at[0, f], at_f(o))
        copies.send(bias_ref, bias_buf.at[f], small_sems.at[1, f], at_f(o))
        copies.send(table_ref, table_all.at[f], small_sems.at[2, f], at_f(o))
    copies.local(table_ref, table_all.at[f])

    outs = (go_all, hid_all)
    rows = x_ref.shape[0]
    half = rows // 2

    def piece(a, fb, cb, part):
        ref = outs[a].at[fb, cb]
        if part is None:
            return ref
        return ref.at[pl.ds(part * half, half)]

    def forward(a, fb, cb, part, target, when=None, src=None):
        ref = piece(a, fb, cb, part)
        copies.send(ref if src is None else src, ref, block_sems.at[a, fb, cb, part or 0], target, when)

    def wait_block(a, fb, cb, part, when=None):
        def go():
            arrived(piece(a, fb, cb, part), block_sems.at[a, fb, cb, part or 0])
        if when is None:
            go()
        else:
            pl.when(when)(go)

    up, down = f + 1 < F, f > 0

    def own(a, src):
        forward(a, f, c, None, at_ctx(x_nbr), src=src)
        forward(a, f, c, None, at_ctx(y_nbr), src=src)
        forward(a, f, c, None, at_f(f + 1), when=up, src=src)
        forward(a, f, c, None, at_f(f - 1), when=down, src=src)
        forward(a, f, c, None, at_ctx(core), src=src)
        copies.local(src, outs[a].at[f, c])

    own(0, go_ref)

    values = x_ref[...].astype(F32)
    centred = values - jnp.mean(values, axis=1, keepdims=True)
    normed = centred * lax.rsqrt(jnp.mean(centred * centred, axis=1, keepdims=True) + 1e-05)
    gain_buf[f] = gain_ref[...]
    bias_buf[f] = bias_ref[...]
    for o in others:
        arrived(gain_buf.at[o], small_sems.at[0, o])
        arrived(bias_buf.at[o], small_sems.at[1, o])
    share = gain_ref.shape[1]
    for s in range(F):
        cols = slice(s * share, (s + 1) * share)
        hid_own[:, cols] = (
            normed[:, cols] * gain_buf[s].astype(F32) + bias_buf[s].astype(F32)
        ).astype(BF16)
    own(1, hid_own)

    share_rows = win_ref.shape[2]

    def win_place(src_f):
        return win_all.at[:, pl.ds(pl.multiple_of(src_f * share_rows, share_rows), share_rows)]

    for o in others:
        copies.send(win_ref.at[o], win_place(f), win_sems.at[f], at_f(o))
    copies.local(win_ref.at[f], win_place(f))
    units_per_shard = wout_ref.shape[0] // UNIT
    att_units, ff_units = HEAD // UNIT * (HEADS // (C * F)), FF // (C * F) // UNIT

    def unit_of(rank, i):
        if i < att_units:
            return rank * att_units + i
        return C * F * att_units + rank * ff_units + (i - att_units)

    def unit_rows(ref, unit):
        return ref.at[pl.ds(pl.multiple_of(unit * UNIT, UNIT), UNIT)]

    for step in range(F):
        dest = lax.rem(f + step, F)
        rank = dest * C + c
        for i in range(att_units + ff_units):
            unit = unit_of(rank, i)
            mine = unit // units_per_shard == f
            src = unit_rows(wout_ref, lax.rem(unit, units_per_shard))
            dst = wout_all.at[pl.ds(i * UNIT, UNIT)]
            if step == 0:
                copy = pltpu.make_async_copy(src, dst, wout_sems.at[i])
                pl.when(mine)(copy.start)
            else:
                copies.send(src, dst, wout_sems.at[i], at_f(dest), when=mine)

    def z_step(s):
        for a in range(2):
            for sign in (-1, 1):
                fb = f + sign * s
                valid = (fb >= 0) if sign < 0 else (fb < F)
                onward = valid & (up if sign < 0 else down)
                wait_block(a, fb, c, None, when=valid)
                forward(a, fb, c, None, at_f(f - sign), when=onward)
                forward(a, fb, c, None, at_ctx(x_nbr), when=valid)
                forward(a, fb, c, None, at_ctx(y_nbr), when=valid)
                forward(a, fb, c, None, at_ctx(core), when=valid)

    def blocks_of(s):
        if s == 0:
            return [(f, None)]
        return [(f - s, f - s >= 0), (f + s, f + s < F)]

    def xy_step(s):
        for a in range(2):
            for fb, valid in blocks_of(s):
                wait_block(a, fb, x_nbr, None, when=valid)
                forward(a, fb, x_nbr, 0, at_ctx(y_nbr), when=valid)
                forward(a, fb, x_nbr, None, at_ctx(core), when=valid)
                wait_block(a, fb, y_nbr, None, when=valid)
                forward(a, fb, y_nbr, 1, at_ctx(x_nbr), when=valid)
                forward(a, fb, y_nbr, None, at_ctx(core), when=valid)

    def diag_step(s):
        for a in range(2):
            for fb, valid in blocks_of(s):
                for part in (0, 1):
                    wait_block(a, fb, diag, part, when=valid)
                    forward(a, fb, diag, part, at_ctx(core), when=valid)

    for s in range(F + 2):
        if 0 < s + 1 < F:
            z_step(s + 1)
        if s < F:
            xy_step(s)
        if 0 <= s - 1 < F:
            diag_step(s - 1)

    for a in range(2):
        for fb in range(F):
            wait_block(a, fb, core, None)
            wait_block(a, fb, flip(core, 2), None)
            wait_block(a, fb, flip(core, 4), None)
            for part in (0, 1):
                wait_block(a, fb, flip(flip(core, 2), 4), part)
    for o in others:
        arrived(win_place(o), win_sems.at[o])
        arrived(table_all.at[o], small_sems.at[2, o])
    for i in range(att_units + ff_units):
        arrived(wout_all.at[pl.ds(i * UNIT, UNIT)], wout_sems.at[i])
    copies.finish()


def gather_all(x, go, gain, bias, table, win, wout, C, F):
    rows, width = x.shape
    per_rank = win.shape[1]
    any_ = pl.BlockSpec(memory_space=pl.ANY)
    vmem = pl.BlockSpec(memory_space=pltpu.VMEM)
    wout_rows = HEAD * HEADS // (C * F) + FF // (C * F)
    share = gain.shape[1]
    return pl.pallas_call(
        functools.partial(gather_kernel, (C, F)),
        out_shape=(
            jax.ShapeDtypeStruct((F, C, rows, width), BF16),
            jax.ShapeDtypeStruct((F, C, rows, width), BF16),
            jax.ShapeDtypeStruct((per_rank, width), BF16),
            jax.ShapeDtypeStruct((wout_rows, width), BF16),
            jax.ShapeDtypeStruct((F,) + table.shape, jnp.int32),
        ),
        in_specs=[vmem, any_, vmem, vmem, any_, any_, any_],
        out_specs=(any_,) * 5,
        scratch_shapes=[
            pltpu.VMEM((F, 1, share), BF16),
            pltpu.VMEM((F, 1, share), BF16),
            pltpu.VMEM((rows, width), BF16),
            pltpu.SemaphoreType.DMA((256,)),
            pltpu.SemaphoreType.DMA((2, F, C, 2)),
            pltpu.SemaphoreType.DMA((3, F)),
            pltpu.SemaphoreType.DMA((F,)),
            pltpu.SemaphoreType.DMA((wout_rows // UNIT,)),
        ],
        compiler_params=pltpu.CompilerParams(collective_id=1, has_side_effects=True),
    )(x, go, gain, bias, table, win, wout)


def tp_body(C, F, inputs, gain, bias, in_weight, out_weight, grad_out, lengths, order):
    rows, width = inputs.shape[1:]
    T = C * F
    ff = FF // T
    scale = HEAD ** (-0.5)
    c = lax.axis_index("ctx")
    f = lax.axis_index("fsdp")
    x = inputs[0]
    go = grad_out[0]
    shard = in_weight.shape[0]

    slices = []
    for dest in range(F):
        rank = dest * C + c
        parts = [
            lax.dynamic_slice(in_weight, (0, base + rank * size), (shard, size))
            for base, size in (
                (0, HEAD), (width, HEAD), (2 * width, HEAD), (3 * width, ff), (3 * width + FF, ff)
            )
        ]
        slices.append(jnp.concatenate(parts, axis=1).T)
    win = jnp.stack(slices)
    count = lengths.shape[1] + order.shape[1]
    table = jnp.pad(jnp.concatenate([lengths, order], axis=1), ((0, 0), (0, 128 - count)))

    go_all, hid_all, w_in, w_out, tables = gather_all(
        x, go, gain[None], bias[None], table, win, out_weight, C, F
    )
    hidden = hid_all.reshape(T * rows, width)
    grads = go_all.reshape(T * rows, width)
    batch = C * rows
    lengths_all = tables[:, 0, : lengths.shape[1]]
    order_all = tables[:, 0, lengths.shape[1] : count]
    index = jnp.arange(batch, dtype=jnp.int32)
    place, doc, turn = jax.vmap(lambda l, o: places_of(index, l, o))(lengths_all, order_all)

    joint = lax.dot_general(hidden, w_in, (((1,), (1,)), ((), ())), preferred_element_type=F32)
    grad_mixed = lax.dot_general(grads, w_out, (((1,), (1,)), ((), ())), preferred_element_type=F32)
    turns = turn.reshape(-1)

    def turned(values, sign):
        return rotate(values[:, None, :], turns, sign)[:, 0, :]

    queries = turned(joint[:, :HEAD], 1.0).astype(BF16).reshape(F, batch, HEAD)
    keys = turned(joint[:, HEAD : 2 * HEAD], 1.0).astype(BF16).reshape(F, batch, HEAD)
    values = joint[:, 2 * HEAD : 3 * HEAD].astype(BF16).reshape(F, batch, HEAD)
    gate = joint[:, 3 * HEAD : 3 * HEAD + ff]
    upward = joint[:, 3 * HEAD + ff :]
    scores = jnp.einsum("bqd,bkd->bqk", queries, keys, preferred_element_type=F32) * scale
    allowed = (doc[:, :, None] == doc[:, None, :]) & (place[:, None, :] <= place[:, :, None])
    weights = jnp.where(allowed, jnp.exp(scores), 0.0)
    totals = jnp.sum(weights, axis=2)
    numer = jnp.einsum("bqk,bkd->bqd", weights.astype(BF16), values, preferred_element_type=F32)
    attended = numer / totals[:, :, None]
    sig = jax.nn.sigmoid(gate)
    activated = gate * sig * upward
    mixed = jnp.concatenate(
        [attended.reshape(-1, HEAD).astype(BF16), activated.astype(BF16)], axis=1
    )
    grad_att = grad_mixed[:, :HEAD].astype(BF16).reshape(F, batch, HEAD)
    grad_act = rounded(grad_mixed[:, HEAD:])
    grad_gate = grad_act * upward * sig * (1.0 + gate * (1.0 - sig))
    grad_up = grad_act * gate * sig
    delta = jnp.sum(grad_att.astype(F32) * attended, axis=2)
    grad_numer = (grad_att.astype(F32) / totals[:, :, None]).astype(BF16)
    ratio = delta / totals
    pushed = jnp.einsum("bqd,bkd->bqk", grad_numer, values, preferred_element_type=F32)
    grad_scores = (weights * (pushed - ratio[:, :, None])).astype(BF16)
    grad_q = jnp.einsum("bqk,bkd->bqd", grad_scores, keys, preferred_element_type=F32) * scale
    grad_k = jnp.einsum("bqk,bqd->bkd", grad_scores, queries, preferred_element_type=F32) * scale
    grad_v = jnp.einsum("bqk,bqd->bkd", weights.astype(BF16), grad_numer, preferred_element_type=F32)
    grad_joint = jnp.concatenate(
        [
            turned(grad_q.reshape(-1, HEAD), -1.0).astype(BF16),
            turned(grad_k.reshape(-1, HEAD), -1.0).astype(BF16),
            grad_v.reshape(-1, HEAD).astype(BF16),
            grad_gate.astype(BF16),
            grad_up.astype(BF16),
        ],
        axis=1,
    )
    both = ("fsdp", "ctx")
    part_out = jnp.dot(mixed, w_out, preferred_element_type=F32).astype(BF16)
    mixed_sum = lax.psum_scatter(part_out, both, scatter_dimension=0, tiled=True).astype(F32)
    part_hidden = jnp.dot(grad_joint, w_in, preferred_element_type=F32).astype(BF16)
    grad_hidden = lax.psum_scatter(part_hidden, both, scatter_dimension=0, tiled=True).astype(F32)

    values_in = x.astype(F32)
    centred = values_in - jnp.mean(values_in, axis=1, keepdims=True)
    inverse_std = lax.rsqrt(jnp.mean(centred * centred, axis=1, keepdims=True) + 1e-05)
    normed = centred * inverse_std
    result = (values_in + mixed_sum).astype(BF16)
    gain_full = lax.all_gather(gain, "fsdp", axis=0, tiled=True).astype(F32)
    grad_normed = grad_hidden * gain_full[None, :]
    grad_inputs = inverse_std * (
        grad_normed
        - jnp.mean(grad_normed, axis=1, keepdims=True)
        - normed * jnp.mean(grad_normed * normed, axis=1, keepdims=True)
    )
    grad_in = (go.astype(F32) + grad_inputs).astype(BF16)
    norm_terms = jnp.stack([jnp.sum(grad_hidden * normed, axis=0), jnp.sum(grad_hidden, axis=0)])
    norm_totals = lax.psum(norm_terms, ("ctx", "fsdp"))
    share = width // F
    gain_grad = lax.dynamic_slice_in_dim(norm_totals[0], f * share, share, 0)
    bias_grad = lax.dynamic_slice_in_dim(norm_totals[1], f * share, share, 0)

    dw_in = transposed_dot(grad_joint, hidden).astype(BF16)
    dw_out = transposed_dot(mixed, grads).astype(BF16)
    swapped = lax.all_to_all(dw_in.reshape(-1, F, share).transpose(1, 0, 2), "fsdp", 0, 0)
    spread = lax.all_gather(swapped, "ctx", axis=1)
    edges = (0, HEAD, 2 * HEAD, 3 * HEAD, 3 * HEAD + ff, 3 * HEAD + 2 * ff)
    in_weight_grad = jnp.concatenate(
        [
            spread[:, :, lo:hi].reshape(-1, share).T
            for lo, hi in zip(edges[:-1], edges[1:])
        ],
        axis=1,
    ).astype(F32)
    out_all = lax.all_gather(dw_out, both, axis=0)
    out_rows = jnp.concatenate(
        [out_all[:, :HEAD].reshape(-1, width), out_all[:, HEAD:].reshape(-1, width)], axis=0
    )
    per = out_weight.shape[0]
    out_weight_grad = lax.dynamic_slice_in_dim(out_rows, f * per, per, 0).astype(F32)
    return (result[None], grad_in[None], in_weight_grad, out_weight_grad, gain_grad, bias_grad)


def solution(mesh):
    in_specs = (
        P("fsdp", "ctx", None),
        P("fsdp"),
        P("fsdp"),
        P("fsdp", None),
        P("fsdp", None),
        P("fsdp", "ctx", None),
        P("fsdp", None),
        P("fsdp", None),
    )
    out_specs = (
        P("fsdp", "ctx", None),
        P("fsdp", "ctx", None),
        P("fsdp", None),
        P("fsdp", None),
        P("fsdp"),
        P("fsdp"),
    )
    C, F = mesh.shape["ctx"], mesh.shape["fsdp"]
    if (C, F) == (8, 4):
        work = functools.partial(tp_body, C, F)
    else:
        work = body
    return jax.shard_map(work, mesh=mesh, in_specs=in_specs, out_specs=out_specs, check_vma=False)
```

```python
import functools
import math

import jax
import jax.numpy as jnp
from jax import lax
from jax.experimental import pallas as pl
from jax.experimental.pallas import tpu as pltpu
from jax.sharding import PartitionSpec as P

HEADS = 32
HEAD = 64
ROT = 16
FF = 5632
BLOCK = 64
BF16 = jnp.bfloat16
F32 = jnp.float32
UNIT = 16


def places_of(index, length_row, order_row):
    count = order_row.shape[0]
    hit = (index // BLOCK)[:, None] == jnp.arange(count, dtype=jnp.int32)[None, :]
    block_id = jnp.sum(jnp.where(hit, order_row[None, :], 0), axis=1)
    place = block_id * BLOCK + index % BLOCK
    ends = jnp.cumsum(length_row)
    starts = ends - length_row
    inside = (place[:, None] >= starts[None, :]) & (place[:, None] < ends[None, :])
    docs = jnp.sum(
        jnp.where(inside, jnp.arange(length_row.shape[0], dtype=jnp.int32)[None, :], 0), axis=1
    )
    first = jnp.sum(jnp.where(inside, starts[None, :], 0), axis=1)
    return (place, docs, place - first)


def rotate(values, positions, sign):
    half = ROT // 2
    freq = 10000.0 ** (-2.0 * jnp.arange(half, dtype=jnp.float32) / ROT)
    angle = positions.astype(jnp.float32)[:, None] * freq[None, :]
    cosine = jnp.cos(angle)[:, None, :]
    sine = sign * jnp.sin(angle)[:, None, :]
    first = values[..., :half]
    second = values[..., half:ROT]
    return jnp.concatenate(
        [first * cosine - second * sine, second * cosine + first * sine, values[..., ROT:]], axis=-1
    )


def rounded(values):
    return lax.optimization_barrier(values.astype(jnp.bfloat16)).astype(jnp.float32)


def transposed_dot(left, right):
    return lax.dot_general(
        left, right, (((0,), (0,)), ((), ())), preferred_element_type=jnp.float32
    )


def against_rows(left, right):
    return lax.dot_general(
        left, right, (((1,), (1,)), ((), ())), preferred_element_type=jnp.float32
    )


def body(inputs, gain, bias, in_weight, out_weight, grad_out, lengths, order):
    rows = inputs.shape[1]
    width = inputs.shape[2]
    length_row = lengths[0]
    order_row = order[0]
    local_index = lax.axis_index("ctx") * rows + jnp.arange(rows, dtype=jnp.int32)
    query_place, query_doc, query_turn = places_of(local_index, length_row, order_row)
    scale = HEAD ** (-0.5)
    head_shape = (rows, HEADS, HEAD)
    values_in = inputs[0].astype(jnp.float32)
    centred = values_in - jnp.mean(values_in, axis=1, keepdims=True)
    inverse_std = lax.rsqrt(jnp.mean(centred * centred, axis=1, keepdims=True) + 1e-05)
    normed = centred * inverse_std
    weight_piece = lax.all_gather(in_weight, "fsdp", axis=0, tiled=True)
    gain_piece = lax.all_gather(gain, "fsdp", axis=0, tiled=True)
    bias_piece = lax.all_gather(bias, "fsdp", axis=0, tiled=True)
    count = weight_piece.shape[0]
    columns = normed
    hidden_piece = (
        columns * gain_piece.astype(jnp.float32) + bias_piece.astype(jnp.float32)
    ).astype(jnp.bfloat16)
    joint_sum = jnp.dot(hidden_piece, weight_piece, preferred_element_type=jnp.float32)
    gain_full = gain_piece.astype(jnp.float32)
    joint, hidden_in, gain_full = (joint_sum, hidden_piece, gain_full)
    queries = rotate(joint[:, :width].reshape(head_shape), query_turn, 1.0).astype(jnp.bfloat16)
    keys = (
        rotate(joint[:, width : 2 * width].reshape(head_shape), query_turn, 1.0)
        .astype(jnp.bfloat16)
        .reshape(rows, width)
    )
    values = joint[:, 2 * width : 3 * width].astype(jnp.bfloat16)
    gate = joint[:, 3 * width : 3 * width + FF]
    upward = joint[:, 3 * width + FF :]

    def exp_scores(key_block, start, count):
        key_place, key_doc, unused_turn = places_of(
            start + jnp.arange(count, dtype=jnp.int32), length_row, order_row
        )
        scores = (
            jnp.einsum(
                "qhd,khd->hqk",
                queries,
                key_block.reshape(count, HEADS, HEAD),
                preferred_element_type=jnp.float32,
            )
            * scale
        )
        allowed = (query_doc[:, None] == key_doc[None, :]) & (
            key_place[None, :] <= query_place[:, None]
        )
        return jnp.where(allowed[None], jnp.exp(scores), 0.0)

    empty_attention = (jnp.zeros(head_shape, jnp.float32), jnp.zeros((HEADS, rows), jnp.float32))
    key_piece = lax.all_gather(keys, "ctx", axis=0, tiled=True)
    value_piece = lax.all_gather(values, "ctx", axis=0, tiled=True)
    count = key_piece.shape[0]
    block_rows = math.gcd(count, 512)

    def add_block(j, state):
        numer, totals = state
        offset = j * block_rows
        key_block = lax.dynamic_slice_in_dim(key_piece, offset, block_rows, 0)
        value_block = lax.dynamic_slice_in_dim(value_piece, offset, block_rows, 0)
        weights = exp_scores(key_block, offset, block_rows)
        totals = totals + jnp.sum(weights, axis=2)
        numer = numer + jnp.einsum(
            "hqk,khd->qhd",
            weights.astype(jnp.bfloat16),
            value_block.reshape(block_rows, HEADS, HEAD),
            preferred_element_type=jnp.float32,
        )
        return (numer, totals)

    numer, totals = lax.fori_loop(0, count // block_rows, add_block, empty_attention)
    attended = numer / jnp.transpose(totals)[:, :, None]
    sigmoid_gate = jax.nn.sigmoid(gate)
    activated = gate * sigmoid_gate * upward
    mixed_in = jnp.concatenate(
        [attended.reshape(rows, width).astype(jnp.bfloat16), activated.astype(jnp.bfloat16)], axis=1
    )
    columns = mixed_in
    mixed = jnp.dot(
        columns,
        lax.all_gather(out_weight, "fsdp", axis=0, tiled=True),
        preferred_element_type=jnp.float32,
    )
    result = (values_in + mixed).astype(jnp.bfloat16)
    grad_rows = grad_out[0]
    grad_mixed = against_rows(grad_rows, lax.all_gather(out_weight, "fsdp", axis=0, tiled=True))
    grad_att = grad_mixed[:, :width].astype(jnp.bfloat16).reshape(head_shape)
    grad_act = rounded(grad_mixed[:, width:])
    grad_gate = grad_act * upward * sigmoid_gate * (1.0 + gate * (1.0 - sigmoid_gate))
    grad_up = grad_act * gate * sigmoid_gate
    delta = jnp.transpose(jnp.sum(grad_att.astype(jnp.float32) * attended, axis=2))
    grad_numer = (grad_att.astype(jnp.float32) / jnp.transpose(totals)[:, :, None]).astype(
        jnp.bfloat16
    )
    ratio = delta / totals
    keys_all, values_all = (
        lax.all_gather(keys, "ctx", axis=0, tiled=True),
        lax.all_gather(values, "ctx", axis=0, tiled=True),
    )
    group = keys_all.shape[0]

    def score_grads(key_block, value_block, start, count):
        weights = exp_scores(key_block, start, count)
        pushed = jnp.einsum(
            "qhd,khd->hqk",
            grad_numer,
            value_block.reshape(count, HEADS, HEAD),
            preferred_element_type=jnp.float32,
        )
        return (weights, (weights * (pushed - ratio[:, :, None])).astype(jnp.bfloat16))

    query_rows = math.gcd(group, 512)

    def query_block_grad(j, total):
        offset = j * query_rows
        key_block = lax.dynamic_slice_in_dim(keys_all, offset, query_rows, 0)
        value_block = lax.dynamic_slice_in_dim(values_all, offset, query_rows, 0)
        unused_weights, grad_scores = score_grads(key_block, value_block, offset, query_rows)
        return total + jnp.einsum(
            "hqk,khd->qhd",
            grad_scores,
            key_block.reshape(query_rows, HEADS, HEAD),
            preferred_element_type=jnp.float32,
        )

    grad_query = (
        lax.fori_loop(0, group // query_rows, query_block_grad, jnp.zeros(head_shape, jnp.float32))
        * scale
    )
    key_block_rows = math.gcd(rows * lax.axis_size("ctx"), 512)

    def key_block_grad(j, terms):
        offset = j * key_block_rows
        key_block = lax.dynamic_slice_in_dim(keys_all, offset, key_block_rows, 0)
        value_block = lax.dynamic_slice_in_dim(values_all, offset, key_block_rows, 0)
        weights, grad_scores = score_grads(key_block, value_block, offset, key_block_rows)
        key_part = (
            jnp.einsum("hqk,qhd->khd", grad_scores, queries, preferred_element_type=jnp.float32)
            * scale
        )
        value_part = jnp.einsum(
            "hqk,qhd->khd",
            weights.astype(jnp.bfloat16),
            grad_numer,
            preferred_element_type=jnp.float32,
        )
        block_terms = jnp.concatenate(
            [key_part.reshape(key_block_rows, width), value_part.reshape(key_block_rows, width)],
            axis=1,
        )
        return lax.dynamic_update_slice_in_dim(terms, block_terms, j * key_block_rows, 0)

    key_value_grad = lax.psum_scatter(
        lax.fori_loop(
            0,
            rows * lax.axis_size("ctx") // key_block_rows,
            key_block_grad,
            jnp.zeros((rows * lax.axis_size("ctx"), 2 * width), jnp.float32),
        ).astype(jnp.bfloat16),
        "ctx",
        scatter_dimension=0,
        tiled=True,
    ).astype(jnp.float32)
    grad_key = rotate(key_value_grad[:, :width].reshape(head_shape), query_turn, -1.0).reshape(
        rows, width
    )
    grad_query = rotate(grad_query, query_turn, -1.0).reshape(rows, width)
    grad_joint = jnp.concatenate(
        [
            grad_query.astype(jnp.bfloat16),
            grad_key.astype(jnp.bfloat16),
            key_value_grad[:, width:].astype(jnp.bfloat16),
            grad_gate.astype(jnp.bfloat16),
            grad_up.astype(jnp.bfloat16),
        ],
        axis=1,
    )
    grad_hidden = against_rows(grad_joint, lax.all_gather(in_weight, "fsdp", axis=0, tiled=True))
    grad_normed = grad_hidden * gain_full[None, :]
    grad_inputs = inverse_std * (
        grad_normed
        - jnp.mean(grad_normed, axis=1, keepdims=True)
        - normed * jnp.mean(grad_normed * normed, axis=1, keepdims=True)
    )
    grad_in = (grad_rows.astype(jnp.float32) + grad_inputs).astype(jnp.bfloat16)
    norm_terms = jnp.stack([jnp.sum(grad_hidden * normed, axis=0), jnp.sum(grad_hidden, axis=0)])
    norm_totals = lax.psum(norm_terms, ("ctx", "fsdp"))
    shards = lax.axis_size("fsdp")
    share = width // shards
    gain_grad = lax.dynamic_slice_in_dim(norm_totals[0], lax.axis_index("fsdp") * share, share, 0)
    bias_grad = lax.dynamic_slice_in_dim(norm_totals[1], lax.axis_index("fsdp") * share, share, 0)

    def column_terms(source, partner):
        return transposed_dot(source, partner)

    parts = lax.axis_size("ctx")

    def reorder(matrix):
        columns = matrix.shape[1]
        return (
            matrix.reshape(rows, shards, parts, columns // (shards * parts))
            .transpose(0, 2, 1, 3)
            .reshape(rows, columns)
        )

    in_piece = lax.psum_scatter(
        column_terms(reorder(hidden_in), grad_joint),
        ("ctx", "fsdp"),
        scatter_dimension=0,
        tiled=True,
    )
    out_piece = lax.psum_scatter(
        column_terms(reorder(mixed_in), grad_rows), ("ctx", "fsdp"), scatter_dimension=0, tiled=True
    )
    in_weight_grad, out_weight_grad = (
        lax.all_gather(in_piece.astype(jnp.bfloat16), "ctx", axis=0, tiled=True).astype(
            in_piece.dtype
        ),
        lax.all_gather(out_piece.astype(jnp.bfloat16), "ctx", axis=0, tiled=True).astype(
            out_piece.dtype
        ),
    )
    return (result[None], grad_in[None], in_weight_grad, out_weight_grad, gain_grad, bias_grad)


def flip(index, bit):
    return index + bit - 2 * bit * ((index // bit) % 2)


class Copies:
    def __init__(self, sems):
        self.sems = sems
        self.used = 0
        self.open = []

    def send(self, src, dst, recv_sem, target, when=None):
        copy = pltpu.make_async_remote_copy(
            src_ref=src,
            dst_ref=dst,
            send_sem=self.sems.at[self.used],
            recv_sem=recv_sem,
            device_id=target,
            device_id_type=pl.DeviceIdType.MESH,
        )
        self.used += 1
        self.open.append((copy.wait_send, when))
        if when is None:
            copy.start()
        else:
            pl.when(when)(copy.start)

    def local(self, src, dst, when=None):
        copy = pltpu.make_async_copy(src, dst, self.sems.at[self.used])
        self.used += 1
        if when is None:
            copy.start()
        else:
            pl.when(when)(copy.start)
        self.open.append((copy.wait, when))

    def finish(self):
        for done, when in self.open:
            if when is None:
                done()
            else:
                pl.when(when)(done)


def arrived(ref, recv_sem):
    pltpu.make_async_copy(ref, ref, recv_sem).wait()


def owner_of_unit(unit, att_units, ff_units, heads):
    first = heads * att_units
    is_att = (unit < first).astype(jnp.int32) if hasattr(unit, "astype") else int(unit < first)
    return is_att * (unit // att_units) + (1 - is_att) * ((unit - first) // ff_units)


def gather_kernel(
    sizes,
    x_ref, go_ref, gain_ref, bias_ref, table_ref, win_ref, wout_ref,
    go_all, hid_all, win_all, wout_all, table_all, gain_buf,
    bias_buf, hid_own, send_sems, block_sems, small_sems, win_sems, wout_sems,
):
    C, F = sizes
    c = lax.axis_index("ctx")
    f = lax.axis_index("fsdp")
    x_nbr, y_nbr, core = flip(c, 2), flip(c, 4), flip(c, 1)
    diag = flip(x_nbr, 4)
    copies = Copies(send_sems)
    here = {"ctx": c, "fsdp": f}

    def at_ctx(other):
        return {"ctx": other, "fsdp": f}

    def at_f(other):
        return {"ctx": c, "fsdp": other}

    barrier = pltpu.get_barrier_semaphore()
    others = [lax.rem(f + s, F) for s in range(1, F)]
    for peer in [at_ctx(x_nbr), at_ctx(y_nbr), at_ctx(core)] + [at_f(o) for o in others]:
        pl.semaphore_signal(barrier, inc=1, device_id=peer, device_id_type=pl.DeviceIdType.MESH)
    pl.semaphore_wait(barrier, 3 + F - 1)

    for i, o in enumerate(others):
        copies.send(gain_ref, gain_buf.at[f], small_sems.at[0, f], at_f(o))
        copies.send(bias_ref, bias_buf.at[f], small_sems.at[1, f], at_f(o))
        copies.send(table_ref, table_all.at[f], small_sems.at[2, f], at_f(o))
    copies.local(table_ref, table_all.at[f])

    outs = (go_all, hid_all)
    rows = x_ref.shape[0]
    half = rows // 2

    def piece(a, fb, cb, part):
        ref = outs[a].at[fb, cb]
        if part is None:
            return ref
        return ref.at[pl.ds(part * half, half)]

    def forward(a, fb, cb, part, target, when=None, src=None):
        ref = piece(a, fb, cb, part)
        copies.send(ref if src is None else src, ref, block_sems.at[a, fb, cb, part or 0], target, when)

    def wait_block(a, fb, cb, part, when=None):
        def go():
            arrived(piece(a, fb, cb, part), block_sems.at[a, fb, cb, part or 0])
        if when is None:
            go()
        else:
            pl.when(when)(go)

    up, down = f + 1 < F, f > 0

    def own(a, src):
        forward(a, f, c, None, at_ctx(x_nbr), src=src)
        forward(a, f, c, None, at_ctx(y_nbr), src=src)
        forward(a, f, c, None, at_f(f + 1), when=up, src=src)
        forward(a, f, c, None, at_f(f - 1), when=down, src=src)
        forward(a, f, c, None, at_ctx(core), src=src)
        copies.local(src, outs[a].at[f, c])

    own(0, go_ref)

    values = x_ref[...].astype(F32)
    centred = values - jnp.mean(values, axis=1, keepdims=True)
    normed = centred * lax.rsqrt(jnp.mean(centred * centred, axis=1, keepdims=True) + 1e-05)
    gain_buf[f] = gain_ref[...]
    bias_buf[f] = bias_ref[...]
    for o in others:
        arrived(gain_buf.at[o], small_sems.at[0, o])
        arrived(bias_buf.at[o], small_sems.at[1, o])
    share = gain_ref.shape[1]
    for s in range(F):
        cols = slice(s * share, (s + 1) * share)
        hid_own[:, cols] = (
            normed[:, cols] * gain_buf[s].astype(F32) + bias_buf[s].astype(F32)
        ).astype(BF16)
    own(1, hid_own)

    share_rows = win_ref.shape[2]

    def win_place(src_f):
        return win_all.at[:, pl.ds(pl.multiple_of(src_f * share_rows, share_rows), share_rows)]

    for o in others:
        copies.send(win_ref.at[o], win_place(f), win_sems.at[f], at_f(o))
    copies.local(win_ref.at[f], win_place(f))
    units_per_shard = wout_ref.shape[0] // UNIT
    att_units, ff_units = HEAD // UNIT * (HEADS // (C * F)), FF // (C * F) // UNIT

    def unit_of(rank, i):
        if i < att_units:
            return rank * att_units + i
        return C * F * att_units + rank * ff_units + (i - att_units)

    def unit_rows(ref, unit):
        return ref.at[pl.ds(pl.multiple_of(unit * UNIT, UNIT), UNIT)]

    for step in range(F):
        dest = lax.rem(f + step, F)
        rank = dest * C + c
        for i in range(att_units + ff_units):
            unit = unit_of(rank, i)
            mine = unit // units_per_shard == f
            src = unit_rows(wout_ref, lax.rem(unit, units_per_shard))
            dst = wout_all.at[pl.ds(i * UNIT, UNIT)]
            if step == 0:
                copy = pltpu.make_async_copy(src, dst, wout_sems.at[i])
                pl.when(mine)(copy.start)
            else:
                copies.send(src, dst, wout_sems.at[i], at_f(dest), when=mine)

    def z_step(s):
        for a in range(2):
            for sign in (-1, 1):
                fb = f + sign * s
                valid = (fb >= 0) if sign < 0 else (fb < F)
                onward = valid & (up if sign < 0 else down)
                wait_block(a, fb, c, None, when=valid)
                forward(a, fb, c, None, at_f(f - sign), when=onward)
                forward(a, fb, c, None, at_ctx(x_nbr), when=valid)
                forward(a, fb, c, None, at_ctx(y_nbr), when=valid)
                forward(a, fb, c, None, at_ctx(core), when=valid)

    def blocks_of(s):
        if s == 0:
            return [(f, None)]
        return [(f - s, f - s >= 0), (f + s, f + s < F)]

    def xy_step(s):
        for a in range(2):
            for fb, valid in blocks_of(s):
                wait_block(a, fb, x_nbr, None, when=valid)
                forward(a, fb, x_nbr, 0, at_ctx(y_nbr), when=valid)
                forward(a, fb, x_nbr, None, at_ctx(core), when=valid)
                wait_block(a, fb, y_nbr, None, when=valid)
                forward(a, fb, y_nbr, 1, at_ctx(x_nbr), when=valid)
                forward(a, fb, y_nbr, None, at_ctx(core), when=valid)

    def diag_step(s):
        for a in range(2):
            for fb, valid in blocks_of(s):
                for part in (0, 1):
                    wait_block(a, fb, diag, part, when=valid)
                    forward(a, fb, diag, part, at_ctx(core), when=valid)

    for s in range(F + 2):
        if 0 < s + 1 < F:
            z_step(s + 1)
        if s < F:
            xy_step(s)
        if 0 <= s - 1 < F:
            diag_step(s - 1)

    for a in range(2):
        for fb in range(F):
            wait_block(a, fb, core, None)
            wait_block(a, fb, flip(core, 2), None)
            wait_block(a, fb, flip(core, 4), None)
            for part in (0, 1):
                wait_block(a, fb, flip(flip(core, 2), 4), part)
    for o in others:
        arrived(win_place(o), win_sems.at[o])
        arrived(table_all.at[o], small_sems.at[2, o])
    for i in range(att_units + ff_units):
        arrived(wout_all.at[pl.ds(i * UNIT, UNIT)], wout_sems.at[i])
    copies.finish()


def gather_all(x, go, gain, bias, table, win, wout, C, F):
    rows, width = x.shape
    per_rank = win.shape[1]
    any_ = pl.BlockSpec(memory_space=pl.ANY)
    vmem = pl.BlockSpec(memory_space=pltpu.VMEM)
    wout_rows = HEAD * HEADS // (C * F) + FF // (C * F)
    share = gain.shape[1]
    return pl.pallas_call(
        functools.partial(gather_kernel, (C, F)),
        out_shape=(
            jax.ShapeDtypeStruct((F, C, rows, width), BF16),
            jax.ShapeDtypeStruct((F, C, rows, width), BF16),
            jax.ShapeDtypeStruct((per_rank, width), BF16),
            jax.ShapeDtypeStruct((wout_rows, width), BF16),
            jax.ShapeDtypeStruct((F,) + table.shape, jnp.int32),
            jax.ShapeDtypeStruct((F, 1, share), BF16),
        ),
        in_specs=[vmem, any_, vmem, vmem, any_, any_, any_],
        out_specs=(any_,) * 5 + (vmem,),
        scratch_shapes=[
            pltpu.VMEM((F, 1, share), BF16),
            pltpu.VMEM((rows, width), BF16),
            pltpu.SemaphoreType.DMA((256,)),
            pltpu.SemaphoreType.DMA((2, F, C, 2)),
            pltpu.SemaphoreType.DMA((3, F)),
            pltpu.SemaphoreType.DMA((F,)),
            pltpu.SemaphoreType.DMA((wout_rows // UNIT,)),
        ],
        compiler_params=pltpu.CompilerParams(collective_id=1, has_side_effects=True),
    )(x, go, gain, bias, table, win, wout)


def reduce_kernel(
    sizes,
    a_out_ref, w_out_ref, a_in_ref, w_in_ref, x_ref, go_ref, gain_ref,
    result_ref, grad_in_ref, terms_ref,
    core_send, core_recv, x_send, y_send, x_recv, y_recv, keep_l, keep_r,
    y2_send, x2_send, y2_recv, x2_recv, z_send, z_recv,
    send_sems, core_sems, xy_sems, xy2_sems, z_sems, credit,
):
    C, F = sizes
    c = lax.axis_index("ctx")
    f = lax.axis_index("fsdp")
    x_nbr, y_nbr, core = flip(c, 2), flip(c, 4), flip(c, 1)
    rows, width = x_ref.shape
    mid = width // 2
    tile = 256
    others = [lax.rem(f + s, F) for s in range(1, F)]
    mesh_id = pl.DeviceIdType.MESH

    def at_ctx(other):
        return {"ctx": other, "fsdp": f}

    def at_f(other):
        return {"ctx": c, "fsdp": other}

    barrier = pltpu.get_barrier_semaphore()
    for peer in [at_ctx(x_nbr), at_ctx(y_nbr), at_ctx(core)] + [at_f(o) for o in others]:
        pl.semaphore_signal(barrier, inc=1, device_id=peer, device_id_type=mesh_id)
    pl.semaphore_wait(barrier, 3 + F - 1)

    steps = 2 * F
    open_sends = {}

    def send(key, t, src, dst, recv_sem, target):
        copy = pltpu.make_async_remote_copy(
            src_ref=src, dst_ref=dst, send_sem=send_sems.at[key, t], recv_sem=recv_sem,
            device_id=target, device_id_type=mesh_id,
        )
        copy.start()
        open_sends[key, t] = copy

    def sent(key, t):
        if (key, t) in open_sends:
            open_sends.pop((key, t)).wait_send()

    def operands(t):
        return (a_out_ref, w_out_ref) if t < F else (a_in_ref, w_in_ref)

    def dest_of(t):
        return lax.rem(f + 1 + t % F, F)

    def left_rows(t, base):
        a_ref = operands(t)[0]
        block = dest_of(t) * C
        return jnp.concatenate(
            [
                a_ref[pl.ds(pl.multiple_of((block + cc) * rows, rows), rows), :]
                for cc in (base, flip(base, 2), flip(base, 4), flip(flip(base, 2), 4))
            ],
            axis=0,
        )

    def for_core(t):
        if t >= F:
            pl.semaphore_wait(credit, 1)
        sent(0, t - 2)
        left = left_rows(t, core)
        w_ref = operands(t)[1]

        @pl.loop(0, width // tile)
        def _(n):
            cols = pl.ds(pl.multiple_of(n * tile, tile), tile)
            core_send[t % 2, :, cols] = jnp.dot(
                left, w_ref[:, cols], preferred_element_type=F32
            ).astype(BF16)

        send(0, t, core_send.at[t % 2], core_recv.at[t % F], core_sems.at[t], at_ctx(core))

    def first(t):
        left = left_rows(t, c)
        w_ref = operands(t)[1]
        arrived(core_recv.at[t % F], core_sems.at[t])
        sent(1, t - 2)
        sent(2, t - 2)
        for side, keep, out, kept, sent_rows in (
            (0, keep_l, x_send, (0, 2), (1, 3)),
            (1, keep_r, y_send, (0, 1), (2, 3)),
        ):
            @pl.loop(0, mid // tile)
            def _(n):
                near = pl.ds(pl.multiple_of(n * tile, tile), tile)
                cols = pl.ds(pl.multiple_of(side * mid + n * tile, tile), tile)
                total = jnp.dot(left, w_ref[:, cols], preferred_element_type=F32)
                total = total + core_recv[t % F, :, cols].astype(F32)
                for i, b in enumerate(kept):
                    keep[t % 3, i * rows : (i + 1) * rows, near] = total[b * rows : (b + 1) * rows]
                for i, b in enumerate(sent_rows):
                    out[t % 2, i * rows : (i + 1) * rows, near] = total[
                        b * rows : (b + 1) * rows
                    ].astype(BF16)

            if side == 0:
                send(1, t, x_send.at[t % 2], x_recv.at[t], xy_sems.at[0, t], at_ctx(x_nbr))
            else:
                send(2, t, y_send.at[t % 2], y_recv.at[t], xy_sems.at[1, t], at_ctx(y_nbr))
        if t + F < steps:
            pl.semaphore_signal(credit, inc=1, device_id=at_ctx(core), device_id_type=mesh_id)

    def second(t):
        for key, keep, recv, sem, out, out_recv, target in (
            (3, keep_l, x_recv, 0, y2_send, y2_recv, y_nbr),
            (4, keep_r, y_recv, 1, x2_send, x2_recv, x_nbr),
        ):
            arrived(recv.at[t], xy_sems.at[sem, t])
            sent(key, t - 2)
            out[t % 2] = (keep[t % 3, rows:] + recv[t, rows:].astype(F32)).astype(BF16)
            send(key, t, out.at[t % 2], out_recv.at[t], xy2_sems.at[sem, t], at_ctx(target))
            keep[t % 3, :rows] = keep[t % 3, :rows] + recv[t, :rows].astype(F32)

    def third(t):
        arrived(y2_recv.at[t], xy2_sems.at[0, t])
        arrived(x2_recv.at[t], xy2_sems.at[1, t])
        total_l = keep_l[t % 3, :rows] + y2_recv[t].astype(F32)
        total_r = keep_r[t % 3, :rows] + x2_recv[t].astype(F32)
        op = t // F
        if t % F < F - 1:
            slot = op * (F - 1) + t % F
            z_send[slot, :, :mid] = total_l.astype(BF16)
            z_send[slot, :, mid:] = total_r.astype(BF16)
            send(5, t, z_send.at[slot], z_recv.at[op, f], z_sems.at[op, f], at_f(dest_of(t)))
            return
        total = jnp.concatenate([total_l, total_r], axis=1)
        for o in others:
            arrived(z_recv.at[op, o], z_sems.at[op, o])
            total = total + z_recv[op, o].astype(F32)
        values = x_ref[...].astype(F32)
        if op == 0:
            result_ref[...] = (values + total).astype(BF16)
            return
        centred = values - jnp.mean(values, axis=1, keepdims=True)
        inverse_std = lax.rsqrt(jnp.mean(centred * centred, axis=1, keepdims=True) + 1e-05)
        normed = centred * inverse_std
        terms_ref[0:1, :] = jnp.sum(total * normed, axis=0, keepdims=True)
        terms_ref[1:2, :] = jnp.sum(total, axis=0, keepdims=True)
        gain = jnp.concatenate([gain_ref[s].astype(F32) for s in range(F)], axis=1)
        g = total * gain
        back = inverse_std * (
            g - jnp.mean(g, axis=1, keepdims=True) - normed * jnp.mean(g * normed, axis=1, keepdims=True)
        )
        grad_in_ref[...] = (go_ref[...].astype(F32) + back).astype(BF16)

    for t in range(steps + 2):
        if t < steps:
            for_core(t)
            first(t)
        if 0 <= t - 1 < steps:
            second(t - 1)
        if 0 <= t - 2 < steps:
            third(t - 2)
    for key, t in list(open_sends):
        sent(key, t)


def reduce_all(a_out, w_out, a_in, w_in, x, go, gains, C, F):
    rows, width = x.shape
    mid = width // 2
    steps = 2 * F
    vmem = pl.BlockSpec(memory_space=pltpu.VMEM)
    return pl.pallas_call(
        functools.partial(reduce_kernel, (C, F)),
        out_shape=(
            jax.ShapeDtypeStruct((rows, width), BF16),
            jax.ShapeDtypeStruct((rows, width), BF16),
            jax.ShapeDtypeStruct((2, width), F32),
        ),
        in_specs=[vmem] * 7,
        out_specs=(vmem,) * 3,
        scratch_shapes=[
            pltpu.VMEM((2, 4 * rows, width), BF16),
            pltpu.VMEM((F, 4 * rows, width), BF16),
            pltpu.VMEM((2, 2 * rows, mid), BF16),
            pltpu.VMEM((2, 2 * rows, mid), BF16),
            pltpu.VMEM((steps, 2 * rows, mid), BF16),
            pltpu.VMEM((steps, 2 * rows, mid), BF16),
            pltpu.VMEM((3, 2 * rows, mid), F32),
            pltpu.VMEM((3, 2 * rows, mid), F32),
            pltpu.VMEM((2, rows, mid), BF16),
            pltpu.VMEM((2, rows, mid), BF16),
            pltpu.VMEM((steps, rows, mid), BF16),
            pltpu.VMEM((steps, rows, mid), BF16),
            pltpu.VMEM((2 * (F - 1), rows, width), BF16),
            pltpu.VMEM((2, F, rows, width), BF16),
            pltpu.SemaphoreType.DMA((6, steps)),
            pltpu.SemaphoreType.DMA((steps,)),
            pltpu.SemaphoreType.DMA((2, steps)),
            pltpu.SemaphoreType.DMA((2, steps)),
            pltpu.SemaphoreType.DMA((2, F)),
            pltpu.SemaphoreType.REGULAR,
        ],
        compiler_params=pltpu.CompilerParams(
            collective_id=2, has_side_effects=True, vmem_limit_bytes=60 * 1024 * 1024
        ),
    )(a_out, w_out, a_in, w_in, x, go, gains)


PIECES = ((0, 4), (4, 1), (5, 1), (6, 9))


def spread_kernel(
    sizes, shard_units,
    win_ref, wout_ref, terms_ref,
    win_all, wout_all, sums_ref,
    core_terms, x_terms, y_terms, part_terms, z_terms,
    send_sems, block_sems, piece_sems, term_sems,
):
    C, F = sizes
    c = lax.axis_index("ctx")
    f = lax.axis_index("fsdp")
    x_nbr, y_nbr, core = flip(c, 2), flip(c, 4), flip(c, 1)
    diag = flip(x_nbr, 4)
    copies = Copies(send_sems)
    per_rank, share = win_all.shape[2], win_all.shape[3]
    half = per_rank // 2
    att_units, ff_units = PIECES[0][1], sum(n for _, n in PIECES[1:])

    def at_ctx(other):
        return {"ctx": other, "fsdp": f}

    def at_f(other):
        return {"ctx": c, "fsdp": other}

    barrier = pltpu.get_barrier_semaphore()
    others = [lax.rem(f + s, F) for s in range(1, F)]
    for peer in [at_ctx(x_nbr), at_ctx(y_nbr), at_ctx(core)] + [at_f(o) for o in others]:
        pl.semaphore_signal(barrier, inc=1, device_id=peer, device_id_type=pl.DeviceIdType.MESH)
    pl.semaphore_wait(barrier, 3 + F - 1)

    def win_slice(dest):
        return win_ref.at[:, pl.ds(pl.multiple_of(dest * share, share), share)]

    def block(fb, cb, part):
        ref = win_all.at[fb, cb]
        return ref if part is None else ref.at[pl.ds(part * half, half)]

    def pass_block(fb, cb, part, target, src=None):
        ref = block(fb, cb, part)
        copies.send(ref if src is None else src, ref, block_sems.at[fb, cb, part or 0], target)

    def wait_block(fb, cb, part):
        arrived(block(fb, cb, part), block_sems.at[fb, cb, part or 0])

    def piece(fb, cb, p):
        rank = fb * C + cb
        start, units = PIECES[p]
        if p == 0:
            unit = rank * att_units
        else:
            unit = C * F * att_units + rank * ff_units + (start - att_units)
        place = pl.multiple_of(lax.rem(unit, shard_units) * UNIT, UNIT)
        return unit // shard_units, wout_all.at[pl.ds(place, units * UNIT)]

    def own_piece(p):
        start, units = PIECES[p]
        return wout_ref.at[pl.ds(start * UNIT, units * UNIT)]

    def pass_piece(fb, cb, p, target, when, src=None):
        ref = piece(fb, cb, p)[1]
        copies.send(ref if src is None else src, ref, piece_sems.at[fb, cb, p], target, when)

    def wait_piece(fb, cb, p, when):
        def go():
            arrived(piece(fb, cb, p)[1], piece_sems.at[fb, cb, p])
        pl.when(when)(go)

    for o in others:
        copies.send(win_slice(o), block(f, c, None), block_sems.at[f, c, 0], at_f(o))
    mine = win_slice(f)
    for target in (x_nbr, y_nbr, core):
        pass_block(f, c, None, at_ctx(target), src=mine)
    copies.local(mine, block(f, c, None))
    for p in range(len(PIECES)):
        shard, place = piece(f, c, p)
        for o in others:
            pass_piece(f, c, p, at_f(o), shard == o, src=own_piece(p))
        for target in (x_nbr, y_nbr, core):
            pass_piece(f, c, p, at_ctx(target), shard == f, src=own_piece(p))
        copies.local(own_piece(p), place, shard == f)

    total = terms_ref[...]
    for i, (target, buf) in enumerate(((core, core_terms), (x_nbr, x_terms), (y_nbr, y_terms))):
        part_terms[i] = total
        copies.send(part_terms.at[i], buf, term_sems.at[i], at_ctx(target))
        arrived(buf, term_sems.at[i])
        total = total + buf[...]
    for s in range(F):
        part_terms[3 + s, :, :share] = total[:, s * share : (s + 1) * share]
    for o in others:
        copies.send(
            part_terms.at[3 + o, :, pl.ds(0, share)], z_terms.at[f], term_sems.at[3 + f], at_f(o)
        )

    def z_step(fb):
        wait_block(fb, c, None)
        for target in (x_nbr, y_nbr, core):
            pass_block(fb, c, None, at_ctx(target))
        for p in range(len(PIECES)):
            here = piece(fb, c, p)[0] == f
            wait_piece(fb, c, p, here)
            for target in (x_nbr, y_nbr, core):
                pass_piece(fb, c, p, at_ctx(target), here)

    def xy_step(fb, way):
        wait_block(fb, x_nbr, None)
        pass_block(fb, x_nbr, 0, at_ctx(y_nbr))
        pass_block(fb, x_nbr, None, at_ctx(core))
        wait_block(fb, y_nbr, None)
        pass_block(fb, y_nbr, 1, at_ctx(x_nbr))
        pass_block(fb, y_nbr, None, at_ctx(core))
        for p in range(len(PIECES)):
            by_x = (p < 2) == (way == 0)
            for source, onward, turn in ((x_nbr, y_nbr, by_x), (y_nbr, x_nbr, not by_x)):
                here = piece(fb, source, p)[0] == f
                wait_piece(fb, source, p, here)
                if turn:
                    pass_piece(fb, source, p, at_ctx(onward), here)
                pass_piece(fb, source, p, at_ctx(core), here)

    def diag_step(fb):
        for part in (0, 1):
            wait_block(fb, diag, part)
            pass_block(fb, diag, part, at_ctx(core))
        for p in range(len(PIECES)):
            here = piece(fb, diag, p)[0] == f
            wait_piece(fb, diag, p, here)
            pass_piece(fb, diag, p, at_ctx(core), here)

    order = [f] + [lax.rem(f + F - s, F) for s in range(1, F)]
    for s in range(F + 2):
        if s + 1 < F:
            z_step(order[s + 1])
        if s < F:
            xy_step(order[s], s % 2)
        if 0 <= s - 1 < F:
            diag_step(order[s - 1])

    for fb in range(F):
        for cb in (core, flip(core, 2), flip(core, 4)):
            wait_block(fb, cb, None)
        for part in (0, 1):
            wait_block(fb, flip(flip(core, 2), 4), part)
        for cb in (core, flip(core, 2), flip(core, 4), flip(flip(core, 2), 4)):
            for p in range(len(PIECES)):
                wait_piece(fb, cb, p, piece(fb, cb, p)[0] == f)
    z_terms[f] = part_terms[3 + f, :, :share]
    for o in others:
        arrived(z_terms.at[o], term_sems.at[3 + o])
    total = z_terms[0]
    for s in range(1, F):
        total = total + z_terms[s]
    sums_ref[...] = total
    copies.finish()


def spread_all(dw_in, dw_out, terms, shard_rows, C, F):
    per_rank, width = dw_in.shape
    share = width // F
    any_ = pl.BlockSpec(memory_space=pl.ANY)
    vmem = pl.BlockSpec(memory_space=pltpu.VMEM)
    return pl.pallas_call(
        functools.partial(spread_kernel, (C, F), shard_rows // UNIT),
        out_shape=(
            jax.ShapeDtypeStruct((F, C, per_rank, share), BF16),
            jax.ShapeDtypeStruct((shard_rows, width), BF16),
            jax.ShapeDtypeStruct((2, share), F32),
        ),
        in_specs=[any_, any_, vmem],
        out_specs=(any_, any_, vmem),
        scratch_shapes=[
            pltpu.VMEM((2, width), F32),
            pltpu.VMEM((2, width), F32),
            pltpu.VMEM((2, width), F32),
            pltpu.VMEM((3 + F, 2, width), F32),
            pltpu.VMEM((F, 2, share), F32),
            pltpu.SemaphoreType.DMA((320,)),
            pltpu.SemaphoreType.DMA((F, C, 2)),
            pltpu.SemaphoreType.DMA((F, C, len(PIECES))),
            pltpu.SemaphoreType.DMA((3 + F,)),
        ],
        compiler_params=pltpu.CompilerParams(collective_id=3, has_side_effects=True),
    )(dw_in, dw_out, terms)


def turn_kernel(ff, src, out, in_buf, out_buf, in_sems, out_sems):
    F, C = src.shape[0], src.shape[1]
    share = src.shape[3]
    steps = []
    base = 0
    for row, size in ((0, HEAD), (HEAD, HEAD), (2 * HEAD, HEAD), (3 * HEAD, ff), (3 * HEAD + ff, ff)):
        for fb in range(F):
            steps.append((fb, row, size, base + fb * C * size))
        base += F * C * size

    def fetch(i):
        fb, row, size, _ = steps[i]
        return pltpu.make_async_copy(
            src.at[fb, :, pl.ds(row, size)], in_buf.at[i % 2, :, pl.ds(0, size)], in_sems.at[i % 2]
        )

    def store(i):
        _, _, size, col = steps[i]
        return pltpu.make_async_copy(
            out_buf.at[i % 2, :, pl.ds(0, C * size)], out.at[:, pl.ds(col, C * size)], out_sems.at[i % 2]
        )

    fetch(0).start()
    for i, (fb, row, size, col) in enumerate(steps):
        if i + 1 < len(steps):
            fetch(i + 1).start()
        fetch(i).wait()
        if i >= 2:
            store(i - 2).wait()
        block = in_buf[i % 2, :, :size, :].reshape(C * size, share).astype(F32)
        out_buf[i % 2, :, : C * size] = block.T
        store(i).start()
    store(len(steps) - 2).wait()
    store(len(steps) - 1).wait()


def turn_blocks(blocks, ff):
    F, C, per_rank, share = blocks.shape
    any_ = pl.BlockSpec(memory_space=pl.ANY)
    return pl.pallas_call(
        functools.partial(turn_kernel, ff),
        out_shape=jax.ShapeDtypeStruct((share, F * C * per_rank), F32),
        in_specs=[any_],
        out_specs=any_,
        scratch_shapes=[
            pltpu.VMEM((2, C, ff, share), BF16),
            pltpu.VMEM((2, share, C * ff), F32),
            pltpu.SemaphoreType.DMA((2,)),
            pltpu.SemaphoreType.DMA((2,)),
        ],
        compiler_params=pltpu.CompilerParams(vmem_limit_bytes=40 * 1024 * 1024),
    )(blocks)


def tp_body(C, F, inputs, gain, bias, in_weight, out_weight, grad_out, lengths, order):
    rows, width = inputs.shape[1:]
    T = C * F
    ff = FF // T
    scale = HEAD ** (-0.5)
    c = lax.axis_index("ctx")
    f = lax.axis_index("fsdp")
    x = inputs[0]
    go = grad_out[0]
    shard = in_weight.shape[0]

    slices = []
    for dest in range(F):
        rank = dest * C + c
        parts = [
            lax.dynamic_slice(in_weight, (0, base + rank * size), (shard, size))
            for base, size in (
                (0, HEAD), (width, HEAD), (2 * width, HEAD), (3 * width, ff), (3 * width + FF, ff)
            )
        ]
        slices.append(jnp.concatenate(parts, axis=1).T)
    win = jnp.stack(slices)
    count = lengths.shape[1] + order.shape[1]
    table = jnp.pad(jnp.concatenate([lengths, order], axis=1), ((0, 0), (0, 128 - count)))

    go_all, hid_all, w_in, w_out, tables, gains = gather_all(
        x, go, gain[None], bias[None], table, win, out_weight, C, F
    )
    hidden = hid_all.reshape(T * rows, width)
    grads = go_all.reshape(T * rows, width)
    batch = C * rows
    lengths_all = tables[:, 0, : lengths.shape[1]]
    order_all = tables[:, 0, lengths.shape[1] : count]
    index = jnp.arange(batch, dtype=jnp.int32)
    place, doc, turn = jax.vmap(lambda l, o: places_of(index, l, o))(lengths_all, order_all)

    joint = lax.dot_general(hidden, w_in, (((1,), (1,)), ((), ())), preferred_element_type=F32)
    grad_mixed = lax.dot_general(grads, w_out, (((1,), (1,)), ((), ())), preferred_element_type=F32)
    turns = turn.reshape(-1)

    def turned(values, sign):
        return rotate(values[:, None, :], turns, sign)[:, 0, :]

    queries = turned(joint[:, :HEAD], 1.0).astype(BF16).reshape(F, batch, HEAD)
    keys = turned(joint[:, HEAD : 2 * HEAD], 1.0).astype(BF16).reshape(F, batch, HEAD)
    values = joint[:, 2 * HEAD : 3 * HEAD].astype(BF16).reshape(F, batch, HEAD)
    gate = joint[:, 3 * HEAD : 3 * HEAD + ff]
    upward = joint[:, 3 * HEAD + ff :]
    scores = jnp.einsum("bqd,bkd->bqk", queries, keys, preferred_element_type=F32) * scale
    allowed = (doc[:, :, None] == doc[:, None, :]) & (place[:, None, :] <= place[:, :, None])
    weights = jnp.where(allowed, jnp.exp(scores), 0.0)
    totals = jnp.sum(weights, axis=2)
    numer = jnp.einsum("bqk,bkd->bqd", weights.astype(BF16), values, preferred_element_type=F32)
    attended = numer / totals[:, :, None]
    sig = jax.nn.sigmoid(gate)
    activated = gate * sig * upward
    mixed = jnp.concatenate(
        [attended.reshape(-1, HEAD).astype(BF16), activated.astype(BF16)], axis=1
    )
    grad_att = grad_mixed[:, :HEAD].astype(BF16).reshape(F, batch, HEAD)
    grad_act = rounded(grad_mixed[:, HEAD:])
    grad_gate = grad_act * upward * sig * (1.0 + gate * (1.0 - sig))
    grad_up = grad_act * gate * sig
    delta = jnp.sum(grad_att.astype(F32) * attended, axis=2)
    grad_numer = (grad_att.astype(F32) / totals[:, :, None]).astype(BF16)
    ratio = delta / totals
    pushed = jnp.einsum("bqd,bkd->bqk", grad_numer, values, preferred_element_type=F32)
    grad_scores = (weights * (pushed - ratio[:, :, None])).astype(BF16)
    grad_q = jnp.einsum("bqk,bkd->bqd", grad_scores, keys, preferred_element_type=F32) * scale
    grad_k = jnp.einsum("bqk,bqd->bkd", grad_scores, queries, preferred_element_type=F32) * scale
    grad_v = jnp.einsum("bqk,bqd->bkd", weights.astype(BF16), grad_numer, preferred_element_type=F32)
    grad_joint = jnp.concatenate(
        [
            turned(grad_q.reshape(-1, HEAD), -1.0).astype(BF16),
            turned(grad_k.reshape(-1, HEAD), -1.0).astype(BF16),
            grad_v.reshape(-1, HEAD).astype(BF16),
            grad_gate.astype(BF16),
            grad_up.astype(BF16),
        ],
        axis=1,
    )
    both = ("fsdp", "ctx")
    result, grad_in, norm_terms = reduce_all(mixed, w_out, grad_joint, w_in, x, go, gains, C, F)
    dw_in = transposed_dot(grad_joint, hidden).astype(BF16)
    dw_out = transposed_dot(mixed, grads).astype(BF16)
    blocks, out_rows, sums = spread_all(dw_in, dw_out, norm_terms, out_weight.shape[0], C, F)
    return (
        result[None], grad_in[None], turn_blocks(blocks, ff), out_rows.astype(F32), sums[0], sums[1]
    )


def solution(mesh):
    in_specs = (
        P("fsdp", "ctx", None),
        P("fsdp"),
        P("fsdp"),
        P("fsdp", None),
        P("fsdp", None),
        P("fsdp", "ctx", None),
        P("fsdp", None),
        P("fsdp", None),
    )
    out_specs = (
        P("fsdp", "ctx", None),
        P("fsdp", "ctx", None),
        P("fsdp", None),
        P("fsdp", None),
        P("fsdp"),
        P("fsdp"),
    )
    C, F = mesh.shape["ctx"], mesh.shape["fsdp"]
    if (C, F) == (8, 4):
        work = functools.partial(tp_body, C, F)
    else:
        work = body
    return jax.shard_map(work, mesh=mesh, in_specs=in_specs, out_specs=out_specs, check_vma=False)
```

```python
import functools
import math

import jax
import jax.numpy as jnp
from jax import lax
from jax.experimental import pallas as pl
from jax.experimental.pallas import tpu as pltpu
from jax.sharding import PartitionSpec as P

HEADS = 32
HEAD = 64
ROT = 16
FF = 5632
BLOCK = 64
BF16 = jnp.bfloat16
F32 = jnp.float32
UNIT = 16


def places_of(index, length_row, order_row):
    count = order_row.shape[0]
    hit = (index // BLOCK)[:, None] == jnp.arange(count, dtype=jnp.int32)[None, :]
    block_id = jnp.sum(jnp.where(hit, order_row[None, :], 0), axis=1)
    place = block_id * BLOCK + index % BLOCK
    ends = jnp.cumsum(length_row)
    starts = ends - length_row
    inside = (place[:, None] >= starts[None, :]) & (place[:, None] < ends[None, :])
    docs = jnp.sum(
        jnp.where(inside, jnp.arange(length_row.shape[0], dtype=jnp.int32)[None, :], 0), axis=1
    )
    first = jnp.sum(jnp.where(inside, starts[None, :], 0), axis=1)
    return (place, docs, place - first)


def rotate(values, positions, sign):
    half = ROT // 2
    freq = 10000.0 ** (-2.0 * jnp.arange(half, dtype=jnp.float32) / ROT)
    angle = positions.astype(jnp.float32)[:, None] * freq[None, :]
    cosine = jnp.cos(angle)[:, None, :]
    sine = sign * jnp.sin(angle)[:, None, :]
    first = values[..., :half]
    second = values[..., half:ROT]
    return jnp.concatenate(
        [first * cosine - second * sine, second * cosine + first * sine, values[..., ROT:]], axis=-1
    )


def rounded(values):
    return lax.optimization_barrier(values.astype(jnp.bfloat16)).astype(jnp.float32)


def transposed_dot(left, right):
    return lax.dot_general(
        left, right, (((0,), (0,)), ((), ())), preferred_element_type=jnp.float32
    )


def against_rows(left, right):
    return lax.dot_general(
        left, right, (((1,), (1,)), ((), ())), preferred_element_type=jnp.float32
    )


def body(inputs, gain, bias, in_weight, out_weight, grad_out, lengths, order):
    rows = inputs.shape[1]
    width = inputs.shape[2]
    length_row = lengths[0]
    order_row = order[0]
    local_index = lax.axis_index("ctx") * rows + jnp.arange(rows, dtype=jnp.int32)
    query_place, query_doc, query_turn = places_of(local_index, length_row, order_row)
    scale = HEAD ** (-0.5)
    head_shape = (rows, HEADS, HEAD)
    values_in = inputs[0].astype(jnp.float32)
    centred = values_in - jnp.mean(values_in, axis=1, keepdims=True)
    inverse_std = lax.rsqrt(jnp.mean(centred * centred, axis=1, keepdims=True) + 1e-05)
    normed = centred * inverse_std
    weight_piece = lax.all_gather(in_weight, "fsdp", axis=0, tiled=True)
    gain_piece = lax.all_gather(gain, "fsdp", axis=0, tiled=True)
    bias_piece = lax.all_gather(bias, "fsdp", axis=0, tiled=True)
    count = weight_piece.shape[0]
    columns = normed
    hidden_piece = (
        columns * gain_piece.astype(jnp.float32) + bias_piece.astype(jnp.float32)
    ).astype(jnp.bfloat16)
    joint_sum = jnp.dot(hidden_piece, weight_piece, preferred_element_type=jnp.float32)
    gain_full = gain_piece.astype(jnp.float32)
    joint, hidden_in, gain_full = (joint_sum, hidden_piece, gain_full)
    queries = rotate(joint[:, :width].reshape(head_shape), query_turn, 1.0).astype(jnp.bfloat16)
    keys = (
        rotate(joint[:, width : 2 * width].reshape(head_shape), query_turn, 1.0)
        .astype(jnp.bfloat16)
        .reshape(rows, width)
    )
    values = joint[:, 2 * width : 3 * width].astype(jnp.bfloat16)
    gate = joint[:, 3 * width : 3 * width + FF]
    upward = joint[:, 3 * width + FF :]

    def exp_scores(key_block, start, count):
        key_place, key_doc, unused_turn = places_of(
            start + jnp.arange(count, dtype=jnp.int32), length_row, order_row
        )
        scores = (
            jnp.einsum(
                "qhd,khd->hqk",
                queries,
                key_block.reshape(count, HEADS, HEAD),
                preferred_element_type=jnp.float32,
            )
            * scale
        )
        allowed = (query_doc[:, None] == key_doc[None, :]) & (
            key_place[None, :] <= query_place[:, None]
        )
        return jnp.where(allowed[None], jnp.exp(scores), 0.0)

    empty_attention = (jnp.zeros(head_shape, jnp.float32), jnp.zeros((HEADS, rows), jnp.float32))
    key_piece = lax.all_gather(keys, "ctx", axis=0, tiled=True)
    value_piece = lax.all_gather(values, "ctx", axis=0, tiled=True)
    count = key_piece.shape[0]
    block_rows = math.gcd(count, 512)

    def add_block(j, state):
        numer, totals = state
        offset = j * block_rows
        key_block = lax.dynamic_slice_in_dim(key_piece, offset, block_rows, 0)
        value_block = lax.dynamic_slice_in_dim(value_piece, offset, block_rows, 0)
        weights = exp_scores(key_block, offset, block_rows)
        totals = totals + jnp.sum(weights, axis=2)
        numer = numer + jnp.einsum(
            "hqk,khd->qhd",
            weights.astype(jnp.bfloat16),
            value_block.reshape(block_rows, HEADS, HEAD),
            preferred_element_type=jnp.float32,
        )
        return (numer, totals)

    numer, totals = lax.fori_loop(0, count // block_rows, add_block, empty_attention)
    attended = numer / jnp.transpose(totals)[:, :, None]
    sigmoid_gate = jax.nn.sigmoid(gate)
    activated = gate * sigmoid_gate * upward
    mixed_in = jnp.concatenate(
        [attended.reshape(rows, width).astype(jnp.bfloat16), activated.astype(jnp.bfloat16)], axis=1
    )
    columns = mixed_in
    mixed = jnp.dot(
        columns,
        lax.all_gather(out_weight, "fsdp", axis=0, tiled=True),
        preferred_element_type=jnp.float32,
    )
    result = (values_in + mixed).astype(jnp.bfloat16)
    grad_rows = grad_out[0]
    grad_mixed = against_rows(grad_rows, lax.all_gather(out_weight, "fsdp", axis=0, tiled=True))
    grad_att = grad_mixed[:, :width].astype(jnp.bfloat16).reshape(head_shape)
    grad_act = rounded(grad_mixed[:, width:])
    grad_gate = grad_act * upward * sigmoid_gate * (1.0 + gate * (1.0 - sigmoid_gate))
    grad_up = grad_act * gate * sigmoid_gate
    delta = jnp.transpose(jnp.sum(grad_att.astype(jnp.float32) * attended, axis=2))
    grad_numer = (grad_att.astype(jnp.float32) / jnp.transpose(totals)[:, :, None]).astype(
        jnp.bfloat16
    )
    ratio = delta / totals
    keys_all, values_all = (
        lax.all_gather(keys, "ctx", axis=0, tiled=True),
        lax.all_gather(values, "ctx", axis=0, tiled=True),
    )
    group = keys_all.shape[0]

    def score_grads(key_block, value_block, start, count):
        weights = exp_scores(key_block, start, count)
        pushed = jnp.einsum(
            "qhd,khd->hqk",
            grad_numer,
            value_block.reshape(count, HEADS, HEAD),
            preferred_element_type=jnp.float32,
        )
        return (weights, (weights * (pushed - ratio[:, :, None])).astype(jnp.bfloat16))

    query_rows = math.gcd(group, 512)

    def query_block_grad(j, total):
        offset = j * query_rows
        key_block = lax.dynamic_slice_in_dim(keys_all, offset, query_rows, 0)
        value_block = lax.dynamic_slice_in_dim(values_all, offset, query_rows, 0)
        unused_weights, grad_scores = score_grads(key_block, value_block, offset, query_rows)
        return total + jnp.einsum(
            "hqk,khd->qhd",
            grad_scores,
            key_block.reshape(query_rows, HEADS, HEAD),
            preferred_element_type=jnp.float32,
        )

    grad_query = (
        lax.fori_loop(0, group // query_rows, query_block_grad, jnp.zeros(head_shape, jnp.float32))
        * scale
    )
    key_block_rows = math.gcd(rows * lax.axis_size("ctx"), 512)

    def key_block_grad(j, terms):
        offset = j * key_block_rows
        key_block = lax.dynamic_slice_in_dim(keys_all, offset, key_block_rows, 0)
        value_block = lax.dynamic_slice_in_dim(values_all, offset, key_block_rows, 0)
        weights, grad_scores = score_grads(key_block, value_block, offset, key_block_rows)
        key_part = (
            jnp.einsum("hqk,qhd->khd", grad_scores, queries, preferred_element_type=jnp.float32)
            * scale
        )
        value_part = jnp.einsum(
            "hqk,qhd->khd",
            weights.astype(jnp.bfloat16),
            grad_numer,
            preferred_element_type=jnp.float32,
        )
        block_terms = jnp.concatenate(
            [key_part.reshape(key_block_rows, width), value_part.reshape(key_block_rows, width)],
            axis=1,
        )
        return lax.dynamic_update_slice_in_dim(terms, block_terms, j * key_block_rows, 0)

    key_value_grad = lax.psum_scatter(
        lax.fori_loop(
            0,
            rows * lax.axis_size("ctx") // key_block_rows,
            key_block_grad,
            jnp.zeros((rows * lax.axis_size("ctx"), 2 * width), jnp.float32),
        ).astype(jnp.bfloat16),
        "ctx",
        scatter_dimension=0,
        tiled=True,
    ).astype(jnp.float32)
    grad_key = rotate(key_value_grad[:, :width].reshape(head_shape), query_turn, -1.0).reshape(
        rows, width
    )
    grad_query = rotate(grad_query, query_turn, -1.0).reshape(rows, width)
    grad_joint = jnp.concatenate(
        [
            grad_query.astype(jnp.bfloat16),
            grad_key.astype(jnp.bfloat16),
            key_value_grad[:, width:].astype(jnp.bfloat16),
            grad_gate.astype(jnp.bfloat16),
            grad_up.astype(jnp.bfloat16),
        ],
        axis=1,
    )
    grad_hidden = against_rows(grad_joint, lax.all_gather(in_weight, "fsdp", axis=0, tiled=True))
    grad_normed = grad_hidden * gain_full[None, :]
    grad_inputs = inverse_std * (
        grad_normed
        - jnp.mean(grad_normed, axis=1, keepdims=True)
        - normed * jnp.mean(grad_normed * normed, axis=1, keepdims=True)
    )
    grad_in = (grad_rows.astype(jnp.float32) + grad_inputs).astype(jnp.bfloat16)
    norm_terms = jnp.stack([jnp.sum(grad_hidden * normed, axis=0), jnp.sum(grad_hidden, axis=0)])
    norm_totals = lax.psum(norm_terms, ("ctx", "fsdp"))
    shards = lax.axis_size("fsdp")
    share = width // shards
    gain_grad = lax.dynamic_slice_in_dim(norm_totals[0], lax.axis_index("fsdp") * share, share, 0)
    bias_grad = lax.dynamic_slice_in_dim(norm_totals[1], lax.axis_index("fsdp") * share, share, 0)

    def column_terms(source, partner):
        return transposed_dot(source, partner)

    parts = lax.axis_size("ctx")

    def reorder(matrix):
        columns = matrix.shape[1]
        return (
            matrix.reshape(rows, shards, parts, columns // (shards * parts))
            .transpose(0, 2, 1, 3)
            .reshape(rows, columns)
        )

    in_piece = lax.psum_scatter(
        column_terms(reorder(hidden_in), grad_joint),
        ("ctx", "fsdp"),
        scatter_dimension=0,
        tiled=True,
    )
    out_piece = lax.psum_scatter(
        column_terms(reorder(mixed_in), grad_rows), ("ctx", "fsdp"), scatter_dimension=0, tiled=True
    )
    in_weight_grad, out_weight_grad = (
        lax.all_gather(in_piece.astype(jnp.bfloat16), "ctx", axis=0, tiled=True).astype(
            in_piece.dtype
        ),
        lax.all_gather(out_piece.astype(jnp.bfloat16), "ctx", axis=0, tiled=True).astype(
            out_piece.dtype
        ),
    )
    return (result[None], grad_in[None], in_weight_grad, out_weight_grad, gain_grad, bias_grad)


def flip(index, bit):
    return index + bit - 2 * bit * ((index // bit) % 2)


class Copies:
    def __init__(self, sems):
        self.sems = sems
        self.used = 0
        self.open = []

    def send(self, src, dst, recv_sem, target, when=None):
        copy = pltpu.make_async_remote_copy(
            src_ref=src,
            dst_ref=dst,
            send_sem=self.sems.at[self.used],
            recv_sem=recv_sem,
            device_id=target,
            device_id_type=pl.DeviceIdType.MESH,
        )
        self.used += 1
        self.open.append((copy.wait_send, when, False))
        if when is None:
            copy.start()
        else:
            pl.when(when)(copy.start)

    def local(self, src, dst, when=None):
        copy = pltpu.make_async_copy(src, dst, self.sems.at[self.used])
        self.used += 1
        if when is None:
            copy.start()
        else:
            pl.when(when)(copy.start)
        self.open.append((copy.wait, when, True))

    def finish_local(self):
        self.finish([item for item in self.open if item[2]])
        self.open = [item for item in self.open if not item[2]]

    def finish(self, items=None):
        for done, when, _ in self.open if items is None else items:
            if when is None:
                done()
            else:
                pl.when(when)(done)


def arrived(ref, recv_sem):
    pltpu.make_async_copy(ref, ref, recv_sem).wait()


def owner_of_unit(unit, att_units, ff_units, heads):
    first = heads * att_units
    is_att = (unit < first).astype(jnp.int32) if hasattr(unit, "astype") else int(unit < first)
    return is_att * (unit // att_units) + (1 - is_att) * ((unit - first) // ff_units)


LOG2E = 1.4426950408889634
CHUNK = 512
QT = 256


class Stream:
    def __init__(self, count, source, buf, sems):
        self.count, self.source, self.buf, self.sems = count, source, buf, sems

    def copy(self, i):
        return pltpu.make_async_copy(self.source(i), self.buf.at[i % 2], self.sems.at[i % 2])

    def start(self):
        self.copy(0).start()

    def take(self, i):
        if i + 1 < self.count:
            self.copy(i + 1).start()
        self.copy(i).wait()
        return self.buf[i % 2]


def turn_pair(values, cosine, sine):
    half = ROT // 2
    first, second = values[:half], values[half:ROT]
    return jnp.concatenate(
        [first * cosine - second * sine, second * cosine + first * sine, values[ROT:]], axis=0
    )


def nt_dot(left, right):
    return lax.dot_general(left, right, (((1,), (1,)), ((), ())), preferred_element_type=F32)


def token_tables(row, batch, docs):
    index = lax.broadcasted_iota(jnp.int32, (1, batch), 1)
    place = index % BLOCK
    block = index // BLOCK
    for j in range(batch // BLOCK):
        place = place + jnp.where(block == j, row[:, docs + j : docs + j + 1] * BLOCK, 0)
    start = jnp.zeros((1, 1), jnp.int32)
    first = jnp.zeros((1, batch), jnp.int32)
    for j in range(docs):
        first = jnp.where(place >= start, start, first)
        start = start + row[:, j : j + 1]
    return place, place - first


def as_column(row):
    return jnp.broadcast_to(row, (8, row.shape[1])).T[:, :1]


def allowed_keys(place_col, place_row, turn_row):
    return (place_col <= place_row) & (place_col >= place_row - turn_row)


class Forward:
    def __init__(self, refs, batch, ff):
        self.r, self.batch, self.ff = refs, batch, ff

    def tables(self, b):
        r, batch = self.r, self.batch
        place, turn = token_tables(r["table"][b], batch, 4)
        r["place"][b] = place
        r["turn"][b] = turn
        pair = lax.broadcasted_iota(jnp.int32, (ROT // 2, 1), 0).astype(F32)
        freq = jnp.exp2(pair * (-2.0 * math.log2(10000.0) / ROT))
        angle = turn.astype(F32) * freq
        r["cos"][:, b * batch : (b + 1) * batch] = jnp.cos(angle)
        r["sin"][:, b * batch : (b + 1) * batch] = jnp.sin(angle)

    def project(self, i):
        r, ff = self.r, self.ff
        cols = slice(i * CHUNK, (i + 1) * CHUNK)
        hidden = r["hidden"].take(i).reshape(CHUNK, -1)
        joint = nt_dot(r["w_in"][...], hidden)
        cosine, sine = r["cos"][:, cols], r["sin"][:, cols]
        r["qkv"][:HEAD, cols] = turn_pair(joint[:HEAD], cosine, sine).astype(BF16)
        r["qkv"][HEAD : 2 * HEAD, cols] = turn_pair(joint[HEAD : 2 * HEAD], cosine, sine).astype(BF16)
        r["qkv"][2 * HEAD : 3 * HEAD, cols] = joint[2 * HEAD : 3 * HEAD].astype(BF16)
        slot = i % 2
        if i >= 2:
            self.gates(i - 2).wait()
        gate, upward = joint[3 * HEAD : 3 * HEAD + ff], joint[3 * HEAD + ff :]
        r["gate_buf"][slot, :ff] = gate
        r["gate_buf"][slot, ff:] = upward
        r["mixed"][HEAD:, cols] = (gate * jax.nn.sigmoid(gate) * upward).astype(BF16)
        self.gates(i).start()

    def gates(self, i):
        r = self.r
        return pltpu.make_async_copy(
            r["gate_buf"].at[i % 2], r["gates"].at[:, pl.ds(i * CHUNK, CHUNK)], r["gate_sems"].at[i % 2]
        )

    def attend(self, b, t):
        r, batch = self.r, self.batch
        whole = slice(b * batch, (b + 1) * batch)
        if t == 0:
            r["key_rows"][...] = r["qkv"][HEAD : 2 * HEAD, whole].T
            r["place_col"][...] = as_column(r["place"][b])
        cols = slice(b * batch + t * QT, b * batch + (t + 1) * QT)
        here = slice(t * QT, (t + 1) * QT)
        place, turn = r["place"][b, :, here], r["turn"][b, :, here]
        query = r["qkv"][:HEAD, cols]
        totals = jnp.zeros((1, QT), F32)
        numer = jnp.zeros((HEAD, QT), F32)
        for k in range(batch // QT):
            keys = slice(k * QT, (k + 1) * QT)
            scores = jnp.dot(r["key_rows"][keys], query, preferred_element_type=F32)
            ok = allowed_keys(r["place_col"][keys], place, turn)
            weights = jnp.where(ok, jnp.exp2(scores * (LOG2E * HEAD**-0.5)), 0.0)
            totals = totals + jnp.sum(weights, axis=0, keepdims=True)
            value = r["qkv"][2 * HEAD :, b * batch + k * QT : b * batch + (k + 1) * QT]
            numer = numer + jnp.dot(value, weights.astype(BF16), preferred_element_type=F32)
        attended = numer / totals
        r["attended"][:, cols] = attended
        r["totals"][:, cols] = totals
        r["mixed"][:HEAD, cols] = attended.astype(BF16)


def forward_kernel(
    sizes, ff,
    x_ref, go_ref, gain_ref, bias_ref, table_ref, win_ref, wout_ref,
    go_all, hid_all, win_all, wout_all, gain_buf,
    qkv, gates, mixed, attended, totals, place, turn, cosine, sine,
    table_all, bias_buf, hid_own, win_buf, hidden_buf, gate_buf, key_rows, place_col,
    send_sems, block_sems, small_sems, win_sems, wout_sems, hidden_sems, gate_sems, load_sem,
):
    C, F = sizes
    c = lax.axis_index("ctx")
    f = lax.axis_index("fsdp")
    x_nbr, y_nbr, core = flip(c, 2), flip(c, 4), flip(c, 1)
    diag = flip(x_nbr, 4)
    copies = Copies(send_sems)
    here = {"ctx": c, "fsdp": f}

    def at_ctx(other):
        return {"ctx": other, "fsdp": f}

    def at_f(other):
        return {"ctx": c, "fsdp": other}

    barrier = pltpu.get_barrier_semaphore()
    others = [lax.rem(f + s, F) for s in range(1, F)]
    for peer in [at_ctx(x_nbr), at_ctx(y_nbr), at_ctx(core)] + [at_f(o) for o in others]:
        pl.semaphore_signal(barrier, inc=1, device_id=peer, device_id_type=pl.DeviceIdType.MESH)
    pl.semaphore_wait(barrier, 3 + F - 1)

    for i, o in enumerate(others):
        copies.send(gain_ref, gain_buf.at[f], small_sems.at[0, f], at_f(o))
        copies.send(bias_ref, bias_buf.at[f], small_sems.at[1, f], at_f(o))
        copies.send(table_ref, table_all.at[f], small_sems.at[2, f], at_f(o))

    outs = (go_all, hid_all)
    rows = x_ref.shape[0]
    half = rows // 2

    def piece(a, fb, cb, part):
        ref = outs[a].at[fb, cb]
        if part is None:
            return ref
        return ref.at[pl.ds(part * half, half)]

    def forward(a, fb, cb, part, target, when=None, src=None):
        ref = piece(a, fb, cb, part)
        copies.send(ref if src is None else src, ref, block_sems.at[a, fb, cb, part or 0], target, when)

    def wait_block(a, fb, cb, part, when=None):
        def go():
            arrived(piece(a, fb, cb, part), block_sems.at[a, fb, cb, part or 0])
        if when is None:
            go()
        else:
            pl.when(when)(go)

    up, down = f + 1 < F, f > 0

    def own(a, src):
        forward(a, f, c, None, at_ctx(x_nbr), src=src)
        forward(a, f, c, None, at_ctx(y_nbr), src=src)
        forward(a, f, c, None, at_f(f + 1), when=up, src=src)
        forward(a, f, c, None, at_f(f - 1), when=down, src=src)
        forward(a, f, c, None, at_ctx(core), src=src)
        copies.local(src, outs[a].at[f, c])

    values = x_ref[...].astype(F32)
    centred = values - jnp.mean(values, axis=1, keepdims=True)
    normed = centred * lax.rsqrt(jnp.mean(centred * centred, axis=1, keepdims=True) + 1e-05)
    gain_buf[f] = gain_ref[...]
    bias_buf[f] = bias_ref[...]
    for o in others:
        arrived(gain_buf.at[o], small_sems.at[0, o])
        arrived(bias_buf.at[o], small_sems.at[1, o])
    share = gain_ref.shape[1]
    for s in range(F):
        cols = slice(s * share, (s + 1) * share)
        hid_own[:, cols] = (
            normed[:, cols] * gain_buf[s].astype(F32) + bias_buf[s].astype(F32)
        ).astype(BF16)
    own(1, hid_own)
    own(0, go_ref)

    share_rows = win_ref.shape[2]

    def win_place(src_f):
        return win_all.at[:, pl.ds(pl.multiple_of(src_f * share_rows, share_rows), share_rows)]

    for o in others:
        copies.send(win_ref.at[o], win_place(f), win_sems.at[f], at_f(o))
    copies.local(win_ref.at[f], win_place(f))
    units_per_shard = wout_ref.shape[0] // UNIT
    att_units, ff_units = HEAD // UNIT * (HEADS // (C * F)), FF // (C * F) // UNIT

    def unit_of(rank, i):
        if i < att_units:
            return rank * att_units + i
        return C * F * att_units + rank * ff_units + (i - att_units)

    def unit_rows(ref, unit):
        return ref.at[pl.ds(pl.multiple_of(unit * UNIT, UNIT), UNIT)]

    for step in range(F):
        dest = lax.rem(f + step, F)
        rank = dest * C + c
        for i in range(att_units + ff_units):
            unit = unit_of(rank, i)
            mine = unit // units_per_shard == f
            src = unit_rows(wout_ref, lax.rem(unit, units_per_shard))
            dst = wout_all.at[pl.ds(i * UNIT, UNIT)]
            if step == 0:
                copy = pltpu.make_async_copy(src, dst, wout_sems.at[i])
                pl.when(mine)(copy.start)
            else:
                copies.send(src, dst, wout_sems.at[i], at_f(dest), when=mine)

    def blocks_of(s):
        if s == 0:
            return [(-1, f, None)]
        return [(-1, f - s, f - s >= 0), (1, f + s, f + s < F)]

    def z_step(a, s):
        for sign, fb, valid in blocks_of(s):
            onward = valid & (up if sign < 0 else down)
            wait_block(a, fb, c, None, when=valid)
            forward(a, fb, c, None, at_f(f - sign), when=onward)
            for target in (x_nbr, y_nbr, core):
                forward(a, fb, c, None, at_ctx(target), when=valid)

    def xy_step(a, s):
        for _, fb, valid in blocks_of(s):
            wait_block(a, fb, x_nbr, None, when=valid)
            forward(a, fb, x_nbr, 0, at_ctx(y_nbr), when=valid)
            forward(a, fb, x_nbr, None, at_ctx(core), when=valid)
            wait_block(a, fb, y_nbr, None, when=valid)
            forward(a, fb, y_nbr, 1, at_ctx(x_nbr), when=valid)
            forward(a, fb, y_nbr, None, at_ctx(core), when=valid)

    def diag_step(a, s):
        for _, fb, valid in blocks_of(s):
            for part in (0, 1):
                wait_block(a, fb, diag, part, when=valid)
                forward(a, fb, diag, part, at_ctx(core), when=valid)

    def from_core(a):
        for fb in range(F):
            wait_block(a, fb, core, None)
            wait_block(a, fb, flip(core, 2), None)
            wait_block(a, fb, flip(core, 4), None)
            for part in (0, 1):
                wait_block(a, fb, flip(flip(core, 2), 4), part)

    batch = C * rows
    refs = dict(
        table=table_all, place=place, turn=turn, cos=cosine, sin=sine, w_in=win_buf, qkv=qkv,
        gates=gates, gate_buf=gate_buf, gate_sems=gate_sems, mixed=mixed, attended=attended,
        totals=totals, key_rows=key_rows, place_col=place_col,
        hidden=Stream(
            F * batch // CHUNK,
            lambda i: hid_all.at[
                i * CHUNK // batch, pl.ds(i * CHUNK % batch // rows, CHUNK // rows)
            ],
            hidden_buf, hidden_sems,
        ),
    )
    work = Forward(refs, batch, ff)

    for o in others:
        arrived(table_all.at[o], small_sems.at[2, o])
    table_all[f] = table_ref[...]
    for b in range(F):
        work.tables(b)

    z_step(1, 1)
    xy_step(1, 0)
    z_step(1, 2)
    xy_step(1, 1)
    diag_step(1, 0)
    z_step(1, 3)
    xy_step(1, 2)
    z_step(0, 1)
    diag_step(1, 1)
    xy_step(1, 3)
    diag_step(1, 2)
    diag_step(1, 3)
    for o in others:
        arrived(win_place(o), win_sems.at[o])
    copies.finish_local()
    load = pltpu.make_async_copy(win_all, win_buf, load_sem)
    load.start()
    xy_step(0, 0)
    from_core(1)
    refs["hidden"].start()
    load.wait()

    pieces = []
    for b in range(F):
        for i in range(batch // CHUNK):
            pieces.append(functools.partial(work.project, b * (batch // CHUNK) + i))
        for t in range(batch // QT):
            pieces.append(functools.partial(work.attend, b, t))
    steps = [
        functools.partial(z_step, 0, 2),
        functools.partial(xy_step, 0, 1),
        functools.partial(diag_step, 0, 0),
        functools.partial(z_step, 0, 3),
        functools.partial(xy_step, 0, 2),
        functools.partial(diag_step, 0, 1),
        functools.partial(xy_step, 0, 3),
        functools.partial(diag_step, 0, 2),
        functools.partial(diag_step, 0, 3),
    ]
    weave(steps, pieces)
    from_core(0)
    for i in range(att_units + ff_units):
        arrived(wout_all.at[pl.ds(i * UNIT, UNIT)], wout_sems.at[i])
    last = F * batch // CHUNK
    work.gates(last - 2).wait()
    work.gates(last - 1).wait()
    copies.finish()


def weave(steps, pieces):
    done = 0
    for i, step in enumerate(steps):
        until = (i + 1) * len(pieces) // len(steps)
        for piece in pieces[done:until]:
            piece()
        done = until
        step()


def forward_all(x, go, gain, bias, table, win, wout, C, F):
    rows, width = x.shape
    per_rank = win.shape[1]
    any_ = pl.BlockSpec(memory_space=pl.ANY)
    vmem = pl.BlockSpec(memory_space=pltpu.VMEM)
    ff = FF // (C * F)
    wout_rows = HEAD * HEADS // (C * F) + ff
    share = gain.shape[1]
    batch = C * rows
    tokens = F * batch
    shape = jax.ShapeDtypeStruct
    return pl.pallas_call(
        functools.partial(forward_kernel, (C, F), ff),
        out_shape=(
            shape((F, C, rows, width), BF16),
            shape((F, C, rows, width), BF16),
            shape((per_rank, width), BF16),
            shape((wout_rows, width), BF16),
            shape((F, 1, share), BF16),
            shape((3 * HEAD, tokens), BF16),
            shape((2 * ff, tokens), F32),
            shape((HEAD + ff, tokens), BF16),
            shape((HEAD, tokens), F32),
            shape((1, tokens), F32),
            shape((F, 1, batch), jnp.int32),
            shape((F, 1, batch), jnp.int32),
            shape((ROT // 2, tokens), F32),
            shape((ROT // 2, tokens), F32),
        ),
        in_specs=[vmem, any_, vmem, vmem, vmem, any_, any_],
        out_specs=(any_,) * 4 + (vmem, vmem, any_) + (vmem,) * 7,
        scratch_shapes=[
            pltpu.VMEM((F,) + table.shape, jnp.int32),
            pltpu.VMEM((F, 1, share), BF16),
            pltpu.VMEM((rows, width), BF16),
            pltpu.VMEM((per_rank, width), BF16),
            pltpu.VMEM((2, CHUNK // rows, rows, width), BF16),
            pltpu.VMEM((2, 2 * ff, CHUNK), F32),
            pltpu.VMEM((batch, HEAD), BF16),
            pltpu.VMEM((batch, 1), jnp.int32),
            pltpu.SemaphoreType.DMA((256,)),
            pltpu.SemaphoreType.DMA((2, F, C, 2)),
            pltpu.SemaphoreType.DMA((3, F)),
            pltpu.SemaphoreType.DMA((F,)),
            pltpu.SemaphoreType.DMA((wout_rows // UNIT,)),
            pltpu.SemaphoreType.DMA((2,)),
            pltpu.SemaphoreType.DMA((2,)),
            pltpu.SemaphoreType.DMA,
        ],
        compiler_params=pltpu.CompilerParams(
            collective_id=1, has_side_effects=True, vmem_limit_bytes=56 * 1024 * 1024
        ),
    )(x, go, gain, bias, table, win, wout)


def scores_of(key_rows, query, place_col, place, turn):
    scores = jnp.dot(key_rows, query, preferred_element_type=F32)
    ok = allowed_keys(place_col, place, turn)
    return jnp.where(ok, jnp.exp2(scores * (LOG2E * HEAD**-0.5)), 0.0)


class Backward:
    def __init__(self, refs, batch, ff):
        self.r, self.batch, self.ff = refs, batch, ff

    def mixed(self, i):
        r, ff = self.r, self.ff
        cols = slice(i * CHUNK, (i + 1) * CHUNK)
        grads = r["grads"].take(i).reshape(CHUNK, -1)
        grad = nt_dot(r["w_out"][...], grads)
        gates = r["gates"].take(i)
        grad_att = grad[:HEAD].astype(BF16).astype(F32)
        inverse = 1.0 / r["totals"][:, cols]
        delta = jnp.sum(grad_att * r["attended"][:, cols], axis=0, keepdims=True)
        r["ratio"][:, cols] = delta * inverse
        r["numer"][:, cols] = (grad_att * inverse).astype(BF16)
        grad_act = grad[HEAD:].astype(BF16).astype(F32)
        gate, upward = gates[:ff], gates[ff:]
        sig = jax.nn.sigmoid(gate)
        r["joint"][3 * HEAD : 3 * HEAD + ff, cols] = (
            grad_act * upward * sig * (1.0 + gate * (1.0 - sig))
        ).astype(BF16)
        r["joint"][3 * HEAD + ff :, cols] = (grad_act * gate * sig).astype(BF16)

    def attend(self, b, t):
        r, batch = self.r, self.batch
        whole = slice(b * batch, (b + 1) * batch)
        if t == 0:
            r["key_rows"][...] = r["qkv"][HEAD : 2 * HEAD, whole].T
            r["value_rows"][...] = r["qkv"][2 * HEAD :, whole].T
            r["place_col"][...] = as_column(r["place"][b])
            r["grad_k"][...] = jnp.zeros_like(r["grad_k"])
            r["grad_v"][...] = jnp.zeros_like(r["grad_v"])
        cols = slice(b * batch + t * QT, b * batch + (t + 1) * QT)
        here = slice(t * QT, (t + 1) * QT)
        place, turn = r["place"][b, :, here], r["turn"][b, :, here]
        query, numer, ratio = r["qkv"][:HEAD, cols], r["numer"][:, cols], r["ratio"][:, cols]
        grad_q = jnp.zeros((HEAD, QT), F32)
        for k in range(batch // QT):
            keys = slice(k * QT, (k + 1) * QT)
            key_cols = slice(b * batch + k * QT, b * batch + (k + 1) * QT)
            weights = scores_of(r["key_rows"][keys], query, r["place_col"][keys], place, turn)
            pushed = jnp.dot(r["value_rows"][keys], numer, preferred_element_type=F32)
            grad_scores = (weights * (pushed - ratio)).astype(BF16)
            grad_q = grad_q + jnp.dot(
                r["qkv"][HEAD : 2 * HEAD, key_cols], grad_scores, preferred_element_type=F32
            )
            r["grad_k"][:, keys] += nt_dot(query, grad_scores)
            r["grad_v"][:, keys] += nt_dot(numer, weights.astype(BF16))
        scale = HEAD**-0.5
        r["joint"][:HEAD, cols] = turn_pair(
            grad_q * scale, r["cos"][:, cols], -r["sin"][:, cols]
        ).astype(BF16)
        if t == batch // QT - 1:
            r["joint"][HEAD : 2 * HEAD, whole] = turn_pair(
                r["grad_k"][...] * scale, r["cos"][:, whole], -r["sin"][:, whole]
            ).astype(BF16)
            r["joint"][2 * HEAD : 3 * HEAD, whole] = r["grad_v"][...].astype(BF16)


class Reduce:
    def __init__(self, sizes, left_ref, w_ref, rows, bufs, sems):
        self.C, self.F = sizes
        self.left_ref, self.w_ref, self.rows = left_ref, w_ref, rows
        self.width = w_ref.shape[1]
        self.c = lax.axis_index("ctx")
        self.f = lax.axis_index("fsdp")
        self.x_nbr, self.y_nbr, self.core = flip(self.c, 2), flip(self.c, 4), flip(self.c, 1)
        (
            self.core_send, self.core_recv, self.x_send, self.y_send, self.x_recv, self.y_recv,
            self.keep_l, self.keep_r, self.y2_send, self.x2_send, self.y2_recv, self.x2_recv,
            self.z_send, self.z_recv,
        ) = bufs
        self.send_sems, self.core_sems, self.xy_sems, self.xy2_sems, self.z_sems = sems
        self.open = {}
        self.others = [lax.rem(self.f + s, self.F) for s in range(1, self.F)]

    def at_ctx(self, other):
        return {"ctx": other, "fsdp": self.f}

    def at_f(self, other):
        return {"ctx": self.c, "fsdp": other}

    def greet(self):
        barrier = pltpu.get_barrier_semaphore()
        peers = [self.at_ctx(o) for o in (self.x_nbr, self.y_nbr, self.core)]
        peers += [self.at_f(o) for o in self.others]
        for peer in peers:
            pl.semaphore_signal(
                barrier, inc=1, device_id=peer, device_id_type=pl.DeviceIdType.MESH
            )
        pl.semaphore_wait(barrier, len(peers))

    def send(self, key, t, src, dst, recv_sem, target):
        copy = pltpu.make_async_remote_copy(
            src_ref=src, dst_ref=dst, send_sem=self.send_sems.at[key, t], recv_sem=recv_sem,
            device_id=target, device_id_type=pl.DeviceIdType.MESH,
        )
        copy.start()
        self.open[key, t] = copy

    def sent(self, key, t):
        if (key, t) in self.open:
            self.open.pop((key, t)).wait_send()

    def dest(self, t):
        return lax.rem(self.f + 1 + t, self.F)

    def left(self, t, base):
        rows = self.rows
        block = self.dest(t) * self.C
        parts = [
            self.left_ref[:, pl.ds(pl.multiple_of((block + cc) * rows, rows), rows)]
            for cc in (base, flip(base, 2), flip(base, 4), flip(flip(base, 2), 4))
        ]
        return jnp.concatenate(parts, axis=1).T

    def enter(self, t):
        self.for_core(t)
        self.first(t)

    def for_core(self, t, tile=512):
        self.sent(0, t - 2)
        left = self.left(t, self.core)

        @pl.loop(0, self.width // tile)
        def _(n):
            cols = pl.ds(pl.multiple_of(n * tile, tile), tile)
            self.core_send[t % 2, :, cols] = jnp.dot(
                left, self.w_ref[:, cols], preferred_element_type=F32
            ).astype(BF16)

        self.send(
            0, t, self.core_send.at[t % 2], self.core_recv.at[t], self.core_sems.at[t],
            self.at_ctx(self.core),
        )

    def first(self, t, tile=512):
        rows, mid = self.rows, self.width // 2
        left = self.left(t, self.c)
        arrived(self.core_recv.at[t], self.core_sems.at[t])
        for key, keep, out, recv, kept, sent_rows, target in (
            (1, self.keep_l, self.x_send, self.x_recv, (0, 2), (1, 3), self.x_nbr),
            (2, self.keep_r, self.y_send, self.y_recv, (0, 1), (2, 3), self.y_nbr),
        ):
            self.sent(key, t - 2)

            @pl.loop(0, mid // tile)
            def _(n):
                near = pl.ds(pl.multiple_of(n * tile, tile), tile)
                cols = pl.ds(pl.multiple_of((key - 1) * mid + n * tile, tile), tile)
                total = jnp.dot(left, self.w_ref[:, cols], preferred_element_type=F32)
                total = total + self.core_recv[t, :, cols].astype(F32)
                for i, b in enumerate(kept):
                    keep[t % 3, i * rows : (i + 1) * rows, near] = total[b * rows : (b + 1) * rows]
                for i, b in enumerate(sent_rows):
                    out[t % 2, i * rows : (i + 1) * rows, near] = total[
                        b * rows : (b + 1) * rows
                    ].astype(BF16)

            self.send(
                key, t, out.at[t % 2], recv.at[t], self.xy_sems.at[key - 1, t], self.at_ctx(target)
            )

    def second(self, t):
        rows = self.rows
        for key, keep, recv, sem, out, out_recv, target in (
            (3, self.keep_l, self.x_recv, 0, self.y2_send, self.y2_recv, self.y_nbr),
            (4, self.keep_r, self.y_recv, 1, self.x2_send, self.x2_recv, self.x_nbr),
        ):
            arrived(recv.at[t], self.xy_sems.at[sem, t])
            self.sent(key, t - 2)
            out[t % 2] = (keep[t % 3, rows:] + recv[t, rows:].astype(F32)).astype(BF16)
            self.send(
                key, t, out.at[t % 2], out_recv.at[t], self.xy2_sems.at[sem, t], self.at_ctx(target)
            )
            keep[t % 3, :rows] = keep[t % 3, :rows] + recv[t, :rows].astype(F32)

    def third(self, t):
        rows, mid = self.rows, self.width // 2
        arrived(self.y2_recv.at[t], self.xy2_sems.at[0, t])
        arrived(self.x2_recv.at[t], self.xy2_sems.at[1, t])
        total_l = self.keep_l[t % 3, :rows] + self.y2_recv[t].astype(F32)
        total_r = self.keep_r[t % 3, :rows] + self.x2_recv[t].astype(F32)
        if t < self.F - 1:
            self.z_send[t, :, :mid] = total_l.astype(BF16)
            self.z_send[t, :, mid:] = total_r.astype(BF16)
            self.send(
                5, t, self.z_send.at[t], self.z_recv.at[self.f], self.z_sems.at[self.f],
                self.at_f(self.dest(t)),
            )
            return None
        total = jnp.concatenate([total_l, total_r], axis=1)
        for o in self.others:
            arrived(self.z_recv.at[o], self.z_sems.at[o])
            total = total + self.z_recv[o].astype(F32)
        return total

    def run(self, pieces):
        F = self.F
        gaps = F + 1
        marks = [i * len(pieces) // gaps for i in range(gaps + 1)]

        def fill(i):
            for piece in pieces[marks[i] : marks[i + 1]]:
                piece()

        self.enter(0)
        self.enter(1)
        for t in range(F):
            fill(t)
            self.second(t)
            if t >= 1:
                self.third(t - 1)
            if t + 2 < F:
                self.enter(t + 2)
        fill(F)
        return self.third(F - 1)

    def finish(self):
        for key, t in list(self.open):
            self.sent(key, t)


def reduce_scratch(F, rows, width):
    mid = width // 2
    return [
        pltpu.VMEM((2, 4 * rows, width), BF16),
        pltpu.VMEM((F, 4 * rows, width), BF16),
        pltpu.VMEM((2, 2 * rows, mid), BF16),
        pltpu.VMEM((2, 2 * rows, mid), BF16),
        pltpu.VMEM((F, 2 * rows, mid), BF16),
        pltpu.VMEM((F, 2 * rows, mid), BF16),
        pltpu.VMEM((3, 2 * rows, mid), F32),
        pltpu.VMEM((3, 2 * rows, mid), F32),
        pltpu.VMEM((2, rows, mid), BF16),
        pltpu.VMEM((2, rows, mid), BF16),
        pltpu.VMEM((F, rows, mid), BF16),
        pltpu.VMEM((F, rows, mid), BF16),
        pltpu.VMEM((F - 1, rows, width), BF16),
        pltpu.VMEM((F, rows, width), BF16),
        pltpu.SemaphoreType.DMA((6, F)),
        pltpu.SemaphoreType.DMA((F,)),
        pltpu.SemaphoreType.DMA((2, F)),
        pltpu.SemaphoreType.DMA((2, F)),
        pltpu.SemaphoreType.DMA((F,)),
    ]


def backward_kernel(
    sizes, ff,
    mixed_ref, w_ref, x_ref, qkv, attended, totals, place, turn, cosine, sine, go_all, gates,
    result_ref, joint,
    go_buf, gate_buf, numer, ratio, key_rows, value_rows, place_col, grad_k, grad_v,
    go_sems, gate_sems, *shared,
):
    C, F = sizes
    rows = x_ref.shape[0]
    batch = C * rows
    reduce = Reduce(sizes, mixed_ref, w_ref, rows, shared[:14], shared[14:])
    count = F * batch // CHUNK
    refs = dict(
        grads=Stream(
            count,
            lambda i: go_all.at[
                i * CHUNK // batch, pl.ds(i * CHUNK % batch // rows, CHUNK // rows)
            ],
            go_buf, go_sems,
        ),
        gates=Stream(count, lambda i: gates.at[:, pl.ds(i * CHUNK, CHUNK)], gate_buf, gate_sems),
        w_out=w_ref, totals=totals, attended=attended, ratio=ratio, numer=numer, joint=joint,
        qkv=qkv, key_rows=key_rows, value_rows=value_rows, place_col=place_col, place=place,
        turn=turn, grad_k=grad_k, grad_v=grad_v, cos=cosine, sin=sine,
    )
    refs["grads"].start()
    refs["gates"].start()
    work = Backward(refs, batch, ff)
    pieces = []
    for b in range(F):
        for i in range(batch // CHUNK):
            pieces.append(functools.partial(work.mixed, b * (batch // CHUNK) + i))
        for t in range(batch // QT):
            pieces.append(functools.partial(work.attend, b, t))
    reduce.greet()
    total = reduce.run(pieces)
    result_ref[...] = (x_ref[...].astype(F32) + total).astype(BF16)
    reduce.finish()


def backward_all(mixed, w_out, x, qkv, attended, totals, place, turn, cosine, sine, go_all, gates, C, F):
    rows, width = x.shape
    ff = gates.shape[0] // 2
    batch, tokens = C * rows, C * F * rows
    vmem = pl.BlockSpec(memory_space=pltpu.VMEM)
    any_ = pl.BlockSpec(memory_space=pl.ANY)
    return pl.pallas_call(
        functools.partial(backward_kernel, (C, F), ff),
        out_shape=(
            jax.ShapeDtypeStruct((rows, width), BF16),
            jax.ShapeDtypeStruct((3 * HEAD + 2 * ff, tokens), BF16),
        ),
        in_specs=[vmem] * 10 + [any_] * 2,
        out_specs=(vmem,) * 2,
        scratch_shapes=[
            pltpu.VMEM((2, CHUNK // rows, rows, width), BF16),
            pltpu.VMEM((2, 2 * ff, CHUNK), F32),
            pltpu.VMEM((HEAD, tokens), BF16),
            pltpu.VMEM((1, tokens), F32),
            pltpu.VMEM((batch, HEAD), BF16),
            pltpu.VMEM((batch, HEAD), BF16),
            pltpu.VMEM((batch, 1), jnp.int32),
            pltpu.VMEM((HEAD, batch), F32),
            pltpu.VMEM((HEAD, batch), F32),
            pltpu.SemaphoreType.DMA((2,)),
            pltpu.SemaphoreType.DMA((2,)),
        ] + reduce_scratch(F, rows, width),
        compiler_params=pltpu.CompilerParams(
            collective_id=2, has_side_effects=True, vmem_limit_bytes=60 * 1024 * 1024
        ),
    )(mixed, w_out, x, qkv, attended, totals, place, turn, cosine, sine, go_all, gates)


SLAB = 256


def input_kernel(
    sizes,
    joint_ref, w_ref, mixed_ref, x_ref, go_ref, gain_ref, hid_all, go_all,
    grad_in_ref, terms_ref, dw_in_ref, dw_out_ref,
    slab_buf, slab_sems, *shared,
):
    C, F = sizes
    rows, width = x_ref.shape
    reduce = Reduce(sizes, joint_ref, w_ref, rows, shared[:14], shared[14:])
    count = width // SLAB
    slabs = Stream(
        2 * count,
        lambda i: (hid_all if i < count else go_all).at[:, :, :, pl.ds(i % count * SLAB, SLAB)],
        slab_buf, slab_sems,
    )
    slabs.start()

    def weight_grad(i):
        slab = slabs.take(i).reshape(C * F * rows, SLAB)
        left, out = (joint_ref, dw_in_ref) if i < count else (mixed_ref, dw_out_ref)
        out[:, i % count * SLAB : (i % count + 1) * SLAB] = jnp.dot(
            left[...], slab, preferred_element_type=F32
        ).astype(BF16)

    reduce.greet()
    total = reduce.run([functools.partial(weight_grad, i) for i in range(2 * count)])
    values = x_ref[...].astype(F32)
    centred = values - jnp.mean(values, axis=1, keepdims=True)
    inverse_std = lax.rsqrt(jnp.mean(centred * centred, axis=1, keepdims=True) + 1e-05)
    normed = centred * inverse_std
    terms_ref[0:1, :] = jnp.sum(total * normed, axis=0, keepdims=True)
    terms_ref[1:2, :] = jnp.sum(total, axis=0, keepdims=True)
    gain = jnp.concatenate([gain_ref[s].astype(F32) for s in range(F)], axis=1)
    g = total * gain
    back = inverse_std * (
        g - jnp.mean(g, axis=1, keepdims=True) - normed * jnp.mean(g * normed, axis=1, keepdims=True)
    )
    grad_in_ref[...] = (go_ref[...].astype(F32) + back).astype(BF16)
    reduce.finish()


def input_all(joint, w_in, mixed, x, go, gains, hid_all, go_all, C, F):
    rows, width = x.shape
    vmem = pl.BlockSpec(memory_space=pltpu.VMEM)
    any_ = pl.BlockSpec(memory_space=pl.ANY)
    return pl.pallas_call(
        functools.partial(input_kernel, (C, F)),
        out_shape=(
            jax.ShapeDtypeStruct((rows, width), BF16),
            jax.ShapeDtypeStruct((2, width), F32),
            jax.ShapeDtypeStruct((joint.shape[0], width), BF16),
            jax.ShapeDtypeStruct((mixed.shape[0], width), BF16),
        ),
        in_specs=[vmem] * 6 + [any_] * 2,
        out_specs=(vmem,) * 4,
        scratch_shapes=[
            pltpu.VMEM((2, F, C, rows, SLAB), BF16),
            pltpu.SemaphoreType.DMA((2,)),
        ] + reduce_scratch(F, rows, width),
        compiler_params=pltpu.CompilerParams(
            collective_id=4, has_side_effects=True, vmem_limit_bytes=60 * 1024 * 1024
        ),
    )(joint, w_in, mixed, x, go, gains, hid_all, go_all)


PIECES = ((0, 4), (4, 1), (5, 1), (6, 9))


def spread_kernel(
    sizes, shard_units,
    win_ref, wout_ref, terms_ref,
    win_all, wout_all, sums_ref,
    core_terms, x_terms, y_terms, part_terms, z_terms,
    send_sems, block_sems, piece_sems, term_sems,
):
    C, F = sizes
    c = lax.axis_index("ctx")
    f = lax.axis_index("fsdp")
    x_nbr, y_nbr, core = flip(c, 2), flip(c, 4), flip(c, 1)
    diag = flip(x_nbr, 4)
    copies = Copies(send_sems)
    per_rank, share = win_all.shape[2], win_all.shape[3]
    half = per_rank // 2
    att_units, ff_units = PIECES[0][1], sum(n for _, n in PIECES[1:])

    def at_ctx(other):
        return {"ctx": other, "fsdp": f}

    def at_f(other):
        return {"ctx": c, "fsdp": other}

    barrier = pltpu.get_barrier_semaphore()
    others = [lax.rem(f + s, F) for s in range(1, F)]
    for peer in [at_ctx(x_nbr), at_ctx(y_nbr), at_ctx(core)] + [at_f(o) for o in others]:
        pl.semaphore_signal(barrier, inc=1, device_id=peer, device_id_type=pl.DeviceIdType.MESH)
    pl.semaphore_wait(barrier, 3 + F - 1)

    def win_slice(dest):
        return win_ref.at[:, pl.ds(pl.multiple_of(dest * share, share), share)]

    def block(fb, cb, part):
        ref = win_all.at[fb, cb]
        return ref if part is None else ref.at[pl.ds(part * half, half)]

    def pass_block(fb, cb, part, target, src=None):
        ref = block(fb, cb, part)
        copies.send(ref if src is None else src, ref, block_sems.at[fb, cb, part or 0], target)

    def wait_block(fb, cb, part):
        arrived(block(fb, cb, part), block_sems.at[fb, cb, part or 0])

    def piece(fb, cb, p):
        rank = fb * C + cb
        start, units = PIECES[p]
        if p == 0:
            unit = rank * att_units
        else:
            unit = C * F * att_units + rank * ff_units + (start - att_units)
        place = pl.multiple_of(lax.rem(unit, shard_units) * UNIT, UNIT)
        return unit // shard_units, wout_all.at[pl.ds(place, units * UNIT)]

    def own_piece(p):
        start, units = PIECES[p]
        return wout_ref.at[pl.ds(start * UNIT, units * UNIT)]

    def pass_piece(fb, cb, p, target, when, src=None):
        ref = piece(fb, cb, p)[1]
        copies.send(ref if src is None else src, ref, piece_sems.at[fb, cb, p], target, when)

    def wait_piece(fb, cb, p, when):
        def go():
            arrived(piece(fb, cb, p)[1], piece_sems.at[fb, cb, p])
        pl.when(when)(go)

    for o in others:
        copies.send(win_slice(o), block(f, c, None), block_sems.at[f, c, 0], at_f(o))
    mine = win_slice(f)
    for target in (x_nbr, y_nbr, core):
        pass_block(f, c, None, at_ctx(target), src=mine)
    copies.local(mine, block(f, c, None))
    for p in range(len(PIECES)):
        shard, place = piece(f, c, p)
        for o in others:
            pass_piece(f, c, p, at_f(o), shard == o, src=own_piece(p))
        for target in (x_nbr, y_nbr, core):
            pass_piece(f, c, p, at_ctx(target), shard == f, src=own_piece(p))
        copies.local(own_piece(p), place, shard == f)

    total = terms_ref[...]
    for i, (target, buf) in enumerate(((core, core_terms), (x_nbr, x_terms), (y_nbr, y_terms))):
        part_terms[i] = total
        copies.send(part_terms.at[i], buf, term_sems.at[i], at_ctx(target))
        arrived(buf, term_sems.at[i])
        total = total + buf[...]
    for s in range(F):
        part_terms[3 + s, :, :share] = total[:, s * share : (s + 1) * share]
    for o in others:
        copies.send(
            part_terms.at[3 + o, :, pl.ds(0, share)], z_terms.at[f], term_sems.at[3 + f], at_f(o)
        )

    def z_step(fb):
        wait_block(fb, c, None)
        for target in (x_nbr, y_nbr, core):
            pass_block(fb, c, None, at_ctx(target))
        for p in range(len(PIECES)):
            here = piece(fb, c, p)[0] == f
            wait_piece(fb, c, p, here)
            for target in (x_nbr, y_nbr, core):
                pass_piece(fb, c, p, at_ctx(target), here)

    def xy_step(fb, way):
        wait_block(fb, x_nbr, None)
        pass_block(fb, x_nbr, 0, at_ctx(y_nbr))
        pass_block(fb, x_nbr, None, at_ctx(core))
        wait_block(fb, y_nbr, None)
        pass_block(fb, y_nbr, 1, at_ctx(x_nbr))
        pass_block(fb, y_nbr, None, at_ctx(core))
        for p in range(len(PIECES)):
            by_x = (p < 2) == (way == 0)
            for source, onward, turn in ((x_nbr, y_nbr, by_x), (y_nbr, x_nbr, not by_x)):
                here = piece(fb, source, p)[0] == f
                wait_piece(fb, source, p, here)
                if turn:
                    pass_piece(fb, source, p, at_ctx(onward), here)
                pass_piece(fb, source, p, at_ctx(core), here)

    def diag_step(fb):
        for part in (0, 1):
            wait_block(fb, diag, part)
            pass_block(fb, diag, part, at_ctx(core))
        for p in range(len(PIECES)):
            here = piece(fb, diag, p)[0] == f
            wait_piece(fb, diag, p, here)
            pass_piece(fb, diag, p, at_ctx(core), here)

    order = [f] + [lax.rem(f + F - s, F) for s in range(1, F)]
    for s in range(F + 2):
        if s + 1 < F:
            z_step(order[s + 1])
        if s < F:
            xy_step(order[s], s % 2)
        if 0 <= s - 1 < F:
            diag_step(order[s - 1])

    for fb in range(F):
        for cb in (core, flip(core, 2), flip(core, 4)):
            wait_block(fb, cb, None)
        for part in (0, 1):
            wait_block(fb, flip(flip(core, 2), 4), part)
        for cb in (core, flip(core, 2), flip(core, 4), flip(flip(core, 2), 4)):
            for p in range(len(PIECES)):
                wait_piece(fb, cb, p, piece(fb, cb, p)[0] == f)
    z_terms[f] = part_terms[3 + f, :, :share]
    for o in others:
        arrived(z_terms.at[o], term_sems.at[3 + o])
    total = z_terms[0]
    for s in range(1, F):
        total = total + z_terms[s]
    sums_ref[...] = total
    copies.finish()


def spread_all(dw_in, dw_out, terms, shard_rows, C, F):
    per_rank, width = dw_in.shape
    share = width // F
    any_ = pl.BlockSpec(memory_space=pl.ANY)
    vmem = pl.BlockSpec(memory_space=pltpu.VMEM)
    return pl.pallas_call(
        functools.partial(spread_kernel, (C, F), shard_rows // UNIT),
        out_shape=(
            jax.ShapeDtypeStruct((F, C, per_rank, share), BF16),
            jax.ShapeDtypeStruct((shard_rows, width), BF16),
            jax.ShapeDtypeStruct((2, share), F32),
        ),
        in_specs=[any_, any_, vmem],
        out_specs=(any_, any_, vmem),
        scratch_shapes=[
            pltpu.VMEM((2, width), F32),
            pltpu.VMEM((2, width), F32),
            pltpu.VMEM((2, width), F32),
            pltpu.VMEM((3 + F, 2, width), F32),
            pltpu.VMEM((F, 2, share), F32),
            pltpu.SemaphoreType.DMA((320,)),
            pltpu.SemaphoreType.DMA((F, C, 2)),
            pltpu.SemaphoreType.DMA((F, C, len(PIECES))),
            pltpu.SemaphoreType.DMA((3 + F,)),
        ],
        compiler_params=pltpu.CompilerParams(collective_id=3, has_side_effects=True),
    )(dw_in, dw_out, terms)


def turn_kernel(ff, src, out, in_buf, out_buf, in_sems, out_sems):
    F, C = src.shape[0], src.shape[1]
    share = src.shape[3]
    steps = []
    base = 0
    for row, size in ((0, HEAD), (HEAD, HEAD), (2 * HEAD, HEAD), (3 * HEAD, ff), (3 * HEAD + ff, ff)):
        for fb in range(F):
            steps.append((fb, row, size, base + fb * C * size))
        base += F * C * size

    def fetch(i):
        fb, row, size, _ = steps[i]
        return pltpu.make_async_copy(
            src.at[fb, :, pl.ds(row, size)], in_buf.at[i % 2, :, pl.ds(0, size)], in_sems.at[i % 2]
        )

    def store(i):
        _, _, size, col = steps[i]
        return pltpu.make_async_copy(
            out_buf.at[i % 2, :, pl.ds(0, C * size)], out.at[:, pl.ds(col, C * size)], out_sems.at[i % 2]
        )

    fetch(0).start()
    for i, (fb, row, size, col) in enumerate(steps):
        if i + 1 < len(steps):
            fetch(i + 1).start()
        fetch(i).wait()
        if i >= 2:
            store(i - 2).wait()
        block = in_buf[i % 2, :, :size, :].reshape(C * size, share).astype(F32)
        out_buf[i % 2, :, : C * size] = block.T
        store(i).start()
    store(len(steps) - 2).wait()
    store(len(steps) - 1).wait()


def turn_blocks(blocks, ff):
    F, C, per_rank, share = blocks.shape
    any_ = pl.BlockSpec(memory_space=pl.ANY)
    return pl.pallas_call(
        functools.partial(turn_kernel, ff),
        out_shape=jax.ShapeDtypeStruct((share, F * C * per_rank), F32),
        in_specs=[any_],
        out_specs=any_,
        scratch_shapes=[
            pltpu.VMEM((2, C, ff, share), BF16),
            pltpu.VMEM((2, share, C * ff), F32),
            pltpu.SemaphoreType.DMA((2,)),
            pltpu.SemaphoreType.DMA((2,)),
        ],
        compiler_params=pltpu.CompilerParams(vmem_limit_bytes=40 * 1024 * 1024),
    )(blocks)


def tp_body(C, F, inputs, gain, bias, in_weight, out_weight, grad_out, lengths, order):
    rows, width = inputs.shape[1:]
    T = C * F
    ff = FF // T
    scale = HEAD ** (-0.5)
    c = lax.axis_index("ctx")
    f = lax.axis_index("fsdp")
    x = inputs[0]
    go = grad_out[0]
    shard = in_weight.shape[0]

    slices = []
    for dest in range(F):
        rank = dest * C + c
        parts = [
            lax.dynamic_slice(in_weight, (0, base + rank * size), (shard, size))
            for base, size in (
                (0, HEAD), (width, HEAD), (2 * width, HEAD), (3 * width, ff), (3 * width + FF, ff)
            )
        ]
        slices.append(jnp.concatenate(parts, axis=1).T)
    win = jnp.stack(slices)
    count = lengths.shape[1] + order.shape[1]
    table = jnp.pad(jnp.concatenate([lengths, order], axis=1), ((0, 0), (0, 128 - count)))

    (
        go_all, hid_all, w_in, w_out, gains, qkv, gates, mixed, attended, totals, place, turn, cosine, sine
    ) = forward_all(x, go, gain[None], bias[None], table, win, out_weight, C, F)
    result, joint = backward_all(
        mixed, w_out, x, qkv, attended, totals, place, turn, cosine, sine, go_all, gates, C, F
    )
    grad_in, norm_terms, dw_in, dw_out = input_all(
        joint, w_in, mixed, x, go, gains, hid_all, go_all, C, F
    )
    blocks, out_rows, sums = spread_all(dw_in, dw_out, norm_terms, out_weight.shape[0], C, F)
    return (
        result[None], grad_in[None], turn_blocks(blocks, ff), out_rows.astype(F32), sums[0], sums[1]
    )


def solution(mesh):
    in_specs = (
        P("fsdp", "ctx", None),
        P("fsdp"),
        P("fsdp"),
        P("fsdp", None),
        P("fsdp", None),
        P("fsdp", "ctx", None),
        P("fsdp", None),
        P("fsdp", None),
    )
    out_specs = (
        P("fsdp", "ctx", None),
        P("fsdp", "ctx", None),
        P("fsdp", None),
        P("fsdp", None),
        P("fsdp"),
        P("fsdp"),
    )
    C, F = mesh.shape["ctx"], mesh.shape["fsdp"]
    if (C, F) == (8, 4):
        work = functools.partial(tp_body, C, F)
    else:
        work = body
    return jax.shard_map(work, mesh=mesh, in_specs=in_specs, out_specs=out_specs, check_vma=False)
```

```python
import functools
import math

import jax
import jax.numpy as jnp
from jax import lax
from jax.experimental import pallas as pl
from jax.experimental.pallas import tpu as pltpu
from jax.sharding import PartitionSpec as P

HEADS = 32
HEAD = 64
ROT = 16
FF = 5632
BLOCK = 64
BF16 = jnp.bfloat16
F32 = jnp.float32
UNIT = 16


def places_of(index, length_row, order_row):
    count = order_row.shape[0]
    hit = (index // BLOCK)[:, None] == jnp.arange(count, dtype=jnp.int32)[None, :]
    block_id = jnp.sum(jnp.where(hit, order_row[None, :], 0), axis=1)
    place = block_id * BLOCK + index % BLOCK
    ends = jnp.cumsum(length_row)
    starts = ends - length_row
    inside = (place[:, None] >= starts[None, :]) & (place[:, None] < ends[None, :])
    docs = jnp.sum(
        jnp.where(inside, jnp.arange(length_row.shape[0], dtype=jnp.int32)[None, :], 0), axis=1
    )
    first = jnp.sum(jnp.where(inside, starts[None, :], 0), axis=1)
    return (place, docs, place - first)


def rotate(values, positions, sign):
    half = ROT // 2
    freq = 10000.0 ** (-2.0 * jnp.arange(half, dtype=jnp.float32) / ROT)
    angle = positions.astype(jnp.float32)[:, None] * freq[None, :]
    cosine = jnp.cos(angle)[:, None, :]
    sine = sign * jnp.sin(angle)[:, None, :]
    first = values[..., :half]
    second = values[..., half:ROT]
    return jnp.concatenate(
        [first * cosine - second * sine, second * cosine + first * sine, values[..., ROT:]], axis=-1
    )


def rounded(values):
    return lax.optimization_barrier(values.astype(jnp.bfloat16)).astype(jnp.float32)


def transposed_dot(left, right):
    return lax.dot_general(
        left, right, (((0,), (0,)), ((), ())), preferred_element_type=jnp.float32
    )


def against_rows(left, right):
    return lax.dot_general(
        left, right, (((1,), (1,)), ((), ())), preferred_element_type=jnp.float32
    )


def body(inputs, gain, bias, in_weight, out_weight, grad_out, lengths, order):
    rows = inputs.shape[1]
    width = inputs.shape[2]
    length_row = lengths[0]
    order_row = order[0]
    local_index = lax.axis_index("ctx") * rows + jnp.arange(rows, dtype=jnp.int32)
    query_place, query_doc, query_turn = places_of(local_index, length_row, order_row)
    scale = HEAD ** (-0.5)
    head_shape = (rows, HEADS, HEAD)
    values_in = inputs[0].astype(jnp.float32)
    centred = values_in - jnp.mean(values_in, axis=1, keepdims=True)
    inverse_std = lax.rsqrt(jnp.mean(centred * centred, axis=1, keepdims=True) + 1e-05)
    normed = centred * inverse_std
    weight_piece = lax.all_gather(in_weight, "fsdp", axis=0, tiled=True)
    gain_piece = lax.all_gather(gain, "fsdp", axis=0, tiled=True)
    bias_piece = lax.all_gather(bias, "fsdp", axis=0, tiled=True)
    count = weight_piece.shape[0]
    columns = normed
    hidden_piece = (
        columns * gain_piece.astype(jnp.float32) + bias_piece.astype(jnp.float32)
    ).astype(jnp.bfloat16)
    joint_sum = jnp.dot(hidden_piece, weight_piece, preferred_element_type=jnp.float32)
    gain_full = gain_piece.astype(jnp.float32)
    joint, hidden_in, gain_full = (joint_sum, hidden_piece, gain_full)
    queries = rotate(joint[:, :width].reshape(head_shape), query_turn, 1.0).astype(jnp.bfloat16)
    keys = (
        rotate(joint[:, width : 2 * width].reshape(head_shape), query_turn, 1.0)
        .astype(jnp.bfloat16)
        .reshape(rows, width)
    )
    values = joint[:, 2 * width : 3 * width].astype(jnp.bfloat16)
    gate = joint[:, 3 * width : 3 * width + FF]
    upward = joint[:, 3 * width + FF :]

    def exp_scores(key_block, start, count):
        key_place, key_doc, unused_turn = places_of(
            start + jnp.arange(count, dtype=jnp.int32), length_row, order_row
        )
        scores = (
            jnp.einsum(
                "qhd,khd->hqk",
                queries,
                key_block.reshape(count, HEADS, HEAD),
                preferred_element_type=jnp.float32,
            )
            * scale
        )
        allowed = (query_doc[:, None] == key_doc[None, :]) & (
            key_place[None, :] <= query_place[:, None]
        )
        return jnp.where(allowed[None], jnp.exp(scores), 0.0)

    empty_attention = (jnp.zeros(head_shape, jnp.float32), jnp.zeros((HEADS, rows), jnp.float32))
    key_piece = lax.all_gather(keys, "ctx", axis=0, tiled=True)
    value_piece = lax.all_gather(values, "ctx", axis=0, tiled=True)
    count = key_piece.shape[0]
    block_rows = math.gcd(count, 512)

    def add_block(j, state):
        numer, totals = state
        offset = j * block_rows
        key_block = lax.dynamic_slice_in_dim(key_piece, offset, block_rows, 0)
        value_block = lax.dynamic_slice_in_dim(value_piece, offset, block_rows, 0)
        weights = exp_scores(key_block, offset, block_rows)
        totals = totals + jnp.sum(weights, axis=2)
        numer = numer + jnp.einsum(
            "hqk,khd->qhd",
            weights.astype(jnp.bfloat16),
            value_block.reshape(block_rows, HEADS, HEAD),
            preferred_element_type=jnp.float32,
        )
        return (numer, totals)

    numer, totals = lax.fori_loop(0, count // block_rows, add_block, empty_attention)
    attended = numer / jnp.transpose(totals)[:, :, None]
    sigmoid_gate = jax.nn.sigmoid(gate)
    activated = gate * sigmoid_gate * upward
    mixed_in = jnp.concatenate(
        [attended.reshape(rows, width).astype(jnp.bfloat16), activated.astype(jnp.bfloat16)], axis=1
    )
    columns = mixed_in
    mixed = jnp.dot(
        columns,
        lax.all_gather(out_weight, "fsdp", axis=0, tiled=True),
        preferred_element_type=jnp.float32,
    )
    result = (values_in + mixed).astype(jnp.bfloat16)
    grad_rows = grad_out[0]
    grad_mixed = against_rows(grad_rows, lax.all_gather(out_weight, "fsdp", axis=0, tiled=True))
    grad_att = grad_mixed[:, :width].astype(jnp.bfloat16).reshape(head_shape)
    grad_act = rounded(grad_mixed[:, width:])
    grad_gate = grad_act * upward * sigmoid_gate * (1.0 + gate * (1.0 - sigmoid_gate))
    grad_up = grad_act * gate * sigmoid_gate
    delta = jnp.transpose(jnp.sum(grad_att.astype(jnp.float32) * attended, axis=2))
    grad_numer = (grad_att.astype(jnp.float32) / jnp.transpose(totals)[:, :, None]).astype(
        jnp.bfloat16
    )
    ratio = delta / totals
    keys_all, values_all = (
        lax.all_gather(keys, "ctx", axis=0, tiled=True),
        lax.all_gather(values, "ctx", axis=0, tiled=True),
    )
    group = keys_all.shape[0]

    def score_grads(key_block, value_block, start, count):
        weights = exp_scores(key_block, start, count)
        pushed = jnp.einsum(
            "qhd,khd->hqk",
            grad_numer,
            value_block.reshape(count, HEADS, HEAD),
            preferred_element_type=jnp.float32,
        )
        return (weights, (weights * (pushed - ratio[:, :, None])).astype(jnp.bfloat16))

    query_rows = math.gcd(group, 512)

    def query_block_grad(j, total):
        offset = j * query_rows
        key_block = lax.dynamic_slice_in_dim(keys_all, offset, query_rows, 0)
        value_block = lax.dynamic_slice_in_dim(values_all, offset, query_rows, 0)
        unused_weights, grad_scores = score_grads(key_block, value_block, offset, query_rows)
        return total + jnp.einsum(
            "hqk,khd->qhd",
            grad_scores,
            key_block.reshape(query_rows, HEADS, HEAD),
            preferred_element_type=jnp.float32,
        )

    grad_query = (
        lax.fori_loop(0, group // query_rows, query_block_grad, jnp.zeros(head_shape, jnp.float32))
        * scale
    )
    key_block_rows = math.gcd(rows * lax.axis_size("ctx"), 512)

    def key_block_grad(j, terms):
        offset = j * key_block_rows
        key_block = lax.dynamic_slice_in_dim(keys_all, offset, key_block_rows, 0)
        value_block = lax.dynamic_slice_in_dim(values_all, offset, key_block_rows, 0)
        weights, grad_scores = score_grads(key_block, value_block, offset, key_block_rows)
        key_part = (
            jnp.einsum("hqk,qhd->khd", grad_scores, queries, preferred_element_type=jnp.float32)
            * scale
        )
        value_part = jnp.einsum(
            "hqk,qhd->khd",
            weights.astype(jnp.bfloat16),
            grad_numer,
            preferred_element_type=jnp.float32,
        )
        block_terms = jnp.concatenate(
            [key_part.reshape(key_block_rows, width), value_part.reshape(key_block_rows, width)],
            axis=1,
        )
        return lax.dynamic_update_slice_in_dim(terms, block_terms, j * key_block_rows, 0)

    key_value_grad = lax.psum_scatter(
        lax.fori_loop(
            0,
            rows * lax.axis_size("ctx") // key_block_rows,
            key_block_grad,
            jnp.zeros((rows * lax.axis_size("ctx"), 2 * width), jnp.float32),
        ).astype(jnp.bfloat16),
        "ctx",
        scatter_dimension=0,
        tiled=True,
    ).astype(jnp.float32)
    grad_key = rotate(key_value_grad[:, :width].reshape(head_shape), query_turn, -1.0).reshape(
        rows, width
    )
    grad_query = rotate(grad_query, query_turn, -1.0).reshape(rows, width)
    grad_joint = jnp.concatenate(
        [
            grad_query.astype(jnp.bfloat16),
            grad_key.astype(jnp.bfloat16),
            key_value_grad[:, width:].astype(jnp.bfloat16),
            grad_gate.astype(jnp.bfloat16),
            grad_up.astype(jnp.bfloat16),
        ],
        axis=1,
    )
    grad_hidden = against_rows(grad_joint, lax.all_gather(in_weight, "fsdp", axis=0, tiled=True))
    grad_normed = grad_hidden * gain_full[None, :]
    grad_inputs = inverse_std * (
        grad_normed
        - jnp.mean(grad_normed, axis=1, keepdims=True)
        - normed * jnp.mean(grad_normed * normed, axis=1, keepdims=True)
    )
    grad_in = (grad_rows.astype(jnp.float32) + grad_inputs).astype(jnp.bfloat16)
    norm_terms = jnp.stack([jnp.sum(grad_hidden * normed, axis=0), jnp.sum(grad_hidden, axis=0)])
    norm_totals = lax.psum(norm_terms, ("ctx", "fsdp"))
    shards = lax.axis_size("fsdp")
    share = width // shards
    gain_grad = lax.dynamic_slice_in_dim(norm_totals[0], lax.axis_index("fsdp") * share, share, 0)
    bias_grad = lax.dynamic_slice_in_dim(norm_totals[1], lax.axis_index("fsdp") * share, share, 0)

    def column_terms(source, partner):
        return transposed_dot(source, partner)

    parts = lax.axis_size("ctx")

    def reorder(matrix):
        columns = matrix.shape[1]
        return (
            matrix.reshape(rows, shards, parts, columns // (shards * parts))
            .transpose(0, 2, 1, 3)
            .reshape(rows, columns)
        )

    in_piece = lax.psum_scatter(
        column_terms(reorder(hidden_in), grad_joint),
        ("ctx", "fsdp"),
        scatter_dimension=0,
        tiled=True,
    )
    out_piece = lax.psum_scatter(
        column_terms(reorder(mixed_in), grad_rows), ("ctx", "fsdp"), scatter_dimension=0, tiled=True
    )
    in_weight_grad, out_weight_grad = (
        lax.all_gather(in_piece.astype(jnp.bfloat16), "ctx", axis=0, tiled=True).astype(
            in_piece.dtype
        ),
        lax.all_gather(out_piece.astype(jnp.bfloat16), "ctx", axis=0, tiled=True).astype(
            out_piece.dtype
        ),
    )
    return (result[None], grad_in[None], in_weight_grad, out_weight_grad, gain_grad, bias_grad)


def flip(index, bit):
    return index + bit - 2 * bit * ((index // bit) % 2)


class Copies:
    def __init__(self, sems):
        self.sems = sems
        self.used = 0
        self.open = []

    def send(self, src, dst, recv_sem, target, when=None):
        copy = pltpu.make_async_remote_copy(
            src_ref=src,
            dst_ref=dst,
            send_sem=self.sems.at[self.used],
            recv_sem=recv_sem,
            device_id=target,
            device_id_type=pl.DeviceIdType.MESH,
        )
        self.used += 1
        self.open.append((copy.wait_send, when, False))
        if when is None:
            copy.start()
        else:
            pl.when(when)(copy.start)

    def local(self, src, dst, when=None):
        copy = pltpu.make_async_copy(src, dst, self.sems.at[self.used])
        self.used += 1
        if when is None:
            copy.start()
        else:
            pl.when(when)(copy.start)
        self.open.append((copy.wait, when, True))

    def finish_local(self):
        self.finish([item for item in self.open if item[2]])
        self.open = [item for item in self.open if not item[2]]

    def finish(self, items=None):
        for done, when, _ in self.open if items is None else items:
            if when is None:
                done()
            else:
                pl.when(when)(done)


def arrived(ref, recv_sem):
    pltpu.make_async_copy(ref, ref, recv_sem).wait()


def owner_of_unit(unit, att_units, ff_units, heads):
    first = heads * att_units
    is_att = (unit < first).astype(jnp.int32) if hasattr(unit, "astype") else int(unit < first)
    return is_att * (unit // att_units) + (1 - is_att) * ((unit - first) // ff_units)


LOG2E = 1.4426950408889634
CHUNK = 512
QT = 256


class Stream:
    def __init__(self, count, source, buf, sems):
        self.count, self.source, self.buf, self.sems = count, source, buf, sems

    def copy(self, i):
        return pltpu.make_async_copy(self.source(i), self.buf.at[i % 2], self.sems.at[i % 2])

    def start(self):
        self.copy(0).start()

    def take(self, i):
        if i + 1 < self.count:
            self.copy(i + 1).start()
        self.copy(i).wait()
        return self.buf[i % 2]


def turn_pair(values, cosine, sine):
    half = ROT // 2
    first, second = values[:half], values[half:ROT]
    return jnp.concatenate(
        [first * cosine - second * sine, second * cosine + first * sine, values[ROT:]], axis=0
    )


def nt_dot(left, right):
    return lax.dot_general(left, right, (((1,), (1,)), ((), ())), preferred_element_type=F32)


def token_tables(row, batch, docs):
    index = lax.broadcasted_iota(jnp.int32, (1, batch), 1)
    place = index % BLOCK
    block = index // BLOCK
    for j in range(batch // BLOCK):
        place = place + jnp.where(block == j, row[:, docs + j : docs + j + 1] * BLOCK, 0)
    start = jnp.zeros((1, 1), jnp.int32)
    first = jnp.zeros((1, batch), jnp.int32)
    for j in range(docs):
        first = jnp.where(place >= start, start, first)
        start = start + row[:, j : j + 1]
    return place, place - first


def as_column(row):
    return jnp.broadcast_to(row, (8, row.shape[1])).T[:, :1]


def allowed_keys(place_col, place_row, turn_row):
    return (place_col <= place_row) & (place_col >= place_row - turn_row)


class Forward:
    def __init__(self, refs, batch, ff):
        self.r, self.batch, self.ff = refs, batch, ff

    def tables(self, b):
        r, batch = self.r, self.batch
        place, turn = token_tables(r["table"][b], batch, 4)
        r["place"][b] = place
        r["turn"][b] = turn
        pair = lax.broadcasted_iota(jnp.int32, (ROT // 2, 1), 0).astype(F32)
        freq = jnp.exp2(pair * (-2.0 * math.log2(10000.0) / ROT))
        angle = turn.astype(F32) * freq
        r["cos"][:, b * batch : (b + 1) * batch] = jnp.cos(angle)
        r["sin"][:, b * batch : (b + 1) * batch] = jnp.sin(angle)

    def project(self, i):
        r, ff = self.r, self.ff
        cols = slice(i * CHUNK, (i + 1) * CHUNK)
        hidden = r["hidden"].take(i).reshape(CHUNK, -1)
        joint = nt_dot(r["w_in"][...], hidden)
        cosine, sine = r["cos"][:, cols], r["sin"][:, cols]
        r["qkv"][:HEAD, cols] = turn_pair(joint[:HEAD], cosine, sine).astype(BF16)
        r["qkv"][HEAD : 2 * HEAD, cols] = turn_pair(joint[HEAD : 2 * HEAD], cosine, sine).astype(BF16)
        r["qkv"][2 * HEAD : 3 * HEAD, cols] = joint[2 * HEAD : 3 * HEAD].astype(BF16)
        slot = i % 2
        if i >= 2:
            self.gates(i - 2).wait()
        gate, upward = joint[3 * HEAD : 3 * HEAD + ff], joint[3 * HEAD + ff :]
        r["gate_buf"][slot, :ff] = gate
        r["gate_buf"][slot, ff:] = upward
        r["mixed"][HEAD:, cols] = (gate * jax.nn.sigmoid(gate) * upward).astype(BF16)
        self.gates(i).start()

    def gates(self, i):
        r = self.r
        return pltpu.make_async_copy(
            r["gate_buf"].at[i % 2], r["gates"].at[:, pl.ds(i * CHUNK, CHUNK)], r["gate_sems"].at[i % 2]
        )

    def attend(self, b, t):
        r, batch = self.r, self.batch
        whole = slice(b * batch, (b + 1) * batch)
        if t == 0:
            r["key_rows"][...] = r["qkv"][HEAD : 2 * HEAD, whole].T
            r["place_col"][...] = as_column(r["place"][b])
        cols = slice(b * batch + t * QT, b * batch + (t + 1) * QT)
        here = slice(t * QT, (t + 1) * QT)
        place, turn = r["place"][b, :, here], r["turn"][b, :, here]
        query = r["qkv"][:HEAD, cols]
        totals = jnp.zeros((1, QT), F32)
        numer = jnp.zeros((HEAD, QT), F32)
        for k in range(batch // QT):
            keys = slice(k * QT, (k + 1) * QT)
            scores = jnp.dot(r["key_rows"][keys], query, preferred_element_type=F32)
            ok = allowed_keys(r["place_col"][keys], place, turn)
            weights = jnp.where(ok, jnp.exp2(scores * (LOG2E * HEAD**-0.5)), 0.0)
            totals = totals + jnp.sum(weights, axis=0, keepdims=True)
            value = r["qkv"][2 * HEAD :, b * batch + k * QT : b * batch + (k + 1) * QT]
            numer = numer + jnp.dot(value, weights.astype(BF16), preferred_element_type=F32)
        attended = numer / totals
        r["attended"][:, cols] = attended
        r["totals"][:, cols] = totals
        r["mixed"][:HEAD, cols] = attended.astype(BF16)


def forward_kernel(
    sizes, ff,
    x_ref, go_ref, gain_ref, bias_ref, table_ref, weight_ref, wout_ref,
    go_all, hid_all, win_all, wout_all, gain_buf,
    qkv, gates, mixed, attended, totals, place, turn, cosine, sine,
    table_all, bias_buf, hid_own, win_buf, win_ref, thin_buf, thick_buf, turn_buf, hidden_buf, gate_buf, key_rows, place_col,
    send_sems, block_sems, small_sems, win_sems, wout_sems, hidden_sems, gate_sems, load_sem, slice_sems,
):
    C, F = sizes
    c = lax.axis_index("ctx")
    f = lax.axis_index("fsdp")
    x_nbr, y_nbr, core = flip(c, 2), flip(c, 4), flip(c, 1)
    diag = flip(x_nbr, 4)
    copies = Copies(send_sems)
    here = {"ctx": c, "fsdp": f}

    def at_ctx(other):
        return {"ctx": other, "fsdp": f}

    def at_f(other):
        return {"ctx": c, "fsdp": other}

    width = x_ref.shape[1]
    total_cols = weight_ref.shape[1]
    segments = (
        (0, HEAD, 0), (width, HEAD, HEAD), (2 * width, HEAD, 2 * HEAD),
        (3 * width, ff, 3 * HEAD), (3 * width + FF, ff, 3 * HEAD + ff),
    )

    def cut(dest, k):
        base, size, row = segments[k]
        buf = thin_buf.at[dest, k] if k < 3 else thick_buf.at[dest, k - 3]
        wide = buf.shape[1]
        start = base + (dest * C + c) * size
        first = jnp.minimum(start // 128 * 128, total_cols - wide)
        copy = pltpu.make_async_copy(
            weight_ref.at[:, pl.ds(pl.multiple_of(first, 128), wide)], buf, slice_sems.at[dest, k]
        )
        return copy, start - first, size, row, wide

    for dest in range(F):
        for k in range(len(segments)):
            cut(dest, k)[0].start()

    barrier = pltpu.get_barrier_semaphore()
    others = [lax.rem(f + s, F) for s in range(1, F)]
    for peer in [at_ctx(x_nbr), at_ctx(y_nbr), at_ctx(core)] + [at_f(o) for o in others]:
        pl.semaphore_signal(barrier, inc=1, device_id=peer, device_id_type=pl.DeviceIdType.MESH)
    pl.semaphore_wait(barrier, 3 + F - 1)

    for i, o in enumerate(others):
        copies.send(gain_ref, gain_buf.at[f], small_sems.at[0, f], at_f(o))
        copies.send(bias_ref, bias_buf.at[f], small_sems.at[1, f], at_f(o))
        copies.send(table_ref, table_all.at[f], small_sems.at[2, f], at_f(o))

    outs = (go_all, hid_all)
    rows = x_ref.shape[0]
    half = rows // 2

    def piece(a, fb, cb, part):
        ref = outs[a].at[fb, cb]
        if part is None:
            return ref
        return ref.at[pl.ds(part * half, half)]

    def forward(a, fb, cb, part, target, when=None, src=None):
        ref = piece(a, fb, cb, part)
        copies.send(ref if src is None else src, ref, block_sems.at[a, fb, cb, part or 0], target, when)

    def wait_block(a, fb, cb, part, when=None):
        def go():
            arrived(piece(a, fb, cb, part), block_sems.at[a, fb, cb, part or 0])
        if when is None:
            go()
        else:
            pl.when(when)(go)

    up, down = f + 1 < F, f > 0

    def own_xy(a, src):
        forward(a, f, c, None, at_ctx(x_nbr), src=src)
        forward(a, f, c, None, at_ctx(y_nbr), src=src)
        forward(a, f, c, None, at_ctx(core), src=src)

    def own_z(a, src):
        forward(a, f, c, None, at_f(f + 1), when=up, src=src)
        forward(a, f, c, None, at_f(f - 1), when=down, src=src)

    values = x_ref[...].astype(F32)
    centred = values - jnp.mean(values, axis=1, keepdims=True)
    normed = centred * lax.rsqrt(jnp.mean(centred * centred, axis=1, keepdims=True) + 1e-05)
    gain_buf[f] = gain_ref[...]
    bias_buf[f] = bias_ref[...]
    for o in others:
        arrived(gain_buf.at[o], small_sems.at[0, o])
        arrived(bias_buf.at[o], small_sems.at[1, o])
    share = gain_ref.shape[1]
    for s in range(F):
        cols = slice(s * share, (s + 1) * share)
        hid_own[:, cols] = (
            normed[:, cols] * gain_buf[s].astype(F32) + bias_buf[s].astype(F32)
        ).astype(BF16)
    own_z(1, hid_own)
    own_xy(1, hid_own)
    copies.local(hid_own, hid_all.at[f, c])
    copies.local(go_ref, go_all.at[f, c])

    share_rows = weight_ref.shape[0]

    def win_place(src_f):
        return win_all.at[:, pl.ds(pl.multiple_of(src_f * share_rows, share_rows), share_rows)]

    def win_send(shift):
        o = lax.rem(f + shift, F)
        copies.send(win_ref.at[o], win_place(f), win_sems.at[f], at_f(o))

    def win_wait(shift):
        o = lax.rem(f + F - shift, F)
        arrived(win_place(o), win_sems.at[o])

    def slice_weights():
        for k in range(len(segments)):
            @pl.loop(0, F)
            def _(dest):
                copy, shift, size, row, wide = cut(dest, k)
                copy.wait()
                buf = thin_buf.at[dest, k] if k < 3 else thick_buf.at[dest, k - 3]
                turn_buf[:wide] = buf[...].T
                win_ref[dest, row : row + size] = turn_buf[pl.ds(pl.multiple_of(shift, UNIT), size)]

        copies.local(win_ref.at[f], win_place(f))

    units_per_shard = wout_ref.shape[0] // UNIT
    att_units, ff_units = HEAD // UNIT * (HEADS // (C * F)), FF // (C * F) // UNIT

    def unit_of(rank, i):
        if i < att_units:
            return rank * att_units + i
        return C * F * att_units + rank * ff_units + (i - att_units)

    def unit_rows(ref, unit):
        return ref.at[pl.ds(pl.multiple_of(unit * UNIT, UNIT), UNIT)]

    def wout_sends():
        for step in range(F):
            dest = lax.rem(f + step, F)
            rank = dest * C + c
            for i in range(att_units + ff_units):
                unit = unit_of(rank, i)
                mine = unit // units_per_shard == f
                src = unit_rows(wout_ref, lax.rem(unit, units_per_shard))
                dst = wout_all.at[pl.ds(i * UNIT, UNIT)]
                if step == 0:
                    copy = pltpu.make_async_copy(src, dst, wout_sems.at[i])
                    pl.when(mine)(copy.start)
                else:
                    copies.send(src, dst, wout_sems.at[i], at_f(dest), when=mine)

    def blocks_of(s):
        if s == 0:
            return [(-1, f, None)]
        return [(-1, f - s, f - s >= 0), (1, f + s, f + s < F)]

    def z_step(a, s):
        for sign, fb, valid in blocks_of(s):
            onward = valid & (up if sign < 0 else down)
            wait_block(a, fb, c, None, when=valid)
            forward(a, fb, c, None, at_f(f - sign), when=onward)
            for target in (x_nbr, y_nbr, core):
                forward(a, fb, c, None, at_ctx(target), when=valid)

    def xy_step(a, s):
        for _, fb, valid in blocks_of(s):
            wait_block(a, fb, x_nbr, None, when=valid)
            forward(a, fb, x_nbr, 0, at_ctx(y_nbr), when=valid)
            forward(a, fb, x_nbr, None, at_ctx(core), when=valid)
            wait_block(a, fb, y_nbr, None, when=valid)
            forward(a, fb, y_nbr, 1, at_ctx(x_nbr), when=valid)
            forward(a, fb, y_nbr, None, at_ctx(core), when=valid)

    def diag_step(a, s):
        for _, fb, valid in blocks_of(s):
            for part in (0, 1):
                wait_block(a, fb, diag, part, when=valid)
                forward(a, fb, diag, part, at_ctx(core), when=valid)

    def from_core(a):
        for fb in range(F):
            wait_block(a, fb, core, None)
            wait_block(a, fb, flip(core, 2), None)
            wait_block(a, fb, flip(core, 4), None)
            for part in (0, 1):
                wait_block(a, fb, flip(flip(core, 2), 4), part)

    batch = C * rows
    refs = dict(
        table=table_all, place=place, turn=turn, cos=cosine, sin=sine, w_in=win_buf, qkv=qkv,
        gates=gates, gate_buf=gate_buf, gate_sems=gate_sems, mixed=mixed, attended=attended,
        totals=totals, key_rows=key_rows, place_col=place_col,
        hidden=Stream(
            F * batch // CHUNK,
            lambda i: hid_all.at[
                i * CHUNK // batch, pl.ds(i * CHUNK % batch // rows, CHUNK // rows)
            ],
            hidden_buf, hidden_sems,
        ),
    )
    work = Forward(refs, batch, ff)

    for o in others:
        arrived(table_all.at[o], small_sems.at[2, o])
    table_all[f] = table_ref[...]
    for b in range(F):
        work.tables(b)
    slice_weights()

    z_step(1, 1)
    xy_step(1, 0)
    z_step(1, 2)
    win_send(1)
    xy_step(1, 1)
    diag_step(1, 0)
    z_step(1, 3)
    win_send(2)
    xy_step(1, 2)
    diag_step(1, 1)
    own_z(0, go_ref)
    xy_step(1, 3)
    own_xy(0, go_ref)
    win_wait(1)
    win_wait(2)
    win_send(3)
    diag_step(1, 2)
    diag_step(1, 3)
    z_step(0, 1)
    xy_step(0, 0)
    from_core(1)
    copies.finish_local()
    refs["hidden"].start()
    win_wait(3)
    load = pltpu.make_async_copy(win_all, win_buf, load_sem)
    load.start()
    wout_sends()
    load.wait()

    pieces = []
    for b in range(F):
        for i in range(batch // CHUNK):
            pieces.append(functools.partial(work.project, b * (batch // CHUNK) + i))
        for t in range(batch // QT):
            pieces.append(functools.partial(work.attend, b, t))
    steps = [
        functools.partial(z_step, 0, 2),
        functools.partial(xy_step, 0, 1),
        functools.partial(diag_step, 0, 0),
        functools.partial(z_step, 0, 3),
        functools.partial(xy_step, 0, 2),
        functools.partial(diag_step, 0, 1),
        functools.partial(xy_step, 0, 3),
        functools.partial(diag_step, 0, 2),
        functools.partial(diag_step, 0, 3),
    ]
    weave(steps, pieces)
    from_core(0)
    for i in range(att_units + ff_units):
        arrived(wout_all.at[pl.ds(i * UNIT, UNIT)], wout_sems.at[i])
    last = F * batch // CHUNK
    work.gates(last - 2).wait()
    work.gates(last - 1).wait()
    copies.finish()


def weave(steps, pieces):
    done = 0
    for i, step in enumerate(steps):
        until = (i + 1) * len(pieces) // len(steps)
        for piece in pieces[done:until]:
            piece()
        done = until
        step()


def forward_all(x, go, gain, bias, table, in_weight, wout, C, F):
    rows, width = x.shape
    shard = in_weight.shape[0]
    any_ = pl.BlockSpec(memory_space=pl.ANY)
    vmem = pl.BlockSpec(memory_space=pltpu.VMEM)
    ff = FF // (C * F)
    wout_rows = HEAD * HEADS // (C * F) + ff
    per_rank = 3 * HEAD + 2 * ff
    share = gain.shape[1]
    batch = C * rows
    tokens = F * batch
    shape = jax.ShapeDtypeStruct
    return pl.pallas_call(
        functools.partial(forward_kernel, (C, F), ff),
        out_shape=(
            shape((F, C, rows, width), BF16),
            shape((F, C, rows, width), BF16),
            shape((per_rank, width), BF16),
            shape((wout_rows, width), BF16),
            shape((F, 1, share), BF16),
            shape((3 * HEAD, tokens), BF16),
            shape((2 * ff, tokens), F32),
            shape((HEAD + ff, tokens), BF16),
            shape((HEAD, tokens), F32),
            shape((1, tokens), F32),
            shape((F, 1, batch), jnp.int32),
            shape((F, 1, batch), jnp.int32),
            shape((ROT // 2, tokens), F32),
            shape((ROT // 2, tokens), F32),
        ),
        in_specs=[vmem, any_, vmem, vmem, vmem, any_, any_],
        out_specs=(any_,) * 4 + (vmem, vmem, any_) + (vmem,) * 7,
        scratch_shapes=[
            pltpu.VMEM((F,) + table.shape, jnp.int32),
            pltpu.VMEM((F, 1, share), BF16),
            pltpu.VMEM((rows, width), BF16),
            pltpu.VMEM((per_rank, width), BF16),
            pltpu.VMEM((F, per_rank, shard), BF16),
            pltpu.VMEM((F, 3, shard, 128), BF16),
            pltpu.VMEM((F, 2, shard, 384), BF16),
            pltpu.VMEM((384, shard), BF16),
            pltpu.VMEM((2, CHUNK // rows, rows, width), BF16),
            pltpu.VMEM((2, 2 * ff, CHUNK), F32),
            pltpu.VMEM((batch, HEAD), BF16),
            pltpu.VMEM((batch, 1), jnp.int32),
            pltpu.SemaphoreType.DMA((256,)),
            pltpu.SemaphoreType.DMA((2, F, C, 2)),
            pltpu.SemaphoreType.DMA((3, F)),
            pltpu.SemaphoreType.DMA((F,)),
            pltpu.SemaphoreType.DMA((wout_rows // UNIT,)),
            pltpu.SemaphoreType.DMA((2,)),
            pltpu.SemaphoreType.DMA((2,)),
            pltpu.SemaphoreType.DMA,
            pltpu.SemaphoreType.DMA((F, 5)),
        ],
        compiler_params=pltpu.CompilerParams(
            collective_id=1, has_side_effects=True, vmem_limit_bytes=56 * 1024 * 1024
        ),
    )(x, go, gain, bias, table, in_weight, wout)


def scores_of(key_rows, query, place_col, place, turn):
    scores = jnp.dot(key_rows, query, preferred_element_type=F32)
    ok = allowed_keys(place_col, place, turn)
    return jnp.where(ok, jnp.exp2(scores * (LOG2E * HEAD**-0.5)), 0.0)


class Backward:
    def __init__(self, refs, batch, ff):
        self.r, self.batch, self.ff = refs, batch, ff

    def mixed(self, i):
        r, ff = self.r, self.ff
        cols = slice(i * CHUNK, (i + 1) * CHUNK)
        grads = r["grads"].take(i).reshape(CHUNK, -1)
        grad = nt_dot(r["w_out"][...], grads)
        gates = r["gates"].take(i)
        grad_att = grad[:HEAD].astype(BF16).astype(F32)
        inverse = 1.0 / r["totals"][:, cols]
        delta = jnp.sum(grad_att * r["attended"][:, cols], axis=0, keepdims=True)
        r["ratio"][:, cols] = delta * inverse
        r["numer"][:, cols] = (grad_att * inverse).astype(BF16)
        grad_act = grad[HEAD:].astype(BF16).astype(F32)
        gate, upward = gates[:ff], gates[ff:]
        sig = jax.nn.sigmoid(gate)
        r["joint"][3 * HEAD : 3 * HEAD + ff, cols] = (
            grad_act * upward * sig * (1.0 + gate * (1.0 - sig))
        ).astype(BF16)
        r["joint"][3 * HEAD + ff :, cols] = (grad_act * gate * sig).astype(BF16)

    def attend(self, b, t):
        r, batch = self.r, self.batch
        whole = slice(b * batch, (b + 1) * batch)
        if t == 0:
            r["key_rows"][...] = r["qkv"][HEAD : 2 * HEAD, whole].T
            r["value_rows"][...] = r["qkv"][2 * HEAD :, whole].T
            r["place_col"][...] = as_column(r["place"][b])
            r["grad_k"][...] = jnp.zeros_like(r["grad_k"])
            r["grad_v"][...] = jnp.zeros_like(r["grad_v"])
        cols = slice(b * batch + t * QT, b * batch + (t + 1) * QT)
        here = slice(t * QT, (t + 1) * QT)
        place, turn = r["place"][b, :, here], r["turn"][b, :, here]
        query, numer, ratio = r["qkv"][:HEAD, cols], r["numer"][:, cols], r["ratio"][:, cols]
        grad_q = jnp.zeros((HEAD, QT), F32)
        for k in range(batch // QT):
            keys = slice(k * QT, (k + 1) * QT)
            key_cols = slice(b * batch + k * QT, b * batch + (k + 1) * QT)
            weights = scores_of(r["key_rows"][keys], query, r["place_col"][keys], place, turn)
            pushed = jnp.dot(r["value_rows"][keys], numer, preferred_element_type=F32)
            grad_scores = (weights * (pushed - ratio)).astype(BF16)
            grad_q = grad_q + jnp.dot(
                r["qkv"][HEAD : 2 * HEAD, key_cols], grad_scores, preferred_element_type=F32
            )
            r["grad_k"][:, keys] += nt_dot(query, grad_scores)
            r["grad_v"][:, keys] += nt_dot(numer, weights.astype(BF16))
        scale = HEAD**-0.5
        r["joint"][:HEAD, cols] = turn_pair(
            grad_q * scale, r["cos"][:, cols], -r["sin"][:, cols]
        ).astype(BF16)
        if t == batch // QT - 1:
            r["joint"][HEAD : 2 * HEAD, whole] = turn_pair(
                r["grad_k"][...] * scale, r["cos"][:, whole], -r["sin"][:, whole]
            ).astype(BF16)
            r["joint"][2 * HEAD : 3 * HEAD, whole] = r["grad_v"][...].astype(BF16)


class Reduce:
    def __init__(self, sizes, pairs, rows, width, parts, bufs, sems):
        self.C, self.F = sizes
        self.pairs, self.rows, self.width, self.parts = pairs, rows, width // parts, parts
        self.c = lax.axis_index("ctx")
        self.f = lax.axis_index("fsdp")
        self.x_nbr, self.y_nbr, self.core = flip(self.c, 2), flip(self.c, 4), flip(self.c, 1)
        (
            self.core_send, self.core_recv, self.x_send, self.y_send, self.x_recv, self.y_recv,
            self.keep_l, self.keep_r, self.y2_send, self.x2_send, self.y2_recv, self.x2_recv,
            self.z_send, self.z_recv, self.turned,
        ) = bufs
        self.send_sems, self.core_sems, self.xy_sems, self.xy2_sems, self.z_sems = sems
        self.open = {}
        self.others = [lax.rem(self.f + s, self.F) for s in range(1, self.F)]
        self.steps = len(pairs) * self.F * parts

    def at_ctx(self, other):
        return {"ctx": other, "fsdp": self.f}

    def at_f(self, other):
        return {"ctx": self.c, "fsdp": other}

    def greet(self):
        barrier = pltpu.get_barrier_semaphore()
        peers = [self.at_ctx(o) for o in (self.x_nbr, self.y_nbr, self.core)]
        peers += [self.at_f(o) for o in self.others]
        for peer in peers:
            pl.semaphore_signal(
                barrier, inc=1, device_id=peer, device_id_type=pl.DeviceIdType.MESH
            )
        pl.semaphore_wait(barrier, len(peers))

    def send(self, key, t, src, dst, recv_sem, target):
        copy = pltpu.make_async_remote_copy(
            src_ref=src, dst_ref=dst, send_sem=self.send_sems.at[key, t], recv_sem=recv_sem,
            device_id=target, device_id_type=pl.DeviceIdType.MESH,
        )
        copy.start()
        self.open[key, t] = copy

    def sent(self, key, t):
        if (key, t) in self.open:
            self.open.pop((key, t)).wait_send()

    def place(self, t):
        return t // (self.F * self.parts), t // self.parts % self.F, t % self.parts

    def dest(self, i):
        return lax.rem(self.f + 1 + i, self.F)

    def turn(self, t):
        pair, i, _ = self.place(t)
        left_ref = self.pairs[pair][0]
        size = left_ref.shape[0]
        rows = self.rows
        block = self.dest(i) * self.C
        for slot, base in enumerate((self.core, self.c)):
            parts = [
                left_ref[:, pl.ds(pl.multiple_of((block + cc) * rows, rows), rows)]
                for cc in (base, flip(base, 2), flip(base, 4), flip(flip(base, 2), 4))
            ]
            self.turned[slot, :, :size] = jnp.concatenate(parts, axis=1).T

    def enter(self, t, tile=512):
        pair, i, part = self.place(t)
        w_ref = self.pairs[pair][1]
        size = w_ref.shape[0]
        rows, mid = self.rows, self.width // 2
        if part == 0:
            self.turn(t)
        self.sent(0, t - 2)
        left = self.turned[0, :, :size]
        for n in range(self.width // tile):
            cols = slice(part * self.width + n * tile, part * self.width + (n + 1) * tile)
            self.core_send[t % 2, :, n * tile : (n + 1) * tile] = jnp.dot(
                left, w_ref[:, cols], preferred_element_type=F32
            ).astype(BF16)
        self.send(
            0, t, self.core_send.at[t % 2], self.core_recv.at[t % 2], self.core_sems.at[t],
            self.at_ctx(self.core),
        )
        left = self.turned[1, :, :size]
        sums = []
        for side in range(2):
            cols = slice(part * self.width + side * mid, part * self.width + (side + 1) * mid)
            sums.append(jnp.dot(left, w_ref[:, cols], preferred_element_type=F32))
        arrived(self.core_recv.at[t % 2], self.core_sems.at[t])
        for key, keep, out, recv, kept, sent_rows, target in (
            (1, self.keep_l, self.x_send, self.x_recv, (0, 2), (1, 3), self.x_nbr),
            (2, self.keep_r, self.y_send, self.y_recv, (0, 1), (2, 3), self.y_nbr),
        ):
            self.sent(key, t - 2)
            total = sums[key - 1] + self.core_recv[t % 2, :, (key - 1) * mid : key * mid].astype(F32)
            for i, b in enumerate(sent_rows):
                out[t % 2, i * rows : (i + 1) * rows] = total[b * rows : (b + 1) * rows].astype(BF16)
            self.send(
                key, t, out.at[t % 2], recv.at[t % 3], self.xy_sems.at[key - 1, t], self.at_ctx(target)
            )
            for i, b in enumerate(kept):
                keep[t % 3, i * rows : (i + 1) * rows] = total[b * rows : (b + 1) * rows]

    def second(self, t):
        rows, slot = self.rows, t % 3
        sides = (
            (3, self.keep_l, self.x_recv, self.y2_send, self.y2_recv, self.y_nbr),
            (4, self.keep_r, self.y_recv, self.x2_send, self.x2_recv, self.x_nbr),
        )
        for key, keep, recv, out, _, _ in sides:
            arrived(recv.at[slot], self.xy_sems.at[key - 3, t])
            self.sent(key, t - 2)
            out[t % 2] = (keep[slot, rows:] + recv[slot, rows:].astype(F32)).astype(BF16)
            keep[slot, :rows] = keep[slot, :rows] + recv[slot, :rows].astype(F32)
        for key, _, _, out, out_recv, target in sides:
            self.send(
                key, t, out.at[t % 2], out_recv.at[slot], self.xy2_sems.at[key - 3, t],
                self.at_ctx(target),
            )

    def third(self, t):
        pair, i, part = self.place(t)
        rows, mid, slot = self.rows, self.width // 2, t % 3
        arrived(self.y2_recv.at[slot], self.xy2_sems.at[0, t])
        arrived(self.x2_recv.at[slot], self.xy2_sems.at[1, t])
        total_l = self.keep_l[slot, :rows] + self.y2_recv[slot].astype(F32)
        total_r = self.keep_r[slot, :rows] + self.x2_recv[slot].astype(F32)
        if i < self.F - 1:
            for key, u in list(self.open):
                if key == 5 and u % 2 == t % 2:
                    self.sent(key, u)
            self.z_send[t % 2, :, :mid] = total_l.astype(BF16)
            self.z_send[t % 2, :, mid:] = total_r.astype(BF16)
            self.send(
                5, t, self.z_send.at[t % 2], self.z_recv.at[pair, part, self.f],
                self.z_sems.at[pair, part, self.f], self.at_f(self.dest(i)),
            )
            return None
        total = jnp.concatenate([total_l, total_r], axis=1)
        for o in self.others:
            arrived(self.z_recv.at[pair, part, o], self.z_sems.at[pair, part, o])
            total = total + self.z_recv[pair, part, o].astype(F32)
        return total

    def run(self, fill):
        sums = []
        self.enter(0)
        self.enter(1)
        for t in range(self.steps):
            fill(t)
            self.second(t)
            if t >= 1:
                sums.append(self.third(t - 1))
            if t + 2 < self.steps:
                self.enter(t + 2)
        fill(self.steps)
        sums.append(self.third(self.steps - 1))
        return sums

    def finish(self):
        for key, t in list(self.open):
            self.sent(key, t)


def reduce_scratch(F, rows, width, parts, pairs, features):
    width = width // parts
    mid = width // 2
    steps = pairs * F * parts
    return [
        pltpu.VMEM((2, 4 * rows, width), BF16),
        pltpu.VMEM((2, 4 * rows, width), BF16),
        pltpu.VMEM((2, 2 * rows, mid), BF16),
        pltpu.VMEM((2, 2 * rows, mid), BF16),
        pltpu.VMEM((3, 2 * rows, mid), BF16),
        pltpu.VMEM((3, 2 * rows, mid), BF16),
        pltpu.VMEM((3, 2 * rows, mid), F32),
        pltpu.VMEM((3, 2 * rows, mid), F32),
        pltpu.VMEM((2, rows, mid), BF16),
        pltpu.VMEM((2, rows, mid), BF16),
        pltpu.VMEM((3, rows, mid), BF16),
        pltpu.VMEM((3, rows, mid), BF16),
        pltpu.VMEM((2, rows, width), BF16),
        pltpu.VMEM((pairs, parts, F, rows, width), BF16),
        pltpu.VMEM((2, 4 * rows, features), BF16),
        pltpu.SemaphoreType.DMA((6, steps)),
        pltpu.SemaphoreType.DMA((steps,)),
        pltpu.SemaphoreType.DMA((2, steps)),
        pltpu.SemaphoreType.DMA((2, steps)),
        pltpu.SemaphoreType.DMA((pairs, parts, F)),
    ]


PIECES = ((0, 4), (4, 1), (5, 1), (6, 9))


class Spread:
    def __init__(self, sizes, shard_units, win_ref, wout_ref, win_all, wout_all, copies, block_sems, piece_sems):
        self.C, self.F = sizes
        self.shard_units = shard_units
        self.win_ref, self.wout_ref, self.win_all, self.wout_all = win_ref, wout_ref, win_all, wout_all
        self.copies, self.block_sems, self.piece_sems = copies, block_sems, piece_sems
        self.c = lax.axis_index("ctx")
        self.f = lax.axis_index("fsdp")
        self.x_nbr, self.y_nbr, self.core = flip(self.c, 2), flip(self.c, 4), flip(self.c, 1)
        self.diag = flip(self.x_nbr, 4)
        self.share = win_all.shape[3]
        self.half = win_all.shape[2] // 2
        self.near = (self.x_nbr, self.y_nbr, self.core)

    def at_ctx(self, other):
        return {"ctx": other, "fsdp": self.f}

    def at_f(self, other):
        return {"ctx": self.c, "fsdp": other}

    def win_slice(self, dest):
        return self.win_ref.at[:, pl.ds(pl.multiple_of(dest * self.share, self.share), self.share)]

    def block(self, fb, cb, part):
        ref = self.win_all.at[fb, cb]
        return ref if part is None else ref.at[pl.ds(part * self.half, self.half)]

    def pass_block(self, fb, cb, part, target, src=None):
        ref = self.block(fb, cb, part)
        sem = self.block_sems.at[fb, cb, part or 0]
        self.copies.send(ref if src is None else src, ref, sem, target)

    def wait_block(self, fb, cb, part):
        arrived(self.block(fb, cb, part), self.block_sems.at[fb, cb, part or 0])

    def piece(self, fb, cb, p):
        att_units, ff_units = PIECES[0][1], sum(n for _, n in PIECES[1:])
        rank = fb * self.C + cb
        start, units = PIECES[p]
        if p == 0:
            unit = rank * att_units
        else:
            unit = self.C * self.F * att_units + rank * ff_units + (start - att_units)
        place = pl.multiple_of(lax.rem(unit, self.shard_units) * UNIT, UNIT)
        return unit // self.shard_units, self.wout_all.at[pl.ds(place, units * UNIT)]

    def own_piece(self, p):
        start, units = PIECES[p]
        return self.wout_ref.at[pl.ds(start * UNIT, units * UNIT)]

    def pass_piece(self, fb, cb, p, target, when, src=None):
        ref = self.piece(fb, cb, p)[1]
        self.copies.send(ref if src is None else src, ref, self.piece_sems.at[fb, cb, p], target, when)

    def wait_piece(self, fb, cb, p, when):
        def go():
            arrived(self.piece(fb, cb, p)[1], self.piece_sems.at[fb, cb, p])
        pl.when(when)(go)

    def z_send(self, shift):
        f, c = self.f, self.c
        o = lax.rem(f + shift, self.F)
        self.copies.send(
            self.win_slice(o), self.block(f, c, None), self.block_sems.at[f, c, 0], self.at_f(o)
        )
        for p in range(len(PIECES)):
            self.pass_piece(f, c, p, self.at_f(o), self.piece(f, c, p)[0] == o, src=self.own_piece(p))

    def own(self):
        f, c = self.f, self.c
        mine = self.win_slice(f)
        for target in self.near:
            self.pass_block(f, c, None, self.at_ctx(target), src=mine)
        self.copies.local(mine, self.block(f, c, None))
        for p in range(len(PIECES)):
            shard, place = self.piece(f, c, p)
            for target in self.near:
                self.pass_piece(f, c, p, self.at_ctx(target), shard == f, src=self.own_piece(p))
            self.copies.local(self.own_piece(p), place, shard == f)

    def z_step(self, fb):
        f, c = self.f, self.c
        self.wait_block(fb, c, None)
        for target in self.near:
            self.pass_block(fb, c, None, self.at_ctx(target))
        for p in range(len(PIECES)):
            here = self.piece(fb, c, p)[0] == f
            self.wait_piece(fb, c, p, here)
            for target in self.near:
                self.pass_piece(fb, c, p, self.at_ctx(target), here)

    def xy_step(self, fb, way):
        x_nbr, y_nbr, core = self.near
        self.wait_block(fb, x_nbr, None)
        self.pass_block(fb, x_nbr, 0, self.at_ctx(y_nbr))
        self.pass_block(fb, x_nbr, None, self.at_ctx(core))
        self.wait_block(fb, y_nbr, None)
        self.pass_block(fb, y_nbr, 1, self.at_ctx(x_nbr))
        self.pass_block(fb, y_nbr, None, self.at_ctx(core))
        for p in range(len(PIECES)):
            by_x = (p < 2) == (way == 0)
            for source, onward, turn in ((x_nbr, y_nbr, by_x), (y_nbr, x_nbr, not by_x)):
                here = self.piece(fb, source, p)[0] == self.f
                self.wait_piece(fb, source, p, here)
                if turn:
                    self.pass_piece(fb, source, p, self.at_ctx(onward), here)
                self.pass_piece(fb, source, p, self.at_ctx(core), here)

    def diag_step(self, fb):
        diag, core = self.diag, self.core
        for part in (0, 1):
            self.wait_block(fb, diag, part)
            self.pass_block(fb, diag, part, self.at_ctx(core))
        for p in range(len(PIECES)):
            here = self.piece(fb, diag, p)[0] == self.f
            self.wait_piece(fb, diag, p, here)
            self.pass_piece(fb, diag, p, self.at_ctx(core), here)

    def rest(self, terms, sums):
        F, f = self.F, self.f
        order = [f] + [lax.rem(f + F - s, F) for s in range(1, F)]
        terms.step(0)
        for s in range(F + 2):
            if s + 1 < F:
                self.z_step(order[s + 1])
                if s + 3 < F:
                    self.z_send(s + 3)
            if s < 3:
                terms.step(s + 1)
            if s < F:
                self.xy_step(order[s], s % 2)
            if 0 <= s - 1 < F:
                self.diag_step(order[s - 1])
        core = self.core
        beyond = (core, flip(core, 2), flip(core, 4))
        corner = flip(flip(core, 2), 4)
        for fb in range(F):
            for cb in beyond:
                self.wait_block(fb, cb, None)
            for part in (0, 1):
                self.wait_block(fb, corner, part)
            for cb in beyond + (corner,):
                for p in range(len(PIECES)):
                    self.wait_piece(fb, cb, p, self.piece(fb, cb, p)[0] == f)
        sums[...] = terms.finish()
        self.copies.finish()


class Terms:
    def __init__(self, spread, value, bufs, sems):
        self.spread, self.value, self.bufs, self.sems = spread, value, bufs, sems
        self.others = [lax.rem(spread.f + s, spread.F) for s in range(1, spread.F)]

    def step(self, i):
        spread = self.spread
        near, parts, shares = self.bufs
        x_nbr, y_nbr, core = spread.near
        if i > 0:
            arrived(near.at[i - 1], self.sems.at[i - 1])
            self.value = self.value + near[i - 1]
        if i < 3:
            parts[i] = self.value
            target = spread.at_ctx((core, x_nbr, y_nbr)[i])
            spread.copies.send(parts.at[i], near.at[i], self.sems.at[i], target)
            return
        share = spread.share
        for s in range(spread.F):
            parts[3 + s, :, :share] = self.value[:, s * share : (s + 1) * share]
        for o in self.others:
            spread.copies.send(
                parts.at[3 + o, :, pl.ds(0, share)], shares.at[spread.f], self.sems.at[3 + spread.f],
                spread.at_f(o),
            )

    def finish(self):
        _, parts, shares = self.bufs
        f, share = self.spread.f, self.spread.share
        shares[f] = parts[3 + f, :, :share]
        for o in self.others:
            arrived(shares.at[o], self.sems.at[3 + o])
        total = shares[0]
        for s in range(1, self.spread.F):
            total = total + shares[s]
        return total


SLAB = 256
PARTS = 2


def backward_kernel(
    sizes, ff, shard_units,
    mixed_ref, w_out_ref, w_in_ref, x_ref, go_ref, gain_ref, qkv, attended, totals, place, turn, cosine,
    sine, hid_all, go_all, gates,
    result_ref, grad_in_ref, sums_ref, win_all, wout_all,
    go_buf, slab_buf, gate_buf, numer, ratio, key_rows, value_rows, place_col, grad_k, grad_v, joint, dw_in, dw_out,
    near_terms, part_terms, share_terms,
    go_sems, slab_sems, gate_sems, send_sems, block_sems, piece_sems, term_sems, *shared,
):
    C, F = sizes
    rows, width = x_ref.shape
    batch = C * rows
    reduce = Reduce(
        sizes, ((mixed_ref, w_out_ref), (joint, w_in_ref)), rows, width, PARTS, shared[:15], shared[15:]
    )
    count = F * batch // CHUNK
    slabs = width // SLAB
    wide = Stream(
        count,
        lambda i: go_all.at[i * CHUNK // batch, pl.ds(i * CHUNK % batch // rows, CHUNK // rows)],
        go_buf, go_sems,
    )
    refs = dict(
        grads=wide,
        gates=Stream(count, lambda i: gates.at[:, pl.ds(i * CHUNK, CHUNK)], gate_buf, gate_sems),
        w_out=w_out_ref, totals=totals, attended=attended, ratio=ratio, numer=numer, joint=joint,
        qkv=qkv, key_rows=key_rows, value_rows=value_rows, place_col=place_col, place=place,
        turn=turn, grad_k=grad_k, grad_v=grad_v, cos=cosine, sin=sine,
    )
    refs["grads"].start()
    refs["gates"].start()
    work = Backward(refs, batch, ff)
    pieces = []
    for b in range(F):
        for i in range(batch // CHUNK):
            pieces.append(functools.partial(work.mixed, b * (batch // CHUNK) + i))
        for t in range(batch // QT):
            pieces.append(functools.partial(work.attend, b, t))

    def slab_source(i):
        source = hid_all if i < slabs else go_all
        return source.at[:, :, :, pl.ds(i % slabs * SLAB, SLAB)]

    slab_stream = Stream(2 * slabs, slab_source, slab_buf, slab_sems)

    def weight_grad(i):
        if i == 0:
            slab_stream.start()
        slab = slab_stream.take(i).reshape(C * F * rows, SLAB)
        left, out = (joint, dw_in) if i < slabs else (mixed_ref, dw_out)
        out[:, i % slabs * SLAB : (i % slabs + 1) * SLAB] = jnp.dot(
            left[...], slab, preferred_element_type=F32
        ).astype(BF16)

    spread = Spread(
        sizes, shard_units, dw_in, dw_out, win_all, wout_all, Copies(send_sems), block_sems, piece_sems
    )
    grads = [functools.partial(weight_grad, i) for i in range(2 * slabs)]
    half = reduce.steps // 2
    before = half - 1

    def fill(t):
        if t < before:
            todo = pieces[t * len(pieces) // before : (t + 1) * len(pieces) // before]
        else:
            gaps = half - 1
            k = t - before
            todo = grads[k * len(grads) // gaps : (k + 1) * len(grads) // gaps] if k < gaps else []
        for piece in todo:
            piece()
        if t == reduce.steps - 2:
            spread.z_send(1)

    reduce.greet()
    sums = [part for part in reduce.run(fill) if part is not None]
    spread.own()
    spread.z_send(2)
    total = jnp.concatenate(sums[:PARTS], axis=1)
    values = x_ref[...].astype(F32)
    result_ref[...] = (values + total).astype(BF16)
    total = jnp.concatenate(sums[PARTS:], axis=1)
    centred = values - jnp.mean(values, axis=1, keepdims=True)
    inverse_std = lax.rsqrt(jnp.mean(centred * centred, axis=1, keepdims=True) + 1e-05)
    normed = centred * inverse_std
    gain = jnp.concatenate([gain_ref[s].astype(F32) for s in range(F)], axis=1)
    g = total * gain
    back = inverse_std * (
        g - jnp.mean(g, axis=1, keepdims=True) - normed * jnp.mean(g * normed, axis=1, keepdims=True)
    )
    grad_in_ref[...] = (go_ref[...].astype(F32) + back).astype(BF16)
    terms = jnp.concatenate(
        [jnp.sum(total * normed, axis=0, keepdims=True), jnp.sum(total, axis=0, keepdims=True)], axis=0
    )
    reduce.finish()
    spread.rest(Terms(spread, terms, (near_terms, part_terms, share_terms), term_sems), sums_ref)


def backward_all(
    mixed, w_out, w_in, x, go, gains, qkv, attended, totals, place, turn, cosine, sine, hid_all, go_all, gates,
    shard_rows, C, F,
):
    rows, width = x.shape
    ff = gates.shape[0] // 2
    batch, tokens = C * rows, C * F * rows
    per_rank, share = w_in.shape[0], width // F
    vmem = pl.BlockSpec(memory_space=pltpu.VMEM)
    any_ = pl.BlockSpec(memory_space=pl.ANY)
    shape = jax.ShapeDtypeStruct
    dma = pltpu.SemaphoreType.DMA
    return pl.pallas_call(
        functools.partial(backward_kernel, (C, F), ff, shard_rows // UNIT),
        out_shape=(
            shape((rows, width), BF16),
            shape((rows, width), BF16),
            shape((2, share), F32),
            shape((F, C, per_rank, share), BF16),
            shape((shard_rows, width), BF16),
        ),
        in_specs=[vmem] * 13 + [any_] * 3,
        out_specs=(vmem,) * 3 + (any_,) * 2,
        scratch_shapes=[
            pltpu.VMEM((2, CHUNK // rows, rows, width), BF16),
            pltpu.VMEM((2, F, C, rows, SLAB), BF16),
            pltpu.VMEM((2, 2 * ff, CHUNK), F32),
            pltpu.VMEM((HEAD, tokens), BF16),
            pltpu.VMEM((1, tokens), F32),
            pltpu.VMEM((batch, HEAD), BF16),
            pltpu.VMEM((batch, HEAD), BF16),
            pltpu.VMEM((batch, 1), jnp.int32),
            pltpu.VMEM((HEAD, batch), F32),
            pltpu.VMEM((HEAD, batch), F32),
            pltpu.VMEM((per_rank, tokens), BF16),
            pltpu.VMEM((per_rank, width), BF16),
            pltpu.VMEM(w_out.shape, BF16),
            pltpu.VMEM((3, 2, width), F32),
            pltpu.VMEM((3 + F, 2, width), F32),
            pltpu.VMEM((F, 2, share), F32),
            dma((2,)),
            dma((2,)),
            dma((2,)),
            dma((288,)),
            dma((F, C, 2)),
            dma((F, C, len(PIECES))),
            dma((3 + F,)),
        ] + reduce_scratch(F, rows, width, PARTS, 2, per_rank),
        compiler_params=pltpu.CompilerParams(
            collective_id=2, has_side_effects=True, vmem_limit_bytes=60 * 1024 * 1024
        ),
    )(mixed, w_out, w_in, x, go, gains, qkv, attended, totals, place, turn, cosine, sine, hid_all, go_all, gates)


def turn_kernel(ff, src, out, in_buf, out_buf, in_sems, out_sems):
    F, C = src.shape[0], src.shape[1]
    share = src.shape[3]
    steps = []
    base = 0
    for row, size in ((0, HEAD), (HEAD, HEAD), (2 * HEAD, HEAD), (3 * HEAD, ff), (3 * HEAD + ff, ff)):
        for fb in range(F):
            steps.append((fb, row, size, base + fb * C * size))
        base += F * C * size

    def fetch(i):
        fb, row, size, _ = steps[i]
        return pltpu.make_async_copy(
            src.at[fb, :, pl.ds(row, size)], in_buf.at[i % 2, :, pl.ds(0, size)], in_sems.at[i % 2]
        )

    def store(i):
        _, _, size, col = steps[i]
        return pltpu.make_async_copy(
            out_buf.at[i % 2, :, pl.ds(0, C * size)], out.at[:, pl.ds(col, C * size)], out_sems.at[i % 2]
        )

    fetch(0).start()
    for i, (fb, row, size, col) in enumerate(steps):
        if i + 1 < len(steps):
            fetch(i + 1).start()
        fetch(i).wait()
        if i >= 2:
            store(i - 2).wait()
        block = in_buf[i % 2, :, :size, :].reshape(C * size, share).astype(F32)
        out_buf[i % 2, :, : C * size] = block.T
        store(i).start()
    store(len(steps) - 2).wait()
    store(len(steps) - 1).wait()


def turn_blocks(blocks, ff):
    F, C, per_rank, share = blocks.shape
    any_ = pl.BlockSpec(memory_space=pl.ANY)
    return pl.pallas_call(
        functools.partial(turn_kernel, ff),
        out_shape=jax.ShapeDtypeStruct((share, F * C * per_rank), F32),
        in_specs=[any_],
        out_specs=any_,
        scratch_shapes=[
            pltpu.VMEM((2, C, ff, share), BF16),
            pltpu.VMEM((2, share, C * ff), F32),
            pltpu.SemaphoreType.DMA((2,)),
            pltpu.SemaphoreType.DMA((2,)),
        ],
        compiler_params=pltpu.CompilerParams(vmem_limit_bytes=40 * 1024 * 1024),
    )(blocks)


def tp_body(C, F, inputs, gain, bias, in_weight, out_weight, grad_out, lengths, order):
    rows, width = inputs.shape[1:]
    T = C * F
    ff = FF // T
    x = inputs[0]
    go = grad_out[0]

    count = lengths.shape[1] + order.shape[1]
    table = jnp.pad(jnp.concatenate([lengths, order], axis=1), ((0, 0), (0, 128 - count)))

    (
        go_all, hid_all, w_in, w_out, gains, qkv, gates, mixed, attended, totals, place, turn, cosine, sine
    ) = forward_all(x, go, gain[None], bias[None], table, in_weight, out_weight, C, F)
    result, grad_in, sums, blocks, out_rows = backward_all(
        mixed, w_out, w_in, x, go, gains, qkv, attended, totals, place, turn, cosine, sine, hid_all, go_all,
        gates, out_weight.shape[0], C, F,
    )
    return (
        result[None], grad_in[None], turn_blocks(blocks, ff), out_rows.astype(F32), sums[0], sums[1]
    )


def solution(mesh):
    in_specs = (
        P("fsdp", "ctx", None),
        P("fsdp"),
        P("fsdp"),
        P("fsdp", None),
        P("fsdp", None),
        P("fsdp", "ctx", None),
        P("fsdp", None),
        P("fsdp", None),
    )
    out_specs = (
        P("fsdp", "ctx", None),
        P("fsdp", "ctx", None),
        P("fsdp", None),
        P("fsdp", None),
        P("fsdp"),
        P("fsdp"),
    )
    C, F = mesh.shape["ctx"], mesh.shape["fsdp"]
    if (C, F) == (8, 4):
        work = functools.partial(tp_body, C, F)
    else:
        work = body
    return jax.shard_map(work, mesh=mesh, in_specs=in_specs, out_specs=out_specs, check_vma=False)
```

```python
import functools
import math

import jax
import jax.numpy as jnp
from jax import lax
from jax.experimental import pallas as pl
from jax.experimental.pallas import tpu as pltpu
from jax.sharding import PartitionSpec as P

HEADS = 32
HEAD = 64
ROT = 16
FF = 5632
BLOCK = 64
BF16 = jnp.bfloat16
F32 = jnp.float32
UNIT = 16


def places_of(index, length_row, order_row):
    count = order_row.shape[0]
    hit = (index // BLOCK)[:, None] == jnp.arange(count, dtype=jnp.int32)[None, :]
    block_id = jnp.sum(jnp.where(hit, order_row[None, :], 0), axis=1)
    place = block_id * BLOCK + index % BLOCK
    ends = jnp.cumsum(length_row)
    starts = ends - length_row
    inside = (place[:, None] >= starts[None, :]) & (place[:, None] < ends[None, :])
    docs = jnp.sum(
        jnp.where(inside, jnp.arange(length_row.shape[0], dtype=jnp.int32)[None, :], 0), axis=1
    )
    first = jnp.sum(jnp.where(inside, starts[None, :], 0), axis=1)
    return (place, docs, place - first)


def rotate(values, positions, sign):
    half = ROT // 2
    freq = 10000.0 ** (-2.0 * jnp.arange(half, dtype=jnp.float32) / ROT)
    angle = positions.astype(jnp.float32)[:, None] * freq[None, :]
    cosine = jnp.cos(angle)[:, None, :]
    sine = sign * jnp.sin(angle)[:, None, :]
    first = values[..., :half]
    second = values[..., half:ROT]
    return jnp.concatenate(
        [first * cosine - second * sine, second * cosine + first * sine, values[..., ROT:]], axis=-1
    )


def rounded(values):
    return lax.optimization_barrier(values.astype(jnp.bfloat16)).astype(jnp.float32)


def transposed_dot(left, right):
    return lax.dot_general(
        left, right, (((0,), (0,)), ((), ())), preferred_element_type=jnp.float32
    )


def against_rows(left, right):
    return lax.dot_general(
        left, right, (((1,), (1,)), ((), ())), preferred_element_type=jnp.float32
    )


def body(inputs, gain, bias, in_weight, out_weight, grad_out, lengths, order):
    rows = inputs.shape[1]
    width = inputs.shape[2]
    length_row = lengths[0]
    order_row = order[0]
    local_index = lax.axis_index("ctx") * rows + jnp.arange(rows, dtype=jnp.int32)
    query_place, query_doc, query_turn = places_of(local_index, length_row, order_row)
    scale = HEAD ** (-0.5)
    head_shape = (rows, HEADS, HEAD)
    values_in = inputs[0].astype(jnp.float32)
    centred = values_in - jnp.mean(values_in, axis=1, keepdims=True)
    inverse_std = lax.rsqrt(jnp.mean(centred * centred, axis=1, keepdims=True) + 1e-05)
    normed = centred * inverse_std
    weight_piece = lax.all_gather(in_weight, "fsdp", axis=0, tiled=True)
    gain_piece = lax.all_gather(gain, "fsdp", axis=0, tiled=True)
    bias_piece = lax.all_gather(bias, "fsdp", axis=0, tiled=True)
    count = weight_piece.shape[0]
    columns = normed
    hidden_piece = (
        columns * gain_piece.astype(jnp.float32) + bias_piece.astype(jnp.float32)
    ).astype(jnp.bfloat16)
    joint_sum = jnp.dot(hidden_piece, weight_piece, preferred_element_type=jnp.float32)
    gain_full = gain_piece.astype(jnp.float32)
    joint, hidden_in, gain_full = (joint_sum, hidden_piece, gain_full)
    queries = rotate(joint[:, :width].reshape(head_shape), query_turn, 1.0).astype(jnp.bfloat16)
    keys = (
        rotate(joint[:, width : 2 * width].reshape(head_shape), query_turn, 1.0)
        .astype(jnp.bfloat16)
        .reshape(rows, width)
    )
    values = joint[:, 2 * width : 3 * width].astype(jnp.bfloat16)
    gate = joint[:, 3 * width : 3 * width + FF]
    upward = joint[:, 3 * width + FF :]

    def exp_scores(key_block, start, count):
        key_place, key_doc, unused_turn = places_of(
            start + jnp.arange(count, dtype=jnp.int32), length_row, order_row
        )
        scores = (
            jnp.einsum(
                "qhd,khd->hqk",
                queries,
                key_block.reshape(count, HEADS, HEAD),
                preferred_element_type=jnp.float32,
            )
            * scale
        )
        allowed = (query_doc[:, None] == key_doc[None, :]) & (
            key_place[None, :] <= query_place[:, None]
        )
        return jnp.where(allowed[None], jnp.exp(scores), 0.0)

    empty_attention = (jnp.zeros(head_shape, jnp.float32), jnp.zeros((HEADS, rows), jnp.float32))
    key_piece = lax.all_gather(keys, "ctx", axis=0, tiled=True)
    value_piece = lax.all_gather(values, "ctx", axis=0, tiled=True)
    count = key_piece.shape[0]
    block_rows = math.gcd(count, 512)

    def add_block(j, state):
        numer, totals = state
        offset = j * block_rows
        key_block = lax.dynamic_slice_in_dim(key_piece, offset, block_rows, 0)
        value_block = lax.dynamic_slice_in_dim(value_piece, offset, block_rows, 0)
        weights = exp_scores(key_block, offset, block_rows)
        totals = totals + jnp.sum(weights, axis=2)
        numer = numer + jnp.einsum(
            "hqk,khd->qhd",
            weights.astype(jnp.bfloat16),
            value_block.reshape(block_rows, HEADS, HEAD),
            preferred_element_type=jnp.float32,
        )
        return (numer, totals)

    numer, totals = lax.fori_loop(0, count // block_rows, add_block, empty_attention)
    attended = numer / jnp.transpose(totals)[:, :, None]
    sigmoid_gate = jax.nn.sigmoid(gate)
    activated = gate * sigmoid_gate * upward
    mixed_in = jnp.concatenate(
        [attended.reshape(rows, width).astype(jnp.bfloat16), activated.astype(jnp.bfloat16)], axis=1
    )
    columns = mixed_in
    mixed = jnp.dot(
        columns,
        lax.all_gather(out_weight, "fsdp", axis=0, tiled=True),
        preferred_element_type=jnp.float32,
    )
    result = (values_in + mixed).astype(jnp.bfloat16)
    grad_rows = grad_out[0]
    grad_mixed = against_rows(grad_rows, lax.all_gather(out_weight, "fsdp", axis=0, tiled=True))
    grad_att = grad_mixed[:, :width].astype(jnp.bfloat16).reshape(head_shape)
    grad_act = rounded(grad_mixed[:, width:])
    grad_gate = grad_act * upward * sigmoid_gate * (1.0 + gate * (1.0 - sigmoid_gate))
    grad_up = grad_act * gate * sigmoid_gate
    delta = jnp.transpose(jnp.sum(grad_att.astype(jnp.float32) * attended, axis=2))
    grad_numer = (grad_att.astype(jnp.float32) / jnp.transpose(totals)[:, :, None]).astype(
        jnp.bfloat16
    )
    ratio = delta / totals
    keys_all, values_all = (
        lax.all_gather(keys, "ctx", axis=0, tiled=True),
        lax.all_gather(values, "ctx", axis=0, tiled=True),
    )
    group = keys_all.shape[0]

    def score_grads(key_block, value_block, start, count):
        weights = exp_scores(key_block, start, count)
        pushed = jnp.einsum(
            "qhd,khd->hqk",
            grad_numer,
            value_block.reshape(count, HEADS, HEAD),
            preferred_element_type=jnp.float32,
        )
        return (weights, (weights * (pushed - ratio[:, :, None])).astype(jnp.bfloat16))

    query_rows = math.gcd(group, 512)

    def query_block_grad(j, total):
        offset = j * query_rows
        key_block = lax.dynamic_slice_in_dim(keys_all, offset, query_rows, 0)
        value_block = lax.dynamic_slice_in_dim(values_all, offset, query_rows, 0)
        unused_weights, grad_scores = score_grads(key_block, value_block, offset, query_rows)
        return total + jnp.einsum(
            "hqk,khd->qhd",
            grad_scores,
            key_block.reshape(query_rows, HEADS, HEAD),
            preferred_element_type=jnp.float32,
        )

    grad_query = (
        lax.fori_loop(0, group // query_rows, query_block_grad, jnp.zeros(head_shape, jnp.float32))
        * scale
    )
    key_block_rows = math.gcd(rows * lax.axis_size("ctx"), 512)

    def key_block_grad(j, terms):
        offset = j * key_block_rows
        key_block = lax.dynamic_slice_in_dim(keys_all, offset, key_block_rows, 0)
        value_block = lax.dynamic_slice_in_dim(values_all, offset, key_block_rows, 0)
        weights, grad_scores = score_grads(key_block, value_block, offset, key_block_rows)
        key_part = (
            jnp.einsum("hqk,qhd->khd", grad_scores, queries, preferred_element_type=jnp.float32)
            * scale
        )
        value_part = jnp.einsum(
            "hqk,qhd->khd",
            weights.astype(jnp.bfloat16),
            grad_numer,
            preferred_element_type=jnp.float32,
        )
        block_terms = jnp.concatenate(
            [key_part.reshape(key_block_rows, width), value_part.reshape(key_block_rows, width)],
            axis=1,
        )
        return lax.dynamic_update_slice_in_dim(terms, block_terms, j * key_block_rows, 0)

    key_value_grad = lax.psum_scatter(
        lax.fori_loop(
            0,
            rows * lax.axis_size("ctx") // key_block_rows,
            key_block_grad,
            jnp.zeros((rows * lax.axis_size("ctx"), 2 * width), jnp.float32),
        ).astype(jnp.bfloat16),
        "ctx",
        scatter_dimension=0,
        tiled=True,
    ).astype(jnp.float32)
    grad_key = rotate(key_value_grad[:, :width].reshape(head_shape), query_turn, -1.0).reshape(
        rows, width
    )
    grad_query = rotate(grad_query, query_turn, -1.0).reshape(rows, width)
    grad_joint = jnp.concatenate(
        [
            grad_query.astype(jnp.bfloat16),
            grad_key.astype(jnp.bfloat16),
            key_value_grad[:, width:].astype(jnp.bfloat16),
            grad_gate.astype(jnp.bfloat16),
            grad_up.astype(jnp.bfloat16),
        ],
        axis=1,
    )
    grad_hidden = against_rows(grad_joint, lax.all_gather(in_weight, "fsdp", axis=0, tiled=True))
    grad_normed = grad_hidden * gain_full[None, :]
    grad_inputs = inverse_std * (
        grad_normed
        - jnp.mean(grad_normed, axis=1, keepdims=True)
        - normed * jnp.mean(grad_normed * normed, axis=1, keepdims=True)
    )
    grad_in = (grad_rows.astype(jnp.float32) + grad_inputs).astype(jnp.bfloat16)
    norm_terms = jnp.stack([jnp.sum(grad_hidden * normed, axis=0), jnp.sum(grad_hidden, axis=0)])
    norm_totals = lax.psum(norm_terms, ("ctx", "fsdp"))
    shards = lax.axis_size("fsdp")
    share = width // shards
    gain_grad = lax.dynamic_slice_in_dim(norm_totals[0], lax.axis_index("fsdp") * share, share, 0)
    bias_grad = lax.dynamic_slice_in_dim(norm_totals[1], lax.axis_index("fsdp") * share, share, 0)

    def column_terms(source, partner):
        return transposed_dot(source, partner)

    parts = lax.axis_size("ctx")

    def reorder(matrix):
        columns = matrix.shape[1]
        return (
            matrix.reshape(rows, shards, parts, columns // (shards * parts))
            .transpose(0, 2, 1, 3)
            .reshape(rows, columns)
        )

    in_piece = lax.psum_scatter(
        column_terms(reorder(hidden_in), grad_joint),
        ("ctx", "fsdp"),
        scatter_dimension=0,
        tiled=True,
    )
    out_piece = lax.psum_scatter(
        column_terms(reorder(mixed_in), grad_rows), ("ctx", "fsdp"), scatter_dimension=0, tiled=True
    )
    in_weight_grad, out_weight_grad = (
        lax.all_gather(in_piece.astype(jnp.bfloat16), "ctx", axis=0, tiled=True).astype(
            in_piece.dtype
        ),
        lax.all_gather(out_piece.astype(jnp.bfloat16), "ctx", axis=0, tiled=True).astype(
            out_piece.dtype
        ),
    )
    return (result[None], grad_in[None], in_weight_grad, out_weight_grad, gain_grad, bias_grad)


def flip(index, bit):
    return index + bit - 2 * bit * ((index // bit) % 2)


def ff_chunk(C, fb, cb):
    return fb * C + (cb % 2) * (C // 2) + cb // 2


class Copies:
    def __init__(self, sems):
        self.sems = sems
        self.used = 0
        self.open = []

    def send(self, src, dst, recv_sem, target, when=None):
        copy = pltpu.make_async_remote_copy(
            src_ref=src,
            dst_ref=dst,
            send_sem=self.sems.at[self.used],
            recv_sem=recv_sem,
            device_id=target,
            device_id_type=pl.DeviceIdType.MESH,
        )
        self.used += 1
        self.open.append((copy.wait_send, when, False))
        if when is None:
            copy.start()
        else:
            pl.when(when)(copy.start)

    def local(self, src, dst, when=None):
        copy = pltpu.make_async_copy(src, dst, self.sems.at[self.used])
        self.used += 1
        if when is None:
            copy.start()
        else:
            pl.when(when)(copy.start)
        self.open.append((copy.wait, when, True))

    def finish_local(self):
        self.finish([item for item in self.open if item[2]])
        self.open = [item for item in self.open if not item[2]]

    def finish(self, items=None):
        for done, when, _ in self.open if items is None else items:
            if when is None:
                done()
            else:
                pl.when(when)(done)


def arrived(ref, recv_sem):
    pltpu.make_async_copy(ref, ref, recv_sem).wait()


def owner_of_unit(unit, att_units, ff_units, heads):
    first = heads * att_units
    is_att = (unit < first).astype(jnp.int32) if hasattr(unit, "astype") else int(unit < first)
    return is_att * (unit // att_units) + (1 - is_att) * ((unit - first) // ff_units)


LOG2E = 1.4426950408889634
CHUNK = 512
QT = 256


class Stream:
    def __init__(self, count, source, buf, sems):
        self.count, self.source, self.buf, self.sems = count, source, buf, sems

    def copy(self, i):
        return pltpu.make_async_copy(self.source(i), self.buf.at[i % 2], self.sems.at[i % 2])

    def start(self):
        self.copy(0).start()

    def take(self, i):
        if i + 1 < self.count:
            self.copy(i + 1).start()
        self.copy(i).wait()
        return self.buf[i % 2]


def turn_pair(values, cosine, sine):
    half = ROT // 2
    first, second = values[:half], values[half:ROT]
    return jnp.concatenate(
        [first * cosine - second * sine, second * cosine + first * sine, values[ROT:]], axis=0
    )


def nt_dot(left, right):
    return lax.dot_general(left, right, (((1,), (1,)), ((), ())), preferred_element_type=F32)


def token_tables(row, batch, docs):
    index = lax.broadcasted_iota(jnp.int32, (1, batch), 1)
    place = index % BLOCK
    block = index // BLOCK
    for j in range(batch // BLOCK):
        place = place + jnp.where(block == j, row[:, docs + j : docs + j + 1] * BLOCK, 0)
    start = jnp.zeros((1, 1), jnp.int32)
    first = jnp.zeros((1, batch), jnp.int32)
    for j in range(docs):
        first = jnp.where(place >= start, start, first)
        start = start + row[:, j : j + 1]
    return place, place - first


def as_column(row):
    return jnp.broadcast_to(row, (8, row.shape[1])).T[:, :1]


def allowed_keys(place_col, place_row, turn_row):
    return (place_col <= place_row) & (place_col >= place_row - turn_row)


class Forward:
    def __init__(self, refs, batch, ff):
        self.r, self.batch, self.ff = refs, batch, ff

    def tables(self, b):
        r, batch = self.r, self.batch
        place, turn = token_tables(r["table"][b], batch, 4)
        r["place"][b] = place
        r["turn"][b] = turn
        pair = lax.broadcasted_iota(jnp.int32, (ROT // 2, 1), 0).astype(F32)
        freq = jnp.exp2(pair * (-2.0 * math.log2(10000.0) / ROT))
        angle = turn.astype(F32) * freq
        r["cos"][:, b * batch : (b + 1) * batch] = jnp.cos(angle)
        r["sin"][:, b * batch : (b + 1) * batch] = jnp.sin(angle)

    def project(self, i):
        r, ff = self.r, self.ff
        cols = slice(i * CHUNK, (i + 1) * CHUNK)
        hidden = r["hidden"].take(i).reshape(CHUNK, -1)
        joint = nt_dot(r["w_in"][...], hidden)
        cosine, sine = r["cos"][:, cols], r["sin"][:, cols]
        r["qkv"][:HEAD, cols] = turn_pair(joint[:HEAD], cosine, sine).astype(BF16)
        r["qkv"][HEAD : 2 * HEAD, cols] = turn_pair(joint[HEAD : 2 * HEAD], cosine, sine).astype(BF16)
        r["qkv"][2 * HEAD : 3 * HEAD, cols] = joint[2 * HEAD : 3 * HEAD].astype(BF16)
        slot = i % 2
        if i >= 2:
            self.gates(i - 2).wait()
        gate, upward = joint[3 * HEAD : 3 * HEAD + ff], joint[3 * HEAD + ff :]
        r["gate_buf"][slot, :ff] = gate
        r["gate_buf"][slot, ff:] = upward
        r["mixed"][HEAD:, cols] = (gate * jax.nn.sigmoid(gate) * upward).astype(BF16)
        self.gates(i).start()

    def gates(self, i):
        r = self.r
        return pltpu.make_async_copy(
            r["gate_buf"].at[i % 2], r["gates"].at[:, pl.ds(i * CHUNK, CHUNK)], r["gate_sems"].at[i % 2]
        )

    def attend(self, b, t):
        r, batch = self.r, self.batch
        whole = slice(b * batch, (b + 1) * batch)
        if t == 0:
            r["key_rows"][...] = r["qkv"][HEAD : 2 * HEAD, whole].T
            r["place_col"][...] = as_column(r["place"][b])
        cols = slice(b * batch + t * QT, b * batch + (t + 1) * QT)
        here = slice(t * QT, (t + 1) * QT)
        place, turn = r["place"][b, :, here], r["turn"][b, :, here]
        query = r["qkv"][:HEAD, cols]
        totals = jnp.zeros((1, QT), F32)
        numer = jnp.zeros((HEAD, QT), F32)
        for k in range(batch // QT):
            keys = slice(k * QT, (k + 1) * QT)
            scores = jnp.dot(r["key_rows"][keys], query, preferred_element_type=F32)
            ok = allowed_keys(r["place_col"][keys], place, turn)
            weights = jnp.where(ok, jnp.exp2(scores * (LOG2E * HEAD**-0.5)), 0.0)
            totals = totals + jnp.sum(weights, axis=0, keepdims=True)
            value = r["qkv"][2 * HEAD :, b * batch + k * QT : b * batch + (k + 1) * QT]
            numer = numer + jnp.dot(value, weights.astype(BF16), preferred_element_type=F32)
        attended = numer / totals
        r["attended"][:, cols] = attended
        r["totals"][:, cols] = totals
        r["mixed"][:HEAD, cols] = attended.astype(BF16)


def forward_kernel(
    sizes, ff,
    x_ref, go_ref, gain_ref, bias_ref, table_ref, weight_ref, wout_ref,
    go_all, hid_all, win_all, wout_all, gain_buf,
    qkv, gates, mixed, attended, totals, place, turn, cosine, sine,
    table_all, bias_buf, hid_own, win_buf, win_ref, thin_buf, thick_buf, turn_buf, hidden_buf, gate_buf, key_rows, place_col,
    send_sems, block_sems, small_sems, win_sems, wout_sems, hidden_sems, gate_sems, load_sem, slice_sems,
):
    C, F = sizes
    c = lax.axis_index("ctx")
    f = lax.axis_index("fsdp")
    x_nbr, y_nbr, core = flip(c, 2), flip(c, 4), flip(c, 1)
    diag = flip(x_nbr, 4)
    copies = Copies(send_sems)
    here = {"ctx": c, "fsdp": f}

    def at_ctx(other):
        return {"ctx": other, "fsdp": f}

    def at_f(other):
        return {"ctx": c, "fsdp": other}

    width = x_ref.shape[1]
    total_cols = weight_ref.shape[1]
    segments = (
        (0, HEAD, 0), (width, HEAD, HEAD), (2 * width, HEAD, 2 * HEAD),
        (3 * width, ff, 3 * HEAD), (3 * width + FF, ff, 3 * HEAD + ff),
    )

    def cut(dest, k):
        base, size, row = segments[k]
        buf = thin_buf.at[dest, k] if k < 3 else thick_buf.at[dest, k - 3]
        wide = buf.shape[1]
        start = base + (dest * C + c if k < 3 else ff_chunk(C, dest, c)) * size
        first = jnp.minimum(start // 128 * 128, total_cols - wide)
        copy = pltpu.make_async_copy(
            weight_ref.at[:, pl.ds(pl.multiple_of(first, 128), wide)], buf, slice_sems.at[dest, k]
        )
        return copy, start - first, size, row, wide

    for dest in range(F):
        for k in range(len(segments)):
            cut(dest, k)[0].start()

    barrier = pltpu.get_barrier_semaphore()
    others = [lax.rem(f + s, F) for s in range(1, F)]
    for peer in [at_ctx(x_nbr), at_ctx(y_nbr), at_ctx(core)] + [at_f(o) for o in others]:
        pl.semaphore_signal(barrier, inc=1, device_id=peer, device_id_type=pl.DeviceIdType.MESH)
    pl.semaphore_wait(barrier, 3 + F - 1)

    for i, o in enumerate(others):
        copies.send(gain_ref, gain_buf.at[f], small_sems.at[0, f], at_f(o))
        copies.send(bias_ref, bias_buf.at[f], small_sems.at[1, f], at_f(o))
        copies.send(table_ref, table_all.at[f], small_sems.at[2, f], at_f(o))

    outs = (go_all, hid_all)
    rows = x_ref.shape[0]
    half = rows // 2

    def piece(a, fb, cb, part):
        ref = outs[a].at[fb, cb]
        if part is None:
            return ref
        return ref.at[pl.ds(part * half, half)]

    def forward(a, fb, cb, part, target, when=None, src=None):
        ref = piece(a, fb, cb, part)
        copies.send(ref if src is None else src, ref, block_sems.at[a, fb, cb, part or 0], target, when)

    def wait_block(a, fb, cb, part, when=None):
        def go():
            arrived(piece(a, fb, cb, part), block_sems.at[a, fb, cb, part or 0])
        if when is None:
            go()
        else:
            pl.when(when)(go)

    up, down = f + 1 < F, f > 0

    def own_xy(a, src):
        forward(a, f, c, None, at_ctx(x_nbr), src=src)
        forward(a, f, c, None, at_ctx(y_nbr), src=src)
        forward(a, f, c, None, at_ctx(core), src=src)

    def own_z(a, src):
        forward(a, f, c, None, at_f(f + 1), when=up, src=src)
        forward(a, f, c, None, at_f(f - 1), when=down, src=src)

    values = x_ref[...].astype(F32)
    centred = values - jnp.mean(values, axis=1, keepdims=True)
    normed = centred * lax.rsqrt(jnp.mean(centred * centred, axis=1, keepdims=True) + 1e-05)
    gain_buf[f] = gain_ref[...]
    bias_buf[f] = bias_ref[...]
    for o in others:
        arrived(gain_buf.at[o], small_sems.at[0, o])
        arrived(bias_buf.at[o], small_sems.at[1, o])
    share = gain_ref.shape[1]
    for s in range(F):
        cols = slice(s * share, (s + 1) * share)
        hid_own[:, cols] = (
            normed[:, cols] * gain_buf[s].astype(F32) + bias_buf[s].astype(F32)
        ).astype(BF16)
    own_z(1, hid_own)
    own_xy(1, hid_own)
    copies.local(hid_own, hid_all.at[f, c])
    copies.local(go_ref, go_all.at[f, c])

    share_rows = weight_ref.shape[0]

    def win_place(src_f):
        return win_all.at[:, pl.ds(pl.multiple_of(src_f * share_rows, share_rows), share_rows)]

    def win_send(shift):
        o = lax.rem(f + shift, F)
        copies.send(win_ref.at[o], win_place(f), win_sems.at[f], at_f(o))

    def win_wait(shift):
        o = lax.rem(f + F - shift, F)
        arrived(win_place(o), win_sems.at[o])

    def slice_weights():
        for k in range(len(segments)):
            @pl.loop(0, F)
            def _(dest):
                copy, shift, size, row, wide = cut(dest, k)
                copy.wait()
                buf = thin_buf.at[dest, k] if k < 3 else thick_buf.at[dest, k - 3]
                turn_buf[:wide] = buf[...].T
                win_ref[dest, row : row + size] = turn_buf[pl.ds(pl.multiple_of(shift, UNIT), size)]

        copies.local(win_ref.at[f], win_place(f))

    units_per_shard = wout_ref.shape[0] // UNIT
    att_units, ff_units = HEAD // UNIT * (HEADS // (C * F)), FF // (C * F) // UNIT

    def unit_of(dest, i):
        if i < att_units:
            return (dest * C + c) * att_units + i
        return C * F * att_units + ff_chunk(C, dest, c) * ff_units + (i - att_units)

    def unit_rows(ref, unit):
        return ref.at[pl.ds(pl.multiple_of(unit * UNIT, UNIT), UNIT)]

    def wout_sends():
        for step in range(F):
            dest = lax.rem(f + step, F)
            for i in range(att_units + ff_units):
                unit = unit_of(dest, i)
                mine = unit // units_per_shard == f
                src = unit_rows(wout_ref, lax.rem(unit, units_per_shard))
                dst = wout_all.at[pl.ds(i * UNIT, UNIT)]
                if step == 0:
                    copy = pltpu.make_async_copy(src, dst, wout_sems.at[i])
                    pl.when(mine)(copy.start)
                else:
                    copies.send(src, dst, wout_sems.at[i], at_f(dest), when=mine)

    def blocks_of(s):
        if s == 0:
            return [(-1, f, None)]
        return [(-1, f - s, f - s >= 0), (1, f + s, f + s < F)]

    def z_step(a, s):
        for sign, fb, valid in blocks_of(s):
            onward = valid & (up if sign < 0 else down)
            wait_block(a, fb, c, None, when=valid)
            forward(a, fb, c, None, at_f(f - sign), when=onward)
            for target in (x_nbr, y_nbr, core):
                forward(a, fb, c, None, at_ctx(target), when=valid)

    def xy_step(a, s):
        for _, fb, valid in blocks_of(s):
            wait_block(a, fb, x_nbr, None, when=valid)
            forward(a, fb, x_nbr, 0, at_ctx(y_nbr), when=valid)
            forward(a, fb, x_nbr, None, at_ctx(core), when=valid)
            wait_block(a, fb, y_nbr, None, when=valid)
            forward(a, fb, y_nbr, 1, at_ctx(x_nbr), when=valid)
            forward(a, fb, y_nbr, None, at_ctx(core), when=valid)

    def diag_step(a, s):
        for _, fb, valid in blocks_of(s):
            for part in (0, 1):
                wait_block(a, fb, diag, part, when=valid)
                forward(a, fb, diag, part, at_ctx(core), when=valid)

    def from_core(a):
        for fb in range(F):
            wait_block(a, fb, core, None)
            wait_block(a, fb, flip(core, 2), None)
            wait_block(a, fb, flip(core, 4), None)
            for part in (0, 1):
                wait_block(a, fb, flip(flip(core, 2), 4), part)

    batch = C * rows
    refs = dict(
        table=table_all, place=place, turn=turn, cos=cosine, sin=sine, w_in=win_buf, qkv=qkv,
        gates=gates, gate_buf=gate_buf, gate_sems=gate_sems, mixed=mixed, attended=attended,
        totals=totals, key_rows=key_rows, place_col=place_col,
        hidden=Stream(
            F * batch // CHUNK,
            lambda i: hid_all.at[
                i * CHUNK // batch, pl.ds(i * CHUNK % batch // rows, CHUNK // rows)
            ],
            hidden_buf, hidden_sems,
        ),
    )
    work = Forward(refs, batch, ff)

    for o in others:
        arrived(table_all.at[o], small_sems.at[2, o])
    table_all[f] = table_ref[...]
    for b in range(F):
        work.tables(b)
    slice_weights()

    z_step(1, 1)
    xy_step(1, 0)
    z_step(1, 2)
    win_send(1)
    xy_step(1, 1)
    diag_step(1, 0)
    z_step(1, 3)
    win_send(2)
    xy_step(1, 2)
    diag_step(1, 1)
    own_z(0, go_ref)
    xy_step(1, 3)
    own_xy(0, go_ref)
    win_wait(1)
    win_wait(2)
    win_send(3)
    diag_step(1, 2)
    diag_step(1, 3)
    z_step(0, 1)
    xy_step(0, 0)
    from_core(1)
    copies.finish_local()
    refs["hidden"].start()
    win_wait(3)
    load = pltpu.make_async_copy(win_all, win_buf, load_sem)
    load.start()
    wout_sends()
    load.wait()

    pieces = []
    for b in range(F):
        for i in range(batch // CHUNK):
            pieces.append(functools.partial(work.project, b * (batch // CHUNK) + i))
        for t in range(batch // QT):
            pieces.append(functools.partial(work.attend, b, t))
    steps = [
        functools.partial(z_step, 0, 2),
        functools.partial(xy_step, 0, 1),
        functools.partial(diag_step, 0, 0),
        functools.partial(z_step, 0, 3),
        functools.partial(xy_step, 0, 2),
        functools.partial(diag_step, 0, 1),
        functools.partial(xy_step, 0, 3),
        functools.partial(diag_step, 0, 2),
        functools.partial(diag_step, 0, 3),
    ]
    weave(steps, pieces)
    from_core(0)
    for i in range(att_units + ff_units):
        arrived(wout_all.at[pl.ds(i * UNIT, UNIT)], wout_sems.at[i])
    last = F * batch // CHUNK
    work.gates(last - 2).wait()
    work.gates(last - 1).wait()
    copies.finish()


def weave(steps, pieces):
    done = 0
    for i, step in enumerate(steps):
        until = (i + 1) * len(pieces) // len(steps)
        for piece in pieces[done:until]:
            piece()
        done = until
        step()


def forward_all(x, go, gain, bias, table, in_weight, wout, C, F):
    rows, width = x.shape
    shard = in_weight.shape[0]
    any_ = pl.BlockSpec(memory_space=pl.ANY)
    vmem = pl.BlockSpec(memory_space=pltpu.VMEM)
    ff = FF // (C * F)
    wout_rows = HEAD * HEADS // (C * F) + ff
    per_rank = 3 * HEAD + 2 * ff
    share = gain.shape[1]
    batch = C * rows
    tokens = F * batch
    shape = jax.ShapeDtypeStruct
    return pl.pallas_call(
        functools.partial(forward_kernel, (C, F), ff),
        out_shape=(
            shape((F, C, rows, width), BF16),
            shape((F, C, rows, width), BF16),
            shape((per_rank, width), BF16),
            shape((wout_rows, width), BF16),
            shape((F, 1, share), BF16),
            shape((3 * HEAD, tokens), BF16),
            shape((2 * ff, tokens), F32),
            shape((HEAD + ff, tokens), BF16),
            shape((HEAD, tokens), F32),
            shape((1, tokens), F32),
            shape((F, 1, batch), jnp.int32),
            shape((F, 1, batch), jnp.int32),
            shape((ROT // 2, tokens), F32),
            shape((ROT // 2, tokens), F32),
        ),
        in_specs=[vmem, any_, vmem, vmem, vmem, any_, any_],
        out_specs=(any_,) * 4 + (vmem, vmem, any_) + (vmem,) * 7,
        scratch_shapes=[
            pltpu.VMEM((F,) + table.shape, jnp.int32),
            pltpu.VMEM((F, 1, share), BF16),
            pltpu.VMEM((rows, width), BF16),
            pltpu.VMEM((per_rank, width), BF16),
            pltpu.VMEM((F, per_rank, shard), BF16),
            pltpu.VMEM((F, 3, shard, 128), BF16),
            pltpu.VMEM((F, 2, shard, 384), BF16),
            pltpu.VMEM((384, shard), BF16),
            pltpu.VMEM((2, CHUNK // rows, rows, width), BF16),
            pltpu.VMEM((2, 2 * ff, CHUNK), F32),
            pltpu.VMEM((batch, HEAD), BF16),
            pltpu.VMEM((batch, 1), jnp.int32),
            pltpu.SemaphoreType.DMA((256,)),
            pltpu.SemaphoreType.DMA((2, F, C, 2)),
            pltpu.SemaphoreType.DMA((3, F)),
            pltpu.SemaphoreType.DMA((F,)),
            pltpu.SemaphoreType.DMA((wout_rows // UNIT,)),
            pltpu.SemaphoreType.DMA((2,)),
            pltpu.SemaphoreType.DMA((2,)),
            pltpu.SemaphoreType.DMA,
            pltpu.SemaphoreType.DMA((F, 5)),
        ],
        compiler_params=pltpu.CompilerParams(
            collective_id=1, has_side_effects=True, vmem_limit_bytes=56 * 1024 * 1024
        ),
    )(x, go, gain, bias, table, in_weight, wout)


def scores_of(key_rows, query, place_col, place, turn):
    scores = jnp.dot(key_rows, query, preferred_element_type=F32)
    ok = allowed_keys(place_col, place, turn)
    return jnp.where(ok, jnp.exp2(scores * (LOG2E * HEAD**-0.5)), 0.0)


class Backward:
    def __init__(self, refs, batch, ff):
        self.r, self.batch, self.ff = refs, batch, ff

    def mixed(self, i):
        r, ff = self.r, self.ff
        cols = slice(i * CHUNK, (i + 1) * CHUNK)
        grads = r["grads"].take(i).reshape(CHUNK, -1)
        grad = nt_dot(r["w_out"][...], grads)
        gates = r["gates"].take(i)
        grad_att = grad[:HEAD].astype(BF16).astype(F32)
        inverse = 1.0 / r["totals"][:, cols]
        delta = jnp.sum(grad_att * r["attended"][:, cols], axis=0, keepdims=True)
        r["ratio"][:, cols] = delta * inverse
        r["numer"][:, cols] = (grad_att * inverse).astype(BF16)
        grad_act = grad[HEAD:].astype(BF16).astype(F32)
        gate, upward = gates[:ff], gates[ff:]
        sig = jax.nn.sigmoid(gate)
        r["joint"][3 * HEAD : 3 * HEAD + ff, cols] = (
            grad_act * upward * sig * (1.0 + gate * (1.0 - sig))
        ).astype(BF16)
        r["joint"][3 * HEAD + ff :, cols] = (grad_act * gate * sig).astype(BF16)

    def attend(self, b, t):
        r, batch = self.r, self.batch
        whole = slice(b * batch, (b + 1) * batch)
        if t == 0:
            r["key_rows"][...] = r["qkv"][HEAD : 2 * HEAD, whole].T
            r["value_rows"][...] = r["qkv"][2 * HEAD :, whole].T
            r["place_col"][...] = as_column(r["place"][b])
            r["grad_k"][...] = jnp.zeros_like(r["grad_k"])
            r["grad_v"][...] = jnp.zeros_like(r["grad_v"])
        cols = slice(b * batch + t * QT, b * batch + (t + 1) * QT)
        here = slice(t * QT, (t + 1) * QT)
        place, turn = r["place"][b, :, here], r["turn"][b, :, here]
        query, numer, ratio = r["qkv"][:HEAD, cols], r["numer"][:, cols], r["ratio"][:, cols]
        grad_q = jnp.zeros((HEAD, QT), F32)
        for k in range(batch // QT):
            keys = slice(k * QT, (k + 1) * QT)
            key_cols = slice(b * batch + k * QT, b * batch + (k + 1) * QT)
            weights = scores_of(r["key_rows"][keys], query, r["place_col"][keys], place, turn)
            pushed = jnp.dot(r["value_rows"][keys], numer, preferred_element_type=F32)
            grad_scores = (weights * (pushed - ratio)).astype(BF16)
            grad_q = grad_q + jnp.dot(
                r["qkv"][HEAD : 2 * HEAD, key_cols], grad_scores, preferred_element_type=F32
            )
            r["grad_k"][:, keys] += nt_dot(query, grad_scores)
            r["grad_v"][:, keys] += nt_dot(numer, weights.astype(BF16))
        scale = HEAD**-0.5
        r["joint"][:HEAD, cols] = turn_pair(
            grad_q * scale, r["cos"][:, cols], -r["sin"][:, cols]
        ).astype(BF16)
        if t == batch // QT - 1:
            r["joint"][HEAD : 2 * HEAD, whole] = turn_pair(
                r["grad_k"][...] * scale, r["cos"][:, whole], -r["sin"][:, whole]
            ).astype(BF16)
            r["joint"][2 * HEAD : 3 * HEAD, whole] = r["grad_v"][...].astype(BF16)


class Reduce:
    def __init__(self, sizes, pairs, rows, width, parts, bufs, sems):
        self.C, self.F = sizes
        self.pairs, self.rows, self.width, self.parts = pairs, rows, width // parts, parts
        self.c = lax.axis_index("ctx")
        self.f = lax.axis_index("fsdp")
        self.x_nbr, self.y_nbr, self.core = flip(self.c, 2), flip(self.c, 4), flip(self.c, 1)
        (
            self.core_send, self.core_recv, self.x_send, self.y_send, self.x_recv, self.y_recv,
            self.keep_l, self.keep_r, self.y2_send, self.x2_send, self.y2_recv, self.x2_recv,
            self.z_send, self.z_recv, self.turned,
        ) = bufs
        self.send_sems, self.core_sems, self.xy_sems, self.xy2_sems, self.z_sems = sems
        self.open = {}
        self.others = [lax.rem(self.f + s, self.F) for s in range(1, self.F)]
        self.steps = len(pairs) * self.F * parts

    def at_ctx(self, other):
        return {"ctx": other, "fsdp": self.f}

    def at_f(self, other):
        return {"ctx": self.c, "fsdp": other}

    def greet(self):
        barrier = pltpu.get_barrier_semaphore()
        peers = [self.at_ctx(o) for o in (self.x_nbr, self.y_nbr, self.core)]
        peers += [self.at_f(o) for o in self.others]
        for peer in peers:
            pl.semaphore_signal(
                barrier, inc=1, device_id=peer, device_id_type=pl.DeviceIdType.MESH
            )
        pl.semaphore_wait(barrier, len(peers))

    def send(self, key, t, src, dst, recv_sem, target):
        copy = pltpu.make_async_remote_copy(
            src_ref=src, dst_ref=dst, send_sem=self.send_sems.at[key, t], recv_sem=recv_sem,
            device_id=target, device_id_type=pl.DeviceIdType.MESH,
        )
        copy.start()
        self.open[key, t] = copy

    def sent(self, key, t):
        if (key, t) in self.open:
            self.open.pop((key, t)).wait_send()

    def place(self, t):
        return t // (self.F * self.parts), t // self.parts % self.F, t % self.parts

    def dest(self, i):
        return lax.rem(self.f + 1 + i, self.F)

    def turn(self, t):
        pair, i, _ = self.place(t)
        left_ref = self.pairs[pair][0]
        size = left_ref.shape[0]
        rows = self.rows
        block = self.dest(i) * self.C
        for slot, base in enumerate((self.core, self.c)):
            parts = [
                left_ref[:, pl.ds(pl.multiple_of((block + cc) * rows, rows), rows)]
                for cc in (base, flip(base, 2), flip(base, 4), flip(flip(base, 2), 4))
            ]
            self.turned[slot, :, :size] = jnp.concatenate(parts, axis=1).T

    def enter(self, t, tile=512):
        pair, i, part = self.place(t)
        w_ref = self.pairs[pair][1]
        size = w_ref.shape[0]
        rows, mid = self.rows, self.width // 2
        if part == 0:
            self.turn(t)
        self.sent(0, t - 2)
        left = self.turned[0, :, :size]
        for n in range(self.width // tile):
            cols = slice(part * self.width + n * tile, part * self.width + (n + 1) * tile)
            self.core_send[t % 2, :, n * tile : (n + 1) * tile] = jnp.dot(
                left, w_ref[:, cols], preferred_element_type=F32
            ).astype(BF16)
        self.send(
            0, t, self.core_send.at[t % 2], self.core_recv.at[t % 2], self.core_sems.at[t],
            self.at_ctx(self.core),
        )
        left = self.turned[1, :, :size]
        sums = []
        for side in range(2):
            cols = slice(part * self.width + side * mid, part * self.width + (side + 1) * mid)
            sums.append(jnp.dot(left, w_ref[:, cols], preferred_element_type=F32))
        arrived(self.core_recv.at[t % 2], self.core_sems.at[t])
        for key, keep, out, recv, kept, sent_rows, target in (
            (1, self.keep_l, self.x_send, self.x_recv, (0, 2), (1, 3), self.x_nbr),
            (2, self.keep_r, self.y_send, self.y_recv, (0, 1), (2, 3), self.y_nbr),
        ):
            self.sent(key, t - 2)
            total = sums[key - 1] + self.core_recv[t % 2, :, (key - 1) * mid : key * mid].astype(F32)
            for i, b in enumerate(sent_rows):
                out[t % 2, i * rows : (i + 1) * rows] = total[b * rows : (b + 1) * rows].astype(BF16)
            self.send(
                key, t, out.at[t % 2], recv.at[t % 3], self.xy_sems.at[key - 1, t], self.at_ctx(target)
            )
            for i, b in enumerate(kept):
                keep[t % 3, i * rows : (i + 1) * rows] = total[b * rows : (b + 1) * rows]

    def second(self, t):
        rows, slot = self.rows, t % 3
        sides = (
            (3, self.keep_l, self.x_recv, self.y2_send, self.y2_recv, self.y_nbr),
            (4, self.keep_r, self.y_recv, self.x2_send, self.x2_recv, self.x_nbr),
        )
        for key, keep, recv, out, _, _ in sides:
            arrived(recv.at[slot], self.xy_sems.at[key - 3, t])
            self.sent(key, t - 2)
            out[t % 2] = (keep[slot, rows:] + recv[slot, rows:].astype(F32)).astype(BF16)
            keep[slot, :rows] = keep[slot, :rows] + recv[slot, :rows].astype(F32)
        for key, _, _, out, out_recv, target in sides:
            self.send(
                key, t, out.at[t % 2], out_recv.at[slot], self.xy2_sems.at[key - 3, t],
                self.at_ctx(target),
            )

    def third(self, t):
        pair, i, part = self.place(t)
        rows, mid, slot = self.rows, self.width // 2, t % 3
        arrived(self.y2_recv.at[slot], self.xy2_sems.at[0, t])
        arrived(self.x2_recv.at[slot], self.xy2_sems.at[1, t])
        total_l = self.keep_l[slot, :rows] + self.y2_recv[slot].astype(F32)
        total_r = self.keep_r[slot, :rows] + self.x2_recv[slot].astype(F32)
        if i < self.F - 1:
            for key, u in list(self.open):
                if key == 5 and u % 2 == t % 2:
                    self.sent(key, u)
            self.z_send[t % 2, :, :mid] = total_l.astype(BF16)
            self.z_send[t % 2, :, mid:] = total_r.astype(BF16)
            self.send(
                5, t, self.z_send.at[t % 2], self.z_recv.at[pair, part, self.f],
                self.z_sems.at[pair, part, self.f], self.at_f(self.dest(i)),
            )
            return None
        total = jnp.concatenate([total_l, total_r], axis=1)
        for o in self.others:
            arrived(self.z_recv.at[pair, part, o], self.z_sems.at[pair, part, o])
            total = total + self.z_recv[pair, part, o].astype(F32)
        return total

    def run(self, fill):
        sums = []
        self.enter(0)
        self.enter(1)
        for t in range(self.steps):
            fill(t)
            self.second(t)
            if t >= 1:
                sums.append(self.third(t - 1))
            if t + 2 < self.steps:
                self.enter(t + 2)
        fill(self.steps)
        sums.append(self.third(self.steps - 1))
        return sums

    def finish(self):
        for key, t in list(self.open):
            self.sent(key, t)


def reduce_scratch(F, rows, width, parts, pairs, features):
    width = width // parts
    mid = width // 2
    steps = pairs * F * parts
    return [
        pltpu.VMEM((2, 4 * rows, width), BF16),
        pltpu.VMEM((2, 4 * rows, width), BF16),
        pltpu.VMEM((2, 2 * rows, mid), BF16),
        pltpu.VMEM((2, 2 * rows, mid), BF16),
        pltpu.VMEM((3, 2 * rows, mid), BF16),
        pltpu.VMEM((3, 2 * rows, mid), BF16),
        pltpu.VMEM((3, 2 * rows, mid), F32),
        pltpu.VMEM((3, 2 * rows, mid), F32),
        pltpu.VMEM((2, rows, mid), BF16),
        pltpu.VMEM((2, rows, mid), BF16),
        pltpu.VMEM((3, rows, mid), BF16),
        pltpu.VMEM((3, rows, mid), BF16),
        pltpu.VMEM((2, rows, width), BF16),
        pltpu.VMEM((pairs, parts, F, rows, width), BF16),
        pltpu.VMEM((2, 4 * rows, features), BF16),
        pltpu.SemaphoreType.DMA((6, steps)),
        pltpu.SemaphoreType.DMA((steps,)),
        pltpu.SemaphoreType.DMA((2, steps)),
        pltpu.SemaphoreType.DMA((2, steps)),
        pltpu.SemaphoreType.DMA((pairs, parts, F)),
    ]


PIECES = ((0, 4), (4, 1), (5, 1), (6, 9))


class Spread:
    def __init__(self, sizes, shard_units, win_ref, wout_ref, win_all, wout_all, copies, block_sems, piece_sems):
        self.C, self.F = sizes
        self.shard_units = shard_units
        self.win_ref, self.wout_ref, self.win_all, self.wout_all = win_ref, wout_ref, win_all, wout_all
        self.copies, self.block_sems, self.piece_sems = copies, block_sems, piece_sems
        self.c = lax.axis_index("ctx")
        self.f = lax.axis_index("fsdp")
        self.x_nbr, self.y_nbr, self.core = flip(self.c, 2), flip(self.c, 4), flip(self.c, 1)
        self.diag = flip(self.x_nbr, 4)
        self.share = win_all.shape[3]
        self.half = win_all.shape[2] // 2
        self.near = (self.x_nbr, self.y_nbr, self.core)

    def at_ctx(self, other):
        return {"ctx": other, "fsdp": self.f}

    def at_f(self, other):
        return {"ctx": self.c, "fsdp": other}

    def win_slice(self, dest):
        return self.win_ref.at[:, pl.ds(pl.multiple_of(dest * self.share, self.share), self.share)]

    def block(self, fb, cb, part):
        ref = self.win_all.at[fb, cb]
        return ref if part is None else ref.at[pl.ds(part * self.half, self.half)]

    def pass_block(self, fb, cb, part, target, src=None):
        ref = self.block(fb, cb, part)
        sem = self.block_sems.at[fb, cb, part or 0]
        self.copies.send(ref if src is None else src, ref, sem, target)

    def wait_block(self, fb, cb, part):
        arrived(self.block(fb, cb, part), self.block_sems.at[fb, cb, part or 0])

    def piece(self, fb, cb, p):
        att_units, ff_units = PIECES[0][1], sum(n for _, n in PIECES[1:])
        start, units = PIECES[p]
        if p == 0:
            unit = (fb * self.C + cb) * att_units
        else:
            chunk = ff_chunk(self.C, fb, cb)
            unit = self.C * self.F * att_units + chunk * ff_units + (start - att_units)
        place = pl.multiple_of(lax.rem(unit, self.shard_units) * UNIT, UNIT)
        return unit // self.shard_units, self.wout_all.at[pl.ds(place, units * UNIT)]

    def own_piece(self, p):
        start, units = PIECES[p]
        return self.wout_ref.at[pl.ds(start * UNIT, units * UNIT)]

    def pass_piece(self, fb, cb, p, target, when, src=None):
        ref = self.piece(fb, cb, p)[1]
        self.copies.send(ref if src is None else src, ref, self.piece_sems.at[fb, cb, p], target, when)

    def wait_piece(self, fb, cb, p, when):
        def go():
            arrived(self.piece(fb, cb, p)[1], self.piece_sems.at[fb, cb, p])
        pl.when(when)(go)

    def z_send(self, shift):
        f, c = self.f, self.c
        o = lax.rem(f + shift, self.F)
        self.copies.send(
            self.win_slice(o), self.block(f, c, None), self.block_sems.at[f, c, 0], self.at_f(o)
        )
        for p in range(len(PIECES)):
            self.pass_piece(f, c, p, self.at_f(o), self.piece(f, c, p)[0] == o, src=self.own_piece(p))

    def own(self):
        f, c = self.f, self.c
        mine = self.win_slice(f)
        for target in self.near:
            self.pass_block(f, c, None, self.at_ctx(target), src=mine)
        self.copies.local(mine, self.block(f, c, None))
        for p in range(len(PIECES)):
            shard, place = self.piece(f, c, p)
            for target in self.near:
                self.pass_piece(f, c, p, self.at_ctx(target), shard == f, src=self.own_piece(p))
            self.copies.local(self.own_piece(p), place, shard == f)

    def z_step(self, fb):
        f, c = self.f, self.c
        self.wait_block(fb, c, None)
        for target in self.near:
            self.pass_block(fb, c, None, self.at_ctx(target))
        for p in range(len(PIECES)):
            here = self.piece(fb, c, p)[0] == f
            self.wait_piece(fb, c, p, here)
            for target in self.near:
                self.pass_piece(fb, c, p, self.at_ctx(target), here)

    def xy_step(self, fb, way):
        x_nbr, y_nbr, core = self.near
        self.wait_block(fb, x_nbr, None)
        self.pass_block(fb, x_nbr, 0, self.at_ctx(y_nbr))
        self.pass_block(fb, x_nbr, None, self.at_ctx(core))
        self.wait_block(fb, y_nbr, None)
        self.pass_block(fb, y_nbr, 1, self.at_ctx(x_nbr))
        self.pass_block(fb, y_nbr, None, self.at_ctx(core))
        for p in range(len(PIECES)):
            by_x = (p < 2) == (way == 0)
            for source, onward, turn in ((x_nbr, y_nbr, by_x), (y_nbr, x_nbr, not by_x)):
                here = self.piece(fb, source, p)[0] == self.f
                self.wait_piece(fb, source, p, here)
                if turn:
                    self.pass_piece(fb, source, p, self.at_ctx(onward), here)
                self.pass_piece(fb, source, p, self.at_ctx(core), here)

    def diag_step(self, fb):
        diag, core = self.diag, self.core
        for part in (0, 1):
            self.wait_block(fb, diag, part)
            self.pass_block(fb, diag, part, self.at_ctx(core))
        for p in range(len(PIECES)):
            here = self.piece(fb, diag, p)[0] == self.f
            self.wait_piece(fb, diag, p, here)
            self.pass_piece(fb, diag, p, self.at_ctx(core), here)

    def rest(self, terms, sums):
        F, f = self.F, self.f
        order = [f] + [lax.rem(f + F - s, F) for s in range(1, F)]
        terms.step(0)
        for s in range(F + 2):
            if s + 1 < F:
                self.z_step(order[s + 1])
                if s + 2 < F:
                    self.z_send(s + 2)
            if s < 3:
                terms.step(s + 1)
            if s < F:
                self.xy_step(order[s], s % 2)
            if 0 <= s - 1 < F:
                self.diag_step(order[s - 1])
        core = self.core
        beyond = (core, flip(core, 2), flip(core, 4))
        corner = flip(flip(core, 2), 4)
        for fb in range(F):
            for cb in beyond:
                self.wait_block(fb, cb, None)
            for part in (0, 1):
                self.wait_block(fb, corner, part)
            for cb in beyond + (corner,):
                for p in range(len(PIECES)):
                    self.wait_piece(fb, cb, p, self.piece(fb, cb, p)[0] == f)
        sums[...] = terms.finish()
        self.copies.finish()


class Terms:
    def __init__(self, spread, value, bufs, sems):
        self.spread, self.value, self.bufs, self.sems = spread, value, bufs, sems
        self.others = [lax.rem(spread.f + s, spread.F) for s in range(1, spread.F)]

    def step(self, i):
        spread = self.spread
        near, parts, shares = self.bufs
        x_nbr, y_nbr, core = spread.near
        if i > 0:
            arrived(near.at[i - 1], self.sems.at[i - 1])
            self.value = self.value + near[i - 1]
        if i < 3:
            parts[i] = self.value
            target = spread.at_ctx((core, x_nbr, y_nbr)[i])
            spread.copies.send(parts.at[i], near.at[i], self.sems.at[i], target)
            return
        share = spread.share
        for s in range(spread.F):
            parts[3 + s, :, :share] = self.value[:, s * share : (s + 1) * share]
        for o in self.others:
            spread.copies.send(
                parts.at[3 + o, :, pl.ds(0, share)], shares.at[spread.f], self.sems.at[3 + spread.f],
                spread.at_f(o),
            )

    def finish(self):
        _, parts, shares = self.bufs
        f, share = self.spread.f, self.spread.share
        shares[f] = parts[3 + f, :, :share]
        for o in self.others:
            arrived(shares.at[o], self.sems.at[3 + o])
        total = shares[0]
        for s in range(1, self.spread.F):
            total = total + shares[s]
        return total


SLAB = 256
PARTS = 2


def backward_kernel(
    sizes, ff, shard_units,
    mixed_ref, w_out_ref, w_in_ref, x_ref, go_ref, gain_ref, qkv, attended, totals, place, turn, cosine,
    sine, hid_all, go_all, gates,
    result_ref, grad_in_ref, sums_ref, win_all, wout_all,
    go_buf, slab_buf, gate_buf, numer, ratio, key_rows, value_rows, place_col, grad_k, grad_v, joint, dw_in, dw_out,
    near_terms, part_terms, share_terms,
    go_sems, slab_sems, gate_sems, send_sems, block_sems, piece_sems, term_sems, *shared,
):
    C, F = sizes
    rows, width = x_ref.shape
    batch = C * rows
    reduce = Reduce(
        sizes, ((mixed_ref, w_out_ref), (joint, w_in_ref)), rows, width, PARTS, shared[:15], shared[15:]
    )
    count = F * batch // CHUNK
    slabs = width // SLAB
    wide = Stream(
        count,
        lambda i: go_all.at[i * CHUNK // batch, pl.ds(i * CHUNK % batch // rows, CHUNK // rows)],
        go_buf, go_sems,
    )
    refs = dict(
        grads=wide,
        gates=Stream(count, lambda i: gates.at[:, pl.ds(i * CHUNK, CHUNK)], gate_buf, gate_sems),
        w_out=w_out_ref, totals=totals, attended=attended, ratio=ratio, numer=numer, joint=joint,
        qkv=qkv, key_rows=key_rows, value_rows=value_rows, place_col=place_col, place=place,
        turn=turn, grad_k=grad_k, grad_v=grad_v, cos=cosine, sin=sine,
    )
    refs["grads"].start()
    refs["gates"].start()
    work = Backward(refs, batch, ff)
    pieces = []
    for b in range(F):
        for i in range(batch // CHUNK):
            pieces.append(functools.partial(work.mixed, b * (batch // CHUNK) + i))
        for t in range(batch // QT):
            pieces.append(functools.partial(work.attend, b, t))

    def slab_source(i):
        source = hid_all if i < slabs else go_all
        return source.at[:, :, :, pl.ds(i % slabs * SLAB, SLAB)]

    slab_stream = Stream(2 * slabs, slab_source, slab_buf, slab_sems)

    def weight_grad(i):
        if i == 0:
            slab_stream.start()
        slab = slab_stream.take(i).reshape(C * F * rows, SLAB)
        left, out = (joint, dw_in) if i < slabs else (mixed_ref, dw_out)
        out[:, i % slabs * SLAB : (i % slabs + 1) * SLAB] = jnp.dot(
            left[...], slab, preferred_element_type=F32
        ).astype(BF16)

    spread = Spread(
        sizes, shard_units, dw_in, dw_out, win_all, wout_all, Copies(send_sems), block_sems, piece_sems
    )
    grads = [functools.partial(weight_grad, i) for i in range(2 * slabs)]
    half = reduce.steps // 2
    before = half - 1

    def fill(t):
        if t < before:
            todo = pieces[t * len(pieces) // before : (t + 1) * len(pieces) // before]
        else:
            gaps = half - 1
            k = t - before
            todo = grads[k * len(grads) // gaps : (k + 1) * len(grads) // gaps] if k < gaps else []
        for piece in todo:
            piece()
        if t == reduce.steps - 1:
            spread.z_send(1)

    reduce.greet()
    sums = [part for part in reduce.run(fill) if part is not None]
    spread.own()
    total = jnp.concatenate(sums[:PARTS], axis=1)
    values = x_ref[...].astype(F32)
    result_ref[...] = (values + total).astype(BF16)
    total = jnp.concatenate(sums[PARTS:], axis=1)
    centred = values - jnp.mean(values, axis=1, keepdims=True)
    inverse_std = lax.rsqrt(jnp.mean(centred * centred, axis=1, keepdims=True) + 1e-05)
    normed = centred * inverse_std
    gain = jnp.concatenate([gain_ref[s].astype(F32) for s in range(F)], axis=1)
    g = total * gain
    back = inverse_std * (
        g - jnp.mean(g, axis=1, keepdims=True) - normed * jnp.mean(g * normed, axis=1, keepdims=True)
    )
    grad_in_ref[...] = (go_ref[...].astype(F32) + back).astype(BF16)
    terms = jnp.concatenate(
        [jnp.sum(total * normed, axis=0, keepdims=True), jnp.sum(total, axis=0, keepdims=True)], axis=0
    )
    reduce.finish()
    spread.rest(Terms(spread, terms, (near_terms, part_terms, share_terms), term_sems), sums_ref)


def backward_all(
    mixed, w_out, w_in, x, go, gains, qkv, attended, totals, place, turn, cosine, sine, hid_all, go_all, gates,
    shard_rows, C, F,
):
    rows, width = x.shape
    ff = gates.shape[0] // 2
    batch, tokens = C * rows, C * F * rows
    per_rank, share = w_in.shape[0], width // F
    vmem = pl.BlockSpec(memory_space=pltpu.VMEM)
    any_ = pl.BlockSpec(memory_space=pl.ANY)
    shape = jax.ShapeDtypeStruct
    dma = pltpu.SemaphoreType.DMA
    return pl.pallas_call(
        functools.partial(backward_kernel, (C, F), ff, shard_rows // UNIT),
        out_shape=(
            shape((rows, width), BF16),
            shape((rows, width), BF16),
            shape((2, share), F32),
            shape((F, C, per_rank, share), BF16),
            shape((shard_rows, width), BF16),
        ),
        in_specs=[vmem] * 13 + [any_] * 3,
        out_specs=(vmem,) * 3 + (any_,) * 2,
        scratch_shapes=[
            pltpu.VMEM((2, CHUNK // rows, rows, width), BF16),
            pltpu.VMEM((2, F, C, rows, SLAB), BF16),
            pltpu.VMEM((2, 2 * ff, CHUNK), F32),
            pltpu.VMEM((HEAD, tokens), BF16),
            pltpu.VMEM((1, tokens), F32),
            pltpu.VMEM((batch, HEAD), BF16),
            pltpu.VMEM((batch, HEAD), BF16),
            pltpu.VMEM((batch, 1), jnp.int32),
            pltpu.VMEM((HEAD, batch), F32),
            pltpu.VMEM((HEAD, batch), F32),
            pltpu.VMEM((per_rank, tokens), BF16),
            pltpu.VMEM((per_rank, width), BF16),
            pltpu.VMEM(w_out.shape, BF16),
            pltpu.VMEM((3, 2, width), F32),
            pltpu.VMEM((3 + F, 2, width), F32),
            pltpu.VMEM((F, 2, share), F32),
            dma((2,)),
            dma((2,)),
            dma((2,)),
            dma((288,)),
            dma((F, C, 2)),
            dma((F, C, len(PIECES))),
            dma((3 + F,)),
        ] + reduce_scratch(F, rows, width, PARTS, 2, per_rank),
        compiler_params=pltpu.CompilerParams(
            collective_id=2, has_side_effects=True, vmem_limit_bytes=60 * 1024 * 1024
        ),
    )(mixed, w_out, w_in, x, go, gains, qkv, attended, totals, place, turn, cosine, sine, hid_all, go_all, gates)


TURN_ROWS = 192


def turn_kernel(ff, src, rows_ref, out, rows_out, in_buf, out_buf, row_buf, wide_buf, in_sems, out_sems, row_sems, wide_sems):
    F, C = src.shape[0], src.shape[1]
    share = src.shape[3]
    steps = []
    base = 0
    in_order = list(range(C))
    ff_order = [cb for _, cb in sorted((ff_chunk(C, 0, cb), cb) for cb in in_order)]
    for row, size, devices in (
        (0, HEAD, in_order), (HEAD, HEAD, in_order), (2 * HEAD, HEAD, in_order),
        (3 * HEAD, ff, ff_order), (3 * HEAD + ff, ff, ff_order),
    ):
        for fb in range(F):
            steps.append((fb, row, size, base + fb * C * size, devices))
        base += F * C * size

    def fetch(i):
        fb, row, size, _, devices = steps[i]
        return [
            pltpu.make_async_copy(
                src.at[fb, cb, pl.ds(row, size)], in_buf.at[i % 2, j, pl.ds(0, size)], in_sems.at[i % 2, j]
            )
            for j, cb in enumerate(devices)
        ]

    def store(i):
        _, _, size, col, _ = steps[i]
        return pltpu.make_async_copy(
            out_buf.at[i % 2, :, pl.ds(0, C * size)], out.at[:, pl.ds(col, C * size)], out_sems.at[i % 2]
        )

    def fetch_rows(i):
        return pltpu.make_async_copy(
            rows_ref.at[pl.ds(i * TURN_ROWS, TURN_ROWS)], row_buf.at[i % 2], row_sems.at[i % 2]
        )

    def store_rows(i):
        return pltpu.make_async_copy(
            wide_buf.at[i % 2], rows_out.at[pl.ds(i * TURN_ROWS, TURN_ROWS)], wide_sems.at[i % 2]
        )

    row_steps = rows_ref.shape[0] // TURN_ROWS
    done = 0
    for copy in fetch(0):
        copy.start()
    fetch_rows(0).start()
    for i, (fb, row, size, col, _) in enumerate(steps):
        if i + 1 < len(steps):
            for copy in fetch(i + 1):
                copy.start()
        until = (i + 1) * row_steps // len(steps)
        for j in range(done, until):
            if j + 1 < row_steps:
                fetch_rows(j + 1).start()
            fetch_rows(j).wait()
            if j >= 2:
                store_rows(j - 2).wait()
            wide_buf[j % 2] = row_buf[j % 2].astype(F32)
            store_rows(j).start()
        done = until
        for copy in fetch(i):
            copy.wait()
        if i >= 2:
            store(i - 2).wait()
        block = in_buf[i % 2, :, :size, :].reshape(C * size, share).astype(F32)
        out_buf[i % 2, :, : C * size] = block.T
        store(i).start()
    store(len(steps) - 2).wait()
    store(len(steps) - 1).wait()
    store_rows(row_steps - 2).wait()
    store_rows(row_steps - 1).wait()


def turn_blocks(blocks, out_rows, ff):
    F, C, per_rank, share = blocks.shape
    count, width = out_rows.shape
    any_ = pl.BlockSpec(memory_space=pl.ANY)
    dma = pltpu.SemaphoreType.DMA
    return pl.pallas_call(
        functools.partial(turn_kernel, ff),
        out_shape=(
            jax.ShapeDtypeStruct((share, F * C * per_rank), F32),
            jax.ShapeDtypeStruct((count, width), F32),
        ),
        in_specs=[any_, any_],
        out_specs=(any_, any_),
        scratch_shapes=[
            pltpu.VMEM((2, C, ff, share), BF16),
            pltpu.VMEM((2, share, C * ff), F32),
            pltpu.VMEM((2, TURN_ROWS, width), BF16),
            pltpu.VMEM((2, TURN_ROWS, width), F32),
            dma((2, C)),
            dma((2,)),
            dma((2,)),
            dma((2,)),
        ],
        compiler_params=pltpu.CompilerParams(vmem_limit_bytes=40 * 1024 * 1024),
    )(blocks, out_rows)


def tp_body(C, F, inputs, gain, bias, in_weight, out_weight, grad_out, lengths, order):
    rows, width = inputs.shape[1:]
    T = C * F
    ff = FF // T
    x = inputs[0]
    go = grad_out[0]

    count = lengths.shape[1] + order.shape[1]
    table = jnp.pad(jnp.concatenate([lengths, order], axis=1), ((0, 0), (0, 128 - count)))

    (
        go_all, hid_all, w_in, w_out, gains, qkv, gates, mixed, attended, totals, place, turn, cosine, sine
    ) = forward_all(x, go, gain[None], bias[None], table, in_weight, out_weight, C, F)
    result, grad_in, sums, blocks, out_rows = backward_all(
        mixed, w_out, w_in, x, go, gains, qkv, attended, totals, place, turn, cosine, sine, hid_all, go_all,
        gates, out_weight.shape[0], C, F,
    )
    in_weight_grad, out_weight_grad = turn_blocks(blocks, out_rows, ff)
    return (result[None], grad_in[None], in_weight_grad, out_weight_grad, sums[0], sums[1])


def solution(mesh):
    in_specs = (
        P("fsdp", "ctx", None),
        P("fsdp"),
        P("fsdp"),
        P("fsdp", None),
        P("fsdp", None),
        P("fsdp", "ctx", None),
        P("fsdp", None),
        P("fsdp", None),
    )
    out_specs = (
        P("fsdp", "ctx", None),
        P("fsdp", "ctx", None),
        P("fsdp", None),
        P("fsdp", None),
        P("fsdp"),
        P("fsdp"),
    )
    C, F = mesh.shape["ctx"], mesh.shape["fsdp"]
    if (C, F) == (8, 4):
        work = functools.partial(tp_body, C, F)
    else:
        work = body
    return jax.shard_map(work, mesh=mesh, in_specs=in_specs, out_specs=out_specs, check_vma=False)
```

```python
import functools
import math

import jax
import jax.numpy as jnp
from jax import lax
from jax.experimental import pallas as pl
from jax.experimental.pallas import tpu as pltpu
from jax.sharding import PartitionSpec as P

HEADS = 32
HEAD = 64
ROT = 16
FF = 5632
BLOCK = 64
BF16 = jnp.bfloat16
F32 = jnp.float32
UNIT = 16


def places_of(index, length_row, order_row):
    count = order_row.shape[0]
    hit = (index // BLOCK)[:, None] == jnp.arange(count, dtype=jnp.int32)[None, :]
    block_id = jnp.sum(jnp.where(hit, order_row[None, :], 0), axis=1)
    place = block_id * BLOCK + index % BLOCK
    ends = jnp.cumsum(length_row)
    starts = ends - length_row
    inside = (place[:, None] >= starts[None, :]) & (place[:, None] < ends[None, :])
    docs = jnp.sum(
        jnp.where(inside, jnp.arange(length_row.shape[0], dtype=jnp.int32)[None, :], 0), axis=1
    )
    first = jnp.sum(jnp.where(inside, starts[None, :], 0), axis=1)
    return (place, docs, place - first)


def rotate(values, positions, sign):
    half = ROT // 2
    freq = 10000.0 ** (-2.0 * jnp.arange(half, dtype=jnp.float32) / ROT)
    angle = positions.astype(jnp.float32)[:, None] * freq[None, :]
    cosine = jnp.cos(angle)[:, None, :]
    sine = sign * jnp.sin(angle)[:, None, :]
    first = values[..., :half]
    second = values[..., half:ROT]
    return jnp.concatenate(
        [first * cosine - second * sine, second * cosine + first * sine, values[..., ROT:]], axis=-1
    )


def rounded(values):
    return lax.optimization_barrier(values.astype(jnp.bfloat16)).astype(jnp.float32)


def transposed_dot(left, right):
    return lax.dot_general(
        left, right, (((0,), (0,)), ((), ())), preferred_element_type=jnp.float32
    )


def against_rows(left, right):
    return lax.dot_general(
        left, right, (((1,), (1,)), ((), ())), preferred_element_type=jnp.float32
    )


def body(inputs, gain, bias, in_weight, out_weight, grad_out, lengths, order):
    rows = inputs.shape[1]
    width = inputs.shape[2]
    length_row = lengths[0]
    order_row = order[0]
    local_index = lax.axis_index("ctx") * rows + jnp.arange(rows, dtype=jnp.int32)
    query_place, query_doc, query_turn = places_of(local_index, length_row, order_row)
    scale = HEAD ** (-0.5)
    head_shape = (rows, HEADS, HEAD)
    values_in = inputs[0].astype(jnp.float32)
    centred = values_in - jnp.mean(values_in, axis=1, keepdims=True)
    inverse_std = lax.rsqrt(jnp.mean(centred * centred, axis=1, keepdims=True) + 1e-05)
    normed = centred * inverse_std
    weight_piece = lax.all_gather(in_weight, "fsdp", axis=0, tiled=True)
    gain_piece = lax.all_gather(gain, "fsdp", axis=0, tiled=True)
    bias_piece = lax.all_gather(bias, "fsdp", axis=0, tiled=True)
    count = weight_piece.shape[0]
    columns = normed
    hidden_piece = (
        columns * gain_piece.astype(jnp.float32) + bias_piece.astype(jnp.float32)
    ).astype(jnp.bfloat16)
    joint_sum = jnp.dot(hidden_piece, weight_piece, preferred_element_type=jnp.float32)
    gain_full = gain_piece.astype(jnp.float32)
    joint, hidden_in, gain_full = (joint_sum, hidden_piece, gain_full)
    queries = rotate(joint[:, :width].reshape(head_shape), query_turn, 1.0).astype(jnp.bfloat16)
    keys = (
        rotate(joint[:, width : 2 * width].reshape(head_shape), query_turn, 1.0)
        .astype(jnp.bfloat16)
        .reshape(rows, width)
    )
    values = joint[:, 2 * width : 3 * width].astype(jnp.bfloat16)
    gate = joint[:, 3 * width : 3 * width + FF]
    upward = joint[:, 3 * width + FF :]

    def exp_scores(key_block, start, count):
        key_place, key_doc, unused_turn = places_of(
            start + jnp.arange(count, dtype=jnp.int32), length_row, order_row
        )
        scores = (
            jnp.einsum(
                "qhd,khd->hqk",
                queries,
                key_block.reshape(count, HEADS, HEAD),
                preferred_element_type=jnp.float32,
            )
            * scale
        )
        allowed = (query_doc[:, None] == key_doc[None, :]) & (
            key_place[None, :] <= query_place[:, None]
        )
        return jnp.where(allowed[None], jnp.exp(scores), 0.0)

    empty_attention = (jnp.zeros(head_shape, jnp.float32), jnp.zeros((HEADS, rows), jnp.float32))
    key_piece = lax.all_gather(keys, "ctx", axis=0, tiled=True)
    value_piece = lax.all_gather(values, "ctx", axis=0, tiled=True)
    count = key_piece.shape[0]
    block_rows = math.gcd(count, 512)

    def add_block(j, state):
        numer, totals = state
        offset = j * block_rows
        key_block = lax.dynamic_slice_in_dim(key_piece, offset, block_rows, 0)
        value_block = lax.dynamic_slice_in_dim(value_piece, offset, block_rows, 0)
        weights = exp_scores(key_block, offset, block_rows)
        totals = totals + jnp.sum(weights, axis=2)
        numer = numer + jnp.einsum(
            "hqk,khd->qhd",
            weights.astype(jnp.bfloat16),
            value_block.reshape(block_rows, HEADS, HEAD),
            preferred_element_type=jnp.float32,
        )
        return (numer, totals)

    numer, totals = lax.fori_loop(0, count // block_rows, add_block, empty_attention)
    attended = numer / jnp.transpose(totals)[:, :, None]
    sigmoid_gate = jax.nn.sigmoid(gate)
    activated = gate * sigmoid_gate * upward
    mixed_in = jnp.concatenate(
        [attended.reshape(rows, width).astype(jnp.bfloat16), activated.astype(jnp.bfloat16)], axis=1
    )
    columns = mixed_in
    mixed = jnp.dot(
        columns,
        lax.all_gather(out_weight, "fsdp", axis=0, tiled=True),
        preferred_element_type=jnp.float32,
    )
    result = (values_in + mixed).astype(jnp.bfloat16)
    grad_rows = grad_out[0]
    grad_mixed = against_rows(grad_rows, lax.all_gather(out_weight, "fsdp", axis=0, tiled=True))
    grad_att = grad_mixed[:, :width].astype(jnp.bfloat16).reshape(head_shape)
    grad_act = rounded(grad_mixed[:, width:])
    grad_gate = grad_act * upward * sigmoid_gate * (1.0 + gate * (1.0 - sigmoid_gate))
    grad_up = grad_act * gate * sigmoid_gate
    delta = jnp.transpose(jnp.sum(grad_att.astype(jnp.float32) * attended, axis=2))
    grad_numer = (grad_att.astype(jnp.float32) / jnp.transpose(totals)[:, :, None]).astype(
        jnp.bfloat16
    )
    ratio = delta / totals
    keys_all, values_all = (
        lax.all_gather(keys, "ctx", axis=0, tiled=True),
        lax.all_gather(values, "ctx", axis=0, tiled=True),
    )
    group = keys_all.shape[0]

    def score_grads(key_block, value_block, start, count):
        weights = exp_scores(key_block, start, count)
        pushed = jnp.einsum(
            "qhd,khd->hqk",
            grad_numer,
            value_block.reshape(count, HEADS, HEAD),
            preferred_element_type=jnp.float32,
        )
        return (weights, (weights * (pushed - ratio[:, :, None])).astype(jnp.bfloat16))

    query_rows = math.gcd(group, 512)

    def query_block_grad(j, total):
        offset = j * query_rows
        key_block = lax.dynamic_slice_in_dim(keys_all, offset, query_rows, 0)
        value_block = lax.dynamic_slice_in_dim(values_all, offset, query_rows, 0)
        unused_weights, grad_scores = score_grads(key_block, value_block, offset, query_rows)
        return total + jnp.einsum(
            "hqk,khd->qhd",
            grad_scores,
            key_block.reshape(query_rows, HEADS, HEAD),
            preferred_element_type=jnp.float32,
        )

    grad_query = (
        lax.fori_loop(0, group // query_rows, query_block_grad, jnp.zeros(head_shape, jnp.float32))
        * scale
    )
    key_block_rows = math.gcd(rows * lax.axis_size("ctx"), 512)

    def key_block_grad(j, terms):
        offset = j * key_block_rows
        key_block = lax.dynamic_slice_in_dim(keys_all, offset, key_block_rows, 0)
        value_block = lax.dynamic_slice_in_dim(values_all, offset, key_block_rows, 0)
        weights, grad_scores = score_grads(key_block, value_block, offset, key_block_rows)
        key_part = (
            jnp.einsum("hqk,qhd->khd", grad_scores, queries, preferred_element_type=jnp.float32)
            * scale
        )
        value_part = jnp.einsum(
            "hqk,qhd->khd",
            weights.astype(jnp.bfloat16),
            grad_numer,
            preferred_element_type=jnp.float32,
        )
        block_terms = jnp.concatenate(
            [key_part.reshape(key_block_rows, width), value_part.reshape(key_block_rows, width)],
            axis=1,
        )
        return lax.dynamic_update_slice_in_dim(terms, block_terms, j * key_block_rows, 0)

    key_value_grad = lax.psum_scatter(
        lax.fori_loop(
            0,
            rows * lax.axis_size("ctx") // key_block_rows,
            key_block_grad,
            jnp.zeros((rows * lax.axis_size("ctx"), 2 * width), jnp.float32),
        ).astype(jnp.bfloat16),
        "ctx",
        scatter_dimension=0,
        tiled=True,
    ).astype(jnp.float32)
    grad_key = rotate(key_value_grad[:, :width].reshape(head_shape), query_turn, -1.0).reshape(
        rows, width
    )
    grad_query = rotate(grad_query, query_turn, -1.0).reshape(rows, width)
    grad_joint = jnp.concatenate(
        [
            grad_query.astype(jnp.bfloat16),
            grad_key.astype(jnp.bfloat16),
            key_value_grad[:, width:].astype(jnp.bfloat16),
            grad_gate.astype(jnp.bfloat16),
            grad_up.astype(jnp.bfloat16),
        ],
        axis=1,
    )
    grad_hidden = against_rows(grad_joint, lax.all_gather(in_weight, "fsdp", axis=0, tiled=True))
    grad_normed = grad_hidden * gain_full[None, :]
    grad_inputs = inverse_std * (
        grad_normed
        - jnp.mean(grad_normed, axis=1, keepdims=True)
        - normed * jnp.mean(grad_normed * normed, axis=1, keepdims=True)
    )
    grad_in = (grad_rows.astype(jnp.float32) + grad_inputs).astype(jnp.bfloat16)
    norm_terms = jnp.stack([jnp.sum(grad_hidden * normed, axis=0), jnp.sum(grad_hidden, axis=0)])
    norm_totals = lax.psum(norm_terms, ("ctx", "fsdp"))
    shards = lax.axis_size("fsdp")
    share = width // shards
    gain_grad = lax.dynamic_slice_in_dim(norm_totals[0], lax.axis_index("fsdp") * share, share, 0)
    bias_grad = lax.dynamic_slice_in_dim(norm_totals[1], lax.axis_index("fsdp") * share, share, 0)

    def column_terms(source, partner):
        return transposed_dot(source, partner)

    parts = lax.axis_size("ctx")

    def reorder(matrix):
        columns = matrix.shape[1]
        return (
            matrix.reshape(rows, shards, parts, columns // (shards * parts))
            .transpose(0, 2, 1, 3)
            .reshape(rows, columns)
        )

    in_piece = lax.psum_scatter(
        column_terms(reorder(hidden_in), grad_joint),
        ("ctx", "fsdp"),
        scatter_dimension=0,
        tiled=True,
    )
    out_piece = lax.psum_scatter(
        column_terms(reorder(mixed_in), grad_rows), ("ctx", "fsdp"), scatter_dimension=0, tiled=True
    )
    in_weight_grad, out_weight_grad = (
        lax.all_gather(in_piece.astype(jnp.bfloat16), "ctx", axis=0, tiled=True).astype(
            in_piece.dtype
        ),
        lax.all_gather(out_piece.astype(jnp.bfloat16), "ctx", axis=0, tiled=True).astype(
            out_piece.dtype
        ),
    )
    return (result[None], grad_in[None], in_weight_grad, out_weight_grad, gain_grad, bias_grad)


def flip(index, bit):
    return index + bit - 2 * bit * ((index // bit) % 2)


def ff_chunk(C, fb, cb):
    return fb * C + (cb % 2) * (C // 2) + cb // 2


class Copies:
    def __init__(self, sems):
        self.sems = sems
        self.used = 0
        self.open = []

    def send(self, src, dst, recv_sem, target, when=None):
        copy = pltpu.make_async_remote_copy(
            src_ref=src,
            dst_ref=dst,
            send_sem=self.sems.at[self.used],
            recv_sem=recv_sem,
            device_id=target,
            device_id_type=pl.DeviceIdType.MESH,
        )
        self.used += 1
        self.open.append((copy.wait_send, when, False))
        if when is None:
            copy.start()
        else:
            pl.when(when)(copy.start)

    def local(self, src, dst, when=None):
        copy = pltpu.make_async_copy(src, dst, self.sems.at[self.used])
        self.used += 1
        if when is None:
            copy.start()
        else:
            pl.when(when)(copy.start)
        self.open.append((copy.wait, when, True))

    def finish_local(self):
        self.finish([item for item in self.open if item[2]])
        self.open = [item for item in self.open if not item[2]]

    def finish(self, items=None):
        for done, when, _ in self.open if items is None else items:
            if when is None:
                done()
            else:
                pl.when(when)(done)


def arrived(ref, recv_sem):
    pltpu.make_async_copy(ref, ref, recv_sem).wait()


def owner_of_unit(unit, att_units, ff_units, heads):
    first = heads * att_units
    is_att = (unit < first).astype(jnp.int32) if hasattr(unit, "astype") else int(unit < first)
    return is_att * (unit // att_units) + (1 - is_att) * ((unit - first) // ff_units)


LOG2E = 1.4426950408889634
CHUNK = 512
QT = 256


class Stream:
    def __init__(self, count, source, buf, sems):
        self.count, self.source, self.buf, self.sems = count, source, buf, sems

    def copy(self, i):
        return pltpu.make_async_copy(self.source(i), self.buf.at[i % 2], self.sems.at[i % 2])

    def start(self):
        self.copy(0).start()

    def take(self, i):
        if not isinstance(i, int):
            pl.when(i + 1 < self.count)(lambda: self.copy(i + 1).start())
        elif i + 1 < self.count:
            self.copy(i + 1).start()
        self.copy(i).wait()
        return self.buf[i % 2]


def turn_pair(values, cosine, sine):
    half = ROT // 2
    first, second = values[:half], values[half:ROT]
    return jnp.concatenate(
        [first * cosine - second * sine, second * cosine + first * sine, values[ROT:]], axis=0
    )


def nt_dot(left, right):
    return lax.dot_general(left, right, (((1,), (1,)), ((), ())), preferred_element_type=F32)


def token_tables(row, batch, docs):
    index = lax.broadcasted_iota(jnp.int32, (1, batch), 1)
    place = index % BLOCK
    block = index // BLOCK
    for j in range(batch // BLOCK):
        place = place + jnp.where(block == j, row[:, docs + j : docs + j + 1] * BLOCK, 0)
    start = jnp.zeros((1, 1), jnp.int32)
    first = jnp.zeros((1, batch), jnp.int32)
    for j in range(docs):
        first = jnp.where(place >= start, start, first)
        start = start + row[:, j : j + 1]
    return place, place - first


def as_column(row):
    return jnp.broadcast_to(row, (8, row.shape[1])).T[:, :1]


def allowed_keys(place_col, place_row, turn_row):
    return (place_col <= place_row) & (place_col >= place_row - turn_row)


class Forward:
    def __init__(self, refs, batch, ff):
        self.r, self.batch, self.ff = refs, batch, ff

    def tables(self, b):
        r, batch = self.r, self.batch
        place, turn = token_tables(r["table"][b], batch, 4)
        r["place"][b] = place
        r["turn"][b] = turn
        pair = lax.broadcasted_iota(jnp.int32, (ROT // 2, 1), 0).astype(F32)
        freq = jnp.exp2(pair * (-2.0 * math.log2(10000.0) / ROT))
        angle = turn.astype(F32) * freq
        r["cos"][:, b * batch : (b + 1) * batch] = jnp.cos(angle)
        r["sin"][:, b * batch : (b + 1) * batch] = jnp.sin(angle)

    def project(self, i):
        r, ff = self.r, self.ff
        cols = slice(i * CHUNK, (i + 1) * CHUNK)
        hidden = r["hidden"].take(i).reshape(CHUNK, -1)
        joint = nt_dot(r["w_in"][...], hidden)
        cosine, sine = r["cos"][:, cols], r["sin"][:, cols]
        r["qkv"][:HEAD, cols] = turn_pair(joint[:HEAD], cosine, sine).astype(BF16)
        r["qkv"][HEAD : 2 * HEAD, cols] = turn_pair(joint[HEAD : 2 * HEAD], cosine, sine).astype(BF16)
        r["qkv"][2 * HEAD : 3 * HEAD, cols] = joint[2 * HEAD : 3 * HEAD].astype(BF16)
        slot = i % 2
        if i >= 2:
            self.gates(i - 2).wait()
        gate, upward = joint[3 * HEAD : 3 * HEAD + ff], joint[3 * HEAD + ff :]
        r["gate_buf"][slot, :ff] = gate
        r["gate_buf"][slot, ff:] = upward
        r["mixed"][HEAD:, cols] = (gate * jax.nn.sigmoid(gate) * upward).astype(BF16)
        self.gates(i).start()

    def gates(self, i):
        r = self.r
        return pltpu.make_async_copy(
            r["gate_buf"].at[i % 2], r["gates"].at[:, pl.ds(i * CHUNK, CHUNK)], r["gate_sems"].at[i % 2]
        )

    def attend(self, b):
        r, batch = self.r, self.batch
        r["key_rows"][...] = r["qkv"][HEAD : 2 * HEAD, b * batch : (b + 1) * batch].T
        r["place_col"][...] = as_column(r["place"][b])

        @pl.loop(0, batch // QT)
        def _(t):
            cols = pl.ds(pl.multiple_of(b * batch + t * QT, QT), QT)
            here = pl.ds(pl.multiple_of(t * QT, QT), QT)
            place, turn = r["place"][b, :, here], r["turn"][b, :, here]
            query = r["qkv"][:HEAD, cols]
            totals = jnp.zeros((1, QT), F32)
            numer = jnp.zeros((HEAD, QT), F32)
            for k in range(batch // QT):
                keys = slice(k * QT, (k + 1) * QT)
                weights = scores_of(r["key_rows"][keys], query, r["place_col"][keys], place, turn)
                totals = totals + jnp.sum(weights, axis=0, keepdims=True)
                value = r["qkv"][2 * HEAD :, b * batch + k * QT : b * batch + (k + 1) * QT]
                numer = numer + jnp.dot(value, weights.astype(BF16), preferred_element_type=F32)
            attended = numer / totals
            r["attended"][:, cols] = attended
            r["totals"][:, cols] = totals
            r["mixed"][:HEAD, cols] = attended.astype(BF16)


def forward_kernel(
    sizes, ff,
    x_ref, go_ref, gain_ref, bias_ref, table_ref, weight_ref, wout_ref,
    go_all, hid_all, win_all, wout_all, gain_buf,
    qkv, gates, mixed, attended, totals, place, turn, cosine, sine,
    table_all, bias_buf, hid_own, win_buf, win_ref, thin_buf, thick_buf, turn_buf, hidden_buf, gate_buf, key_rows, place_col,
    send_sems, block_sems, small_sems, win_sems, wout_sems, hidden_sems, gate_sems, load_sem, slice_sems,
):
    C, F = sizes
    c = lax.axis_index("ctx")
    f = lax.axis_index("fsdp")
    x_nbr, y_nbr, core = flip(c, 2), flip(c, 4), flip(c, 1)
    diag = flip(x_nbr, 4)
    copies = Copies(send_sems)
    here = {"ctx": c, "fsdp": f}

    def at_ctx(other):
        return {"ctx": other, "fsdp": f}

    def at_f(other):
        return {"ctx": c, "fsdp": other}

    width = x_ref.shape[1]
    total_cols = weight_ref.shape[1]
    segments = (
        (0, HEAD, 0), (width, HEAD, HEAD), (2 * width, HEAD, 2 * HEAD),
        (3 * width, ff, 3 * HEAD), (3 * width + FF, ff, 3 * HEAD + ff),
    )

    def cut(dest, k):
        base, size, row = segments[k]
        buf = thin_buf.at[dest, k] if k < 3 else thick_buf.at[dest, k - 3]
        wide = buf.shape[1]
        start = base + (dest * C + c if k < 3 else ff_chunk(C, dest, c)) * size
        first = jnp.minimum(start // 128 * 128, total_cols - wide)
        copy = pltpu.make_async_copy(
            weight_ref.at[:, pl.ds(pl.multiple_of(first, 128), wide)], buf, slice_sems.at[dest, k]
        )
        return copy, start - first, size, row, wide

    for dest in range(F):
        for k in range(len(segments)):
            cut(dest, k)[0].start()

    barrier = pltpu.get_barrier_semaphore()
    others = [lax.rem(f + s, F) for s in range(1, F)]
    for peer in [at_ctx(x_nbr), at_ctx(y_nbr), at_ctx(core)] + [at_f(o) for o in others]:
        pl.semaphore_signal(barrier, inc=1, device_id=peer, device_id_type=pl.DeviceIdType.MESH)
    pl.semaphore_wait(barrier, 3 + F - 1)

    for i, o in enumerate(others):
        copies.send(gain_ref, gain_buf.at[f], small_sems.at[0, f], at_f(o))
        copies.send(bias_ref, bias_buf.at[f], small_sems.at[1, f], at_f(o))
        copies.send(table_ref, table_all.at[f], small_sems.at[2, f], at_f(o))

    outs = (go_all, hid_all)
    rows = x_ref.shape[0]
    half = rows // 2

    def piece(a, fb, cb, part):
        ref = outs[a].at[fb, cb]
        if part is None:
            return ref
        return ref.at[pl.ds(part * half, half)]

    def forward(a, fb, cb, part, target, when=None, src=None):
        ref = piece(a, fb, cb, part)
        copies.send(ref if src is None else src, ref, block_sems.at[a, fb, cb, part or 0], target, when)

    def wait_block(a, fb, cb, part, when=None):
        def go():
            arrived(piece(a, fb, cb, part), block_sems.at[a, fb, cb, part or 0])
        if when is None:
            go()
        else:
            pl.when(when)(go)

    up, down = f + 1 < F, f > 0

    def own_xy(a, src):
        forward(a, f, c, None, at_ctx(x_nbr), src=src)
        forward(a, f, c, None, at_ctx(y_nbr), src=src)
        forward(a, f, c, None, at_ctx(core), src=src)

    def own_z(a, src):
        forward(a, f, c, None, at_f(f + 1), when=up, src=src)
        forward(a, f, c, None, at_f(f - 1), when=down, src=src)

    values = x_ref[...].astype(F32)
    centred = values - jnp.mean(values, axis=1, keepdims=True)
    normed = centred * lax.rsqrt(jnp.mean(centred * centred, axis=1, keepdims=True) + 1e-05)
    gain_buf[f] = gain_ref[...]
    bias_buf[f] = bias_ref[...]
    for o in others:
        arrived(gain_buf.at[o], small_sems.at[0, o])
        arrived(bias_buf.at[o], small_sems.at[1, o])
    share = gain_ref.shape[1]
    for s in range(F):
        cols = slice(s * share, (s + 1) * share)
        hid_own[:, cols] = (
            normed[:, cols] * gain_buf[s].astype(F32) + bias_buf[s].astype(F32)
        ).astype(BF16)
    own_z(1, hid_own)
    own_xy(1, hid_own)
    copies.local(hid_own, hid_all.at[f, c])
    copies.local(go_ref, go_all.at[f, c])

    share_rows = weight_ref.shape[0]

    def win_place(src_f):
        return win_all.at[:, pl.ds(pl.multiple_of(src_f * share_rows, share_rows), share_rows)]

    def win_send(shift):
        o = lax.rem(f + shift, F)
        copies.send(win_ref.at[o], win_place(f), win_sems.at[f], at_f(o))

    def win_wait(shift):
        o = lax.rem(f + F - shift, F)
        arrived(win_place(o), win_sems.at[o])

    def slice_weights():
        for k in range(len(segments)):
            @pl.loop(0, F)
            def _(dest):
                copy, shift, size, row, wide = cut(dest, k)
                copy.wait()
                buf = thin_buf.at[dest, k] if k < 3 else thick_buf.at[dest, k - 3]
                turn_buf[:wide] = buf[...].T
                win_ref[dest, row : row + size] = turn_buf[pl.ds(pl.multiple_of(shift, UNIT), size)]

        copies.local(win_ref.at[f], win_place(f))

    units_per_shard = wout_ref.shape[0] // UNIT
    att_units, ff_units = HEAD // UNIT * (HEADS // (C * F)), FF // (C * F) // UNIT

    def unit_of(dest, i):
        if i < att_units:
            return (dest * C + c) * att_units + i
        return C * F * att_units + ff_chunk(C, dest, c) * ff_units + (i - att_units)

    def unit_rows(ref, unit):
        return ref.at[pl.ds(pl.multiple_of(unit * UNIT, UNIT), UNIT)]

    def wout_sends():
        for step in range(F):
            dest = lax.rem(f + step, F)
            for i in range(att_units + ff_units):
                unit = unit_of(dest, i)
                mine = unit // units_per_shard == f
                src = unit_rows(wout_ref, lax.rem(unit, units_per_shard))
                dst = wout_all.at[pl.ds(i * UNIT, UNIT)]
                if step == 0:
                    copy = pltpu.make_async_copy(src, dst, wout_sems.at[i])
                    pl.when(mine)(copy.start)
                else:
                    copies.send(src, dst, wout_sems.at[i], at_f(dest), when=mine)

    def blocks_of(s):
        if s == 0:
            return [(-1, f, None)]
        return [(-1, f - s, f - s >= 0), (1, f + s, f + s < F)]

    def z_step(a, s):
        for sign, fb, valid in blocks_of(s):
            onward = valid & (up if sign < 0 else down)
            wait_block(a, fb, c, None, when=valid)
            forward(a, fb, c, None, at_f(f - sign), when=onward)
            for target in (x_nbr, y_nbr, core):
                forward(a, fb, c, None, at_ctx(target), when=valid)

    def xy_step(a, s):
        for _, fb, valid in blocks_of(s):
            wait_block(a, fb, x_nbr, None, when=valid)
            forward(a, fb, x_nbr, 0, at_ctx(y_nbr), when=valid)
            forward(a, fb, x_nbr, None, at_ctx(core), when=valid)
            wait_block(a, fb, y_nbr, None, when=valid)
            forward(a, fb, y_nbr, 1, at_ctx(x_nbr), when=valid)
            forward(a, fb, y_nbr, None, at_ctx(core), when=valid)

    def diag_step(a, s):
        for _, fb, valid in blocks_of(s):
            for part in (0, 1):
                wait_block(a, fb, diag, part, when=valid)
                forward(a, fb, diag, part, at_ctx(core), when=valid)

    def from_core(a):
        for fb in range(F):
            wait_block(a, fb, core, None)
            wait_block(a, fb, flip(core, 2), None)
            wait_block(a, fb, flip(core, 4), None)
            for part in (0, 1):
                wait_block(a, fb, flip(flip(core, 2), 4), part)

    batch = C * rows
    refs = dict(
        table=table_all, place=place, turn=turn, cos=cosine, sin=sine, w_in=win_buf, qkv=qkv,
        gates=gates, gate_buf=gate_buf, gate_sems=gate_sems, mixed=mixed, attended=attended,
        totals=totals, key_rows=key_rows, place_col=place_col,
        hidden=Stream(
            F * batch // CHUNK,
            lambda i: hid_all.at[
                i * CHUNK // batch, pl.ds(i * CHUNK % batch // rows, CHUNK // rows)
            ],
            hidden_buf, hidden_sems,
        ),
    )
    work = Forward(refs, batch, ff)

    for o in others:
        arrived(table_all.at[o], small_sems.at[2, o])
    table_all[f] = table_ref[...]
    for b in range(F):
        work.tables(b)
    slice_weights()

    z_step(1, 1)
    xy_step(1, 0)
    z_step(1, 2)
    win_send(1)
    xy_step(1, 1)
    diag_step(1, 0)
    z_step(1, 3)
    win_send(2)
    xy_step(1, 2)
    diag_step(1, 1)
    own_z(0, go_ref)
    xy_step(1, 3)
    own_xy(0, go_ref)
    win_wait(1)
    win_wait(2)
    win_send(3)
    diag_step(1, 2)
    diag_step(1, 3)
    z_step(0, 1)
    xy_step(0, 0)
    from_core(1)
    copies.finish_local()
    refs["hidden"].start()
    win_wait(3)
    load = pltpu.make_async_copy(win_all, win_buf, load_sem)
    load.start()
    wout_sends()
    load.wait()

    pieces = []
    for b in range(F):
        for i in range(batch // CHUNK):
            pieces.append(functools.partial(work.project, b * (batch // CHUNK) + i))
        pieces.append(functools.partial(work.attend, b))
    steps = [
        functools.partial(z_step, 0, 2),
        functools.partial(xy_step, 0, 1),
        functools.partial(diag_step, 0, 0),
        functools.partial(z_step, 0, 3),
        functools.partial(xy_step, 0, 2),
        functools.partial(diag_step, 0, 1),
        functools.partial(xy_step, 0, 3),
        functools.partial(diag_step, 0, 2),
        functools.partial(diag_step, 0, 3),
    ]
    weave(steps, pieces)
    from_core(0)
    for i in range(att_units + ff_units):
        arrived(wout_all.at[pl.ds(i * UNIT, UNIT)], wout_sems.at[i])
    last = F * batch // CHUNK
    work.gates(last - 2).wait()
    work.gates(last - 1).wait()
    copies.finish()


def weave(steps, pieces):
    done = 0
    for i, step in enumerate(steps):
        until = (i + 1) * len(pieces) // len(steps)
        for piece in pieces[done:until]:
            piece()
        done = until
        step()


def forward_all(x, go, gain, bias, table, in_weight, wout, C, F):
    rows, width = x.shape
    shard = in_weight.shape[0]
    any_ = pl.BlockSpec(memory_space=pl.ANY)
    vmem = pl.BlockSpec(memory_space=pltpu.VMEM)
    ff = FF // (C * F)
    wout_rows = HEAD * HEADS // (C * F) + ff
    per_rank = 3 * HEAD + 2 * ff
    share = gain.shape[1]
    batch = C * rows
    tokens = F * batch
    shape = jax.ShapeDtypeStruct
    return pl.pallas_call(
        functools.partial(forward_kernel, (C, F), ff),
        out_shape=(
            shape((F, C, rows, width), BF16),
            shape((F, C, rows, width), BF16),
            shape((per_rank, width), BF16),
            shape((wout_rows, width), BF16),
            shape((F, 1, share), BF16),
            shape((3 * HEAD, tokens), BF16),
            shape((2 * ff, tokens), F32),
            shape((HEAD + ff, tokens), BF16),
            shape((HEAD, tokens), F32),
            shape((1, tokens), F32),
            shape((F, 1, batch), jnp.int32),
            shape((F, 1, batch), jnp.int32),
            shape((ROT // 2, tokens), F32),
            shape((ROT // 2, tokens), F32),
        ),
        in_specs=[vmem, any_, vmem, vmem, vmem, any_, any_],
        out_specs=(any_,) * 4 + (vmem, vmem, any_) + (vmem,) * 7,
        scratch_shapes=[
            pltpu.VMEM((F,) + table.shape, jnp.int32),
            pltpu.VMEM((F, 1, share), BF16),
            pltpu.VMEM((rows, width), BF16),
            pltpu.VMEM((per_rank, width), BF16),
            pltpu.VMEM((F, per_rank, shard), BF16),
            pltpu.VMEM((F, 3, shard, 128), BF16),
            pltpu.VMEM((F, 2, shard, 384), BF16),
            pltpu.VMEM((384, shard), BF16),
            pltpu.VMEM((2, CHUNK // rows, rows, width), BF16),
            pltpu.VMEM((2, 2 * ff, CHUNK), F32),
            pltpu.VMEM((batch, HEAD), BF16),
            pltpu.VMEM((batch, 1), jnp.int32),
            pltpu.SemaphoreType.DMA((256,)),
            pltpu.SemaphoreType.DMA((2, F, C, 2)),
            pltpu.SemaphoreType.DMA((3, F)),
            pltpu.SemaphoreType.DMA((F,)),
            pltpu.SemaphoreType.DMA((wout_rows // UNIT,)),
            pltpu.SemaphoreType.DMA((2,)),
            pltpu.SemaphoreType.DMA((2,)),
            pltpu.SemaphoreType.DMA,
            pltpu.SemaphoreType.DMA((F, 5)),
        ],
        compiler_params=pltpu.CompilerParams(
            collective_id=1, has_side_effects=True, vmem_limit_bytes=56 * 1024 * 1024
        ),
    )(x, go, gain, bias, table, in_weight, wout)


def scores_of(key_rows, query, place_col, place, turn):
    scores = jnp.dot(key_rows, query, preferred_element_type=F32)
    ok = allowed_keys(place_col, place, turn)
    return jnp.where(ok, jnp.exp2(scores * (LOG2E * HEAD**-0.5)), 0.0)


class Backward:
    def __init__(self, refs, batch, ff):
        self.r, self.batch, self.ff = refs, batch, ff

    def mixed(self, i):
        r, ff = self.r, self.ff
        cols = slice(i * CHUNK, (i + 1) * CHUNK)
        grads = r["grads"].take(i).reshape(CHUNK, -1)
        grad = nt_dot(r["w_out"][...], grads)
        gates = r["gates"].take(i)
        grad_att = grad[:HEAD].astype(BF16).astype(F32)
        inverse = 1.0 / r["totals"][:, cols]
        delta = jnp.sum(grad_att * r["attended"][:, cols], axis=0, keepdims=True)
        r["ratio"][:, cols] = delta * inverse
        r["numer"][:, cols] = (grad_att * inverse).astype(BF16)
        grad_act = grad[HEAD:].astype(BF16).astype(F32)
        gate, upward = gates[:ff], gates[ff:]
        sig = jax.nn.sigmoid(gate)
        r["joint"][3 * HEAD : 3 * HEAD + ff, cols] = (
            grad_act * upward * sig * (1.0 + gate * (1.0 - sig))
        ).astype(BF16)
        r["joint"][3 * HEAD + ff :, cols] = (grad_act * gate * sig).astype(BF16)

    def attend(self, b):
        r, batch = self.r, self.batch
        whole = slice(b * batch, (b + 1) * batch)
        scale = HEAD**-0.5
        r["key_rows"][...] = r["qkv"][HEAD : 2 * HEAD, whole].T
        r["value_rows"][...] = r["qkv"][2 * HEAD :, whole].T
        r["place_col"][...] = as_column(r["place"][b])
        r["grad_k"][...] = jnp.zeros_like(r["grad_k"])
        r["grad_v"][...] = jnp.zeros_like(r["grad_v"])

        @pl.loop(0, batch // QT)
        def _(t):
            cols = pl.ds(pl.multiple_of(b * batch + t * QT, QT), QT)
            here = pl.ds(pl.multiple_of(t * QT, QT), QT)
            place, turn = r["place"][b, :, here], r["turn"][b, :, here]
            query, numer, ratio = r["qkv"][:HEAD, cols], r["numer"][:, cols], r["ratio"][:, cols]
            grad_q = jnp.zeros((HEAD, QT), F32)
            for k in range(batch // QT):
                keys = slice(k * QT, (k + 1) * QT)
                key_cols = slice(b * batch + k * QT, b * batch + (k + 1) * QT)
                weights = scores_of(r["key_rows"][keys], query, r["place_col"][keys], place, turn)
                pushed = jnp.dot(r["value_rows"][keys], numer, preferred_element_type=F32)
                grad_scores = (weights * (pushed - ratio)).astype(BF16)
                grad_q = grad_q + jnp.dot(
                    r["qkv"][HEAD : 2 * HEAD, key_cols], grad_scores, preferred_element_type=F32
                )
                r["grad_k"][:, keys] += nt_dot(query, grad_scores)
                r["grad_v"][:, keys] += nt_dot(numer, weights.astype(BF16))
            r["joint"][:HEAD, cols] = turn_pair(
                grad_q * scale, r["cos"][:, cols], -r["sin"][:, cols]
            ).astype(BF16)

        r["joint"][HEAD : 2 * HEAD, whole] = turn_pair(
            r["grad_k"][...] * scale, r["cos"][:, whole], -r["sin"][:, whole]
        ).astype(BF16)
        r["joint"][2 * HEAD : 3 * HEAD, whole] = r["grad_v"][...].astype(BF16)


class Reduce:
    def __init__(self, sizes, pairs, rows, width, parts, bufs, sems):
        self.C, self.F = sizes
        self.pairs, self.rows, self.width, self.parts = pairs, rows, width // parts, parts
        self.c = lax.axis_index("ctx")
        self.f = lax.axis_index("fsdp")
        self.x_nbr, self.y_nbr, self.core = flip(self.c, 2), flip(self.c, 4), flip(self.c, 1)
        (
            self.core_send, self.core_recv, self.x_send, self.y_send, self.x_recv, self.y_recv,
            self.keep_l, self.keep_r, self.y2_send, self.x2_send, self.y2_recv, self.x2_recv,
            self.z_send, self.z_recv, self.turned,
        ) = bufs
        self.send_sems, self.core_sems, self.xy_sems, self.xy2_sems, self.z_sems = sems
        self.open = {}
        self.others = [lax.rem(self.f + s, self.F) for s in range(1, self.F)]
        self.steps = len(pairs) * self.F * parts

    def at_ctx(self, other):
        return {"ctx": other, "fsdp": self.f}

    def at_f(self, other):
        return {"ctx": self.c, "fsdp": other}

    def greet(self):
        barrier = pltpu.get_barrier_semaphore()
        peers = [self.at_ctx(o) for o in (self.x_nbr, self.y_nbr, self.core)]
        peers += [self.at_f(o) for o in self.others]
        for peer in peers:
            pl.semaphore_signal(
                barrier, inc=1, device_id=peer, device_id_type=pl.DeviceIdType.MESH
            )
        pl.semaphore_wait(barrier, len(peers))

    def send(self, key, t, src, dst, recv_sem, target):
        copy = pltpu.make_async_remote_copy(
            src_ref=src, dst_ref=dst, send_sem=self.send_sems.at[key, t], recv_sem=recv_sem,
            device_id=target, device_id_type=pl.DeviceIdType.MESH,
        )
        copy.start()
        self.open[key, t] = copy

    def sent(self, key, t):
        if (key, t) in self.open:
            self.open.pop((key, t)).wait_send()

    def place(self, t):
        return t // (self.F * self.parts), t // self.parts % self.F, t % self.parts

    def dest(self, i):
        return lax.rem(self.f + 1 + i, self.F)

    def turn(self, t):
        pair, i, _ = self.place(t)
        left_ref = self.pairs[pair][0]
        size = left_ref.shape[0]
        rows = self.rows
        block = self.dest(i) * self.C
        for slot, base in enumerate((self.core, self.c)):
            parts = [
                left_ref[:, pl.ds(pl.multiple_of((block + cc) * rows, rows), rows)]
                for cc in (base, flip(base, 2), flip(base, 4), flip(flip(base, 2), 4))
            ]
            self.turned[slot, :, :size] = jnp.concatenate(parts, axis=1).T

    def enter(self, t, tile=512):
        pair, i, part = self.place(t)
        w_ref = self.pairs[pair][1]
        size = w_ref.shape[0]
        rows, mid = self.rows, self.width // 2
        if part == 0:
            self.turn(t)
        self.sent(0, t - 2)
        left = self.turned[0, :, :size]
        for n in range(self.width // tile):
            cols = slice(part * self.width + n * tile, part * self.width + (n + 1) * tile)
            self.core_send[t % 2, :, n * tile : (n + 1) * tile] = jnp.dot(
                left, w_ref[:, cols], preferred_element_type=F32
            ).astype(BF16)
        self.send(
            0, t, self.core_send.at[t % 2], self.core_recv.at[t % 2], self.core_sems.at[t],
            self.at_ctx(self.core),
        )
        left = self.turned[1, :, :size]
        sums = []
        for side in range(2):
            cols = slice(part * self.width + side * mid, part * self.width + (side + 1) * mid)
            sums.append(jnp.dot(left, w_ref[:, cols], preferred_element_type=F32))
        arrived(self.core_recv.at[t % 2], self.core_sems.at[t])
        for key, keep, out, recv, kept, sent_rows, target in (
            (1, self.keep_l, self.x_send, self.x_recv, (0, 2), (1, 3), self.x_nbr),
            (2, self.keep_r, self.y_send, self.y_recv, (0, 1), (2, 3), self.y_nbr),
        ):
            self.sent(key, t - 2)
            total = sums[key - 1] + self.core_recv[t % 2, :, (key - 1) * mid : key * mid].astype(F32)
            for i, b in enumerate(sent_rows):
                out[t % 2, i * rows : (i + 1) * rows] = total[b * rows : (b + 1) * rows].astype(BF16)
            self.send(
                key, t, out.at[t % 2], recv.at[t % 3], self.xy_sems.at[key - 1, t], self.at_ctx(target)
            )
            for i, b in enumerate(kept):
                keep[t % 3, i * rows : (i + 1) * rows] = total[b * rows : (b + 1) * rows]

    def second(self, t):
        rows, slot = self.rows, t % 3
        sides = (
            (3, self.keep_l, self.x_recv, self.y2_send, self.y2_recv, self.y_nbr),
            (4, self.keep_r, self.y_recv, self.x2_send, self.x2_recv, self.x_nbr),
        )
        for key, keep, recv, out, _, _ in sides:
            arrived(recv.at[slot], self.xy_sems.at[key - 3, t])
            self.sent(key, t - 2)
            out[t % 2] = (keep[slot, rows:] + recv[slot, rows:].astype(F32)).astype(BF16)
            keep[slot, :rows] = keep[slot, :rows] + recv[slot, :rows].astype(F32)
        for key, _, _, out, out_recv, target in sides:
            self.send(
                key, t, out.at[t % 2], out_recv.at[slot], self.xy2_sems.at[key - 3, t],
                self.at_ctx(target),
            )

    def third(self, t):
        pair, i, part = self.place(t)
        rows, mid, slot = self.rows, self.width // 2, t % 3
        arrived(self.y2_recv.at[slot], self.xy2_sems.at[0, t])
        arrived(self.x2_recv.at[slot], self.xy2_sems.at[1, t])
        total_l = self.keep_l[slot, :rows] + self.y2_recv[slot].astype(F32)
        total_r = self.keep_r[slot, :rows] + self.x2_recv[slot].astype(F32)
        if i < self.F - 1:
            for key, u in list(self.open):
                if key == 5 and u % 2 == t % 2:
                    self.sent(key, u)
            self.z_send[t % 2, :, :mid] = total_l.astype(BF16)
            self.z_send[t % 2, :, mid:] = total_r.astype(BF16)
            self.send(
                5, t, self.z_send.at[t % 2], self.z_recv.at[pair, part, self.f],
                self.z_sems.at[pair, part, self.f], self.at_f(self.dest(i)),
            )
            return None
        total = jnp.concatenate([total_l, total_r], axis=1)
        for o in self.others:
            arrived(self.z_recv.at[pair, part, o], self.z_sems.at[pair, part, o])
            total = total + self.z_recv[pair, part, o].astype(F32)
        return total

    def run(self, fill):
        sums = []
        self.enter(0)
        self.enter(1)
        for t in range(self.steps):
            fill(t)
            self.second(t)
            if t >= 1:
                sums.append(self.third(t - 1))
            if t + 2 < self.steps:
                self.enter(t + 2)
        fill(self.steps)
        sums.append(self.third(self.steps - 1))
        return sums

    def finish(self):
        for key, t in list(self.open):
            self.sent(key, t)


def reduce_scratch(F, rows, width, parts, pairs, features):
    width = width // parts
    mid = width // 2
    steps = pairs * F * parts
    return [
        pltpu.VMEM((2, 4 * rows, width), BF16),
        pltpu.VMEM((2, 4 * rows, width), BF16),
        pltpu.VMEM((2, 2 * rows, mid), BF16),
        pltpu.VMEM((2, 2 * rows, mid), BF16),
        pltpu.VMEM((3, 2 * rows, mid), BF16),
        pltpu.VMEM((3, 2 * rows, mid), BF16),
        pltpu.VMEM((3, 2 * rows, mid), F32),
        pltpu.VMEM((3, 2 * rows, mid), F32),
        pltpu.VMEM((2, rows, mid), BF16),
        pltpu.VMEM((2, rows, mid), BF16),
        pltpu.VMEM((3, rows, mid), BF16),
        pltpu.VMEM((3, rows, mid), BF16),
        pltpu.VMEM((2, rows, width), BF16),
        pltpu.VMEM((pairs, parts, F, rows, width), BF16),
        pltpu.VMEM((2, 4 * rows, features), BF16),
        pltpu.SemaphoreType.DMA((6, steps)),
        pltpu.SemaphoreType.DMA((steps,)),
        pltpu.SemaphoreType.DMA((2, steps)),
        pltpu.SemaphoreType.DMA((2, steps)),
        pltpu.SemaphoreType.DMA((pairs, parts, F)),
    ]


PIECES = ((0, 4), (4, 1), (5, 1), (6, 9))


class Spread:
    def __init__(self, sizes, shard_units, win_ref, wout_ref, win_all, wout_all, copies, block_sems, piece_sems):
        self.C, self.F = sizes
        self.shard_units = shard_units
        self.win_ref, self.wout_ref, self.win_all, self.wout_all = win_ref, wout_ref, win_all, wout_all
        self.copies, self.block_sems, self.piece_sems = copies, block_sems, piece_sems
        self.c = lax.axis_index("ctx")
        self.f = lax.axis_index("fsdp")
        self.x_nbr, self.y_nbr, self.core = flip(self.c, 2), flip(self.c, 4), flip(self.c, 1)
        self.diag = flip(self.x_nbr, 4)
        self.share = win_all.shape[3]
        self.half = win_all.shape[2] // 2
        self.near = (self.x_nbr, self.y_nbr, self.core)

    def at_ctx(self, other):
        return {"ctx": other, "fsdp": self.f}

    def at_f(self, other):
        return {"ctx": self.c, "fsdp": other}

    def win_slice(self, dest):
        return self.win_ref.at[:, pl.ds(pl.multiple_of(dest * self.share, self.share), self.share)]

    def block(self, fb, cb, part):
        ref = self.win_all.at[fb, cb]
        return ref if part is None else ref.at[pl.ds(part * self.half, self.half)]

    def pass_block(self, fb, cb, part, target, src=None):
        ref = self.block(fb, cb, part)
        sem = self.block_sems.at[fb, cb, part or 0]
        self.copies.send(ref if src is None else src, ref, sem, target)

    def wait_block(self, fb, cb, part):
        arrived(self.block(fb, cb, part), self.block_sems.at[fb, cb, part or 0])

    def piece(self, fb, cb, p):
        att_units, ff_units = PIECES[0][1], sum(n for _, n in PIECES[1:])
        start, units = PIECES[p]
        if p == 0:
            unit = (fb * self.C + cb) * att_units
        else:
            chunk = ff_chunk(self.C, fb, cb)
            unit = self.C * self.F * att_units + chunk * ff_units + (start - att_units)
        place = pl.multiple_of(lax.rem(unit, self.shard_units) * UNIT, UNIT)
        return unit // self.shard_units, self.wout_all.at[pl.ds(place, units * UNIT)]

    def own_piece(self, p):
        start, units = PIECES[p]
        return self.wout_ref.at[pl.ds(start * UNIT, units * UNIT)]

    def pass_piece(self, fb, cb, p, target, when, src=None):
        ref = self.piece(fb, cb, p)[1]
        self.copies.send(ref if src is None else src, ref, self.piece_sems.at[fb, cb, p], target, when)

    def wait_piece(self, fb, cb, p, when):
        def go():
            arrived(self.piece(fb, cb, p)[1], self.piece_sems.at[fb, cb, p])
        pl.when(when)(go)

    def z_send(self, shift):
        f, c = self.f, self.c
        o = lax.rem(f + shift, self.F)
        self.copies.send(
            self.win_slice(o), self.block(f, c, None), self.block_sems.at[f, c, 0], self.at_f(o)
        )
        for p in range(len(PIECES)):
            self.pass_piece(f, c, p, self.at_f(o), self.piece(f, c, p)[0] == o, src=self.own_piece(p))

    def own(self):
        f, c = self.f, self.c
        mine = self.win_slice(f)
        for target in self.near:
            self.pass_block(f, c, None, self.at_ctx(target), src=mine)
        self.copies.local(mine, self.block(f, c, None))
        for p in range(len(PIECES)):
            shard, place = self.piece(f, c, p)
            for target in self.near:
                self.pass_piece(f, c, p, self.at_ctx(target), shard == f, src=self.own_piece(p))
            self.copies.local(self.own_piece(p), place, shard == f)

    def z_step(self, fb):
        f, c = self.f, self.c
        self.wait_block(fb, c, None)
        for target in self.near:
            self.pass_block(fb, c, None, self.at_ctx(target))
        for p in range(len(PIECES)):
            here = self.piece(fb, c, p)[0] == f
            self.wait_piece(fb, c, p, here)
            for target in self.near:
                self.pass_piece(fb, c, p, self.at_ctx(target), here)

    def xy_step(self, fb, way):
        x_nbr, y_nbr, core = self.near
        self.wait_block(fb, x_nbr, None)
        self.pass_block(fb, x_nbr, 0, self.at_ctx(y_nbr))
        self.pass_block(fb, x_nbr, None, self.at_ctx(core))
        self.wait_block(fb, y_nbr, None)
        self.pass_block(fb, y_nbr, 1, self.at_ctx(x_nbr))
        self.pass_block(fb, y_nbr, None, self.at_ctx(core))
        for p in range(len(PIECES)):
            by_x = (p < 2) == (way == 0)
            for source, onward, turn in ((x_nbr, y_nbr, by_x), (y_nbr, x_nbr, not by_x)):
                here = self.piece(fb, source, p)[0] == self.f
                self.wait_piece(fb, source, p, here)
                if turn:
                    self.pass_piece(fb, source, p, self.at_ctx(onward), here)
                self.pass_piece(fb, source, p, self.at_ctx(core), here)

    def diag_step(self, fb):
        diag, core = self.diag, self.core
        for part in (0, 1):
            self.wait_block(fb, diag, part)
            self.pass_block(fb, diag, part, self.at_ctx(core))
        for p in range(len(PIECES)):
            here = self.piece(fb, diag, p)[0] == self.f
            self.wait_piece(fb, diag, p, here)
            self.pass_piece(fb, diag, p, self.at_ctx(core), here)

    def rest(self, terms, sums):
        F, f = self.F, self.f
        order = [f] + [lax.rem(f + F - s, F) for s in range(1, F)]
        terms.step(0)
        for s in range(F + 2):
            if s + 1 < F:
                self.z_step(order[s + 1])
                if s + 2 < F:
                    self.z_send(s + 2)
            if s < 3:
                terms.step(s + 1)
            if s < F:
                self.xy_step(order[s], s % 2)
            if 0 <= s - 1 < F:
                self.diag_step(order[s - 1])
        core = self.core
        beyond = (core, flip(core, 2), flip(core, 4))
        corner = flip(flip(core, 2), 4)
        for fb in range(F):
            for cb in beyond:
                self.wait_block(fb, cb, None)
            for part in (0, 1):
                self.wait_block(fb, corner, part)
            for cb in beyond + (corner,):
                for p in range(len(PIECES)):
                    self.wait_piece(fb, cb, p, self.piece(fb, cb, p)[0] == f)
        sums[...] = terms.finish()
        self.copies.finish()


class Terms:
    def __init__(self, spread, value, bufs, sems):
        self.spread, self.value, self.bufs, self.sems = spread, value, bufs, sems
        self.others = [lax.rem(spread.f + s, spread.F) for s in range(1, spread.F)]

    def step(self, i):
        spread = self.spread
        near, parts, shares = self.bufs
        x_nbr, y_nbr, core = spread.near
        if i > 0:
            arrived(near.at[i - 1], self.sems.at[i - 1])
            self.value = self.value + near[i - 1]
        if i < 3:
            parts[i] = self.value
            target = spread.at_ctx((core, x_nbr, y_nbr)[i])
            spread.copies.send(parts.at[i], near.at[i], self.sems.at[i], target)
            return
        share = spread.share
        for s in range(spread.F):
            parts[3 + s, :, :share] = self.value[:, s * share : (s + 1) * share]
        for o in self.others:
            spread.copies.send(
                parts.at[3 + o, :, pl.ds(0, share)], shares.at[spread.f], self.sems.at[3 + spread.f],
                spread.at_f(o),
            )

    def finish(self):
        _, parts, shares = self.bufs
        f, share = self.spread.f, self.spread.share
        shares[f] = parts[3 + f, :, :share]
        for o in self.others:
            arrived(shares.at[o], self.sems.at[3 + o])
        total = shares[0]
        for s in range(1, self.spread.F):
            total = total + shares[s]
        return total


SLAB = 256
PARTS = 2


def backward_kernel(
    sizes, ff, shard_units,
    mixed_ref, w_out_ref, w_in_ref, x_ref, go_ref, gain_ref, qkv, attended, totals, place, turn, cosine,
    sine, hid_all, go_all, gates,
    result_ref, grad_in_ref, sums_ref, win_all, wout_all,
    go_buf, slab_buf, gate_buf, numer, ratio, key_rows, value_rows, place_col, grad_k, grad_v, joint, dw_in, dw_out,
    near_terms, part_terms, share_terms,
    go_sems, slab_sems, gate_sems, send_sems, block_sems, piece_sems, term_sems, *shared,
):
    C, F = sizes
    rows, width = x_ref.shape
    batch = C * rows
    reduce = Reduce(
        sizes, ((mixed_ref, w_out_ref), (joint, w_in_ref)), rows, width, PARTS, shared[:15], shared[15:]
    )
    count = F * batch // CHUNK
    slabs = width // SLAB
    wide = Stream(
        count,
        lambda i: go_all.at[i * CHUNK // batch, pl.ds(i * CHUNK % batch // rows, CHUNK // rows)],
        go_buf, go_sems,
    )
    refs = dict(
        grads=wide,
        gates=Stream(count, lambda i: gates.at[:, pl.ds(i * CHUNK, CHUNK)], gate_buf, gate_sems),
        w_out=w_out_ref, totals=totals, attended=attended, ratio=ratio, numer=numer, joint=joint,
        qkv=qkv, key_rows=key_rows, value_rows=value_rows, place_col=place_col, place=place,
        turn=turn, grad_k=grad_k, grad_v=grad_v, cos=cosine, sin=sine,
    )
    refs["grads"].start()
    refs["gates"].start()
    work = Backward(refs, batch, ff)
    pieces = []
    for b in range(F):
        for i in range(batch // CHUNK):
            pieces.append(functools.partial(work.mixed, b * (batch // CHUNK) + i))
        pieces.append(functools.partial(work.attend, b))

    def weight_grad(source, left, out, start, stop):
        stream = Stream(
            slabs,
            lambda i: source.at[:, :, :, pl.ds(pl.multiple_of(i * SLAB, SLAB), SLAB)],
            slab_buf, slab_sems,
        )
        if start == 0:
            stream.start()

        @pl.loop(start, stop)
        def _(i):
            slab = stream.take(i).reshape(C * F * rows, SLAB)
            out[:, pl.ds(pl.multiple_of(i * SLAB, SLAB), SLAB)] = jnp.dot(
                left[...], slab, preferred_element_type=F32
            ).astype(BF16)

    spread = Spread(
        sizes, shard_units, dw_in, dw_out, win_all, wout_all, Copies(send_sems), block_sems, piece_sems
    )
    grads = [
        functools.partial(weight_grad, *operands, i, i + 2)
        for operands in ((hid_all, joint, dw_in), (go_all, mixed_ref, dw_out))
        for i in range(0, slabs, 2)
    ]
    half = reduce.steps // 2
    before = half - 1

    def fill(t):
        if t < before:
            todo = pieces[t * len(pieces) // before : (t + 1) * len(pieces) // before]
        else:
            gaps = half - 1
            k = t - before
            todo = grads[k * len(grads) // gaps : (k + 1) * len(grads) // gaps] if k < gaps else []
        for piece in todo:
            piece()
        if t == reduce.steps - 1:
            spread.z_send(1)

    reduce.greet()
    sums = [part for part in reduce.run(fill) if part is not None]
    spread.own()
    total = jnp.concatenate(sums[:PARTS], axis=1)
    values = x_ref[...].astype(F32)
    result_ref[...] = (values + total).astype(BF16)
    total = jnp.concatenate(sums[PARTS:], axis=1)
    centred = values - jnp.mean(values, axis=1, keepdims=True)
    inverse_std = lax.rsqrt(jnp.mean(centred * centred, axis=1, keepdims=True) + 1e-05)
    normed = centred * inverse_std
    gain = jnp.concatenate([gain_ref[s].astype(F32) for s in range(F)], axis=1)
    g = total * gain
    back = inverse_std * (
        g - jnp.mean(g, axis=1, keepdims=True) - normed * jnp.mean(g * normed, axis=1, keepdims=True)
    )
    grad_in_ref[...] = (go_ref[...].astype(F32) + back).astype(BF16)
    terms = jnp.concatenate(
        [jnp.sum(total * normed, axis=0, keepdims=True), jnp.sum(total, axis=0, keepdims=True)], axis=0
    )
    reduce.finish()
    spread.rest(Terms(spread, terms, (near_terms, part_terms, share_terms), term_sems), sums_ref)


def backward_all(
    mixed, w_out, w_in, x, go, gains, qkv, attended, totals, place, turn, cosine, sine, hid_all, go_all, gates,
    shard_rows, C, F,
):
    rows, width = x.shape
    ff = gates.shape[0] // 2
    batch, tokens = C * rows, C * F * rows
    per_rank, share = w_in.shape[0], width // F
    vmem = pl.BlockSpec(memory_space=pltpu.VMEM)
    any_ = pl.BlockSpec(memory_space=pl.ANY)
    shape = jax.ShapeDtypeStruct
    dma = pltpu.SemaphoreType.DMA
    return pl.pallas_call(
        functools.partial(backward_kernel, (C, F), ff, shard_rows // UNIT),
        out_shape=(
            shape((rows, width), BF16),
            shape((rows, width), BF16),
            shape((2, share), F32),
            shape((F, C, per_rank, share), BF16),
            shape((shard_rows, width), BF16),
        ),
        in_specs=[vmem] * 13 + [any_] * 3,
        out_specs=(vmem,) * 3 + (any_,) * 2,
        scratch_shapes=[
            pltpu.VMEM((2, CHUNK // rows, rows, width), BF16),
            pltpu.VMEM((2, F, C, rows, SLAB), BF16),
            pltpu.VMEM((2, 2 * ff, CHUNK), F32),
            pltpu.VMEM((HEAD, tokens), BF16),
            pltpu.VMEM((1, tokens), F32),
            pltpu.VMEM((batch, HEAD), BF16),
            pltpu.VMEM((batch, HEAD), BF16),
            pltpu.VMEM((batch, 1), jnp.int32),
            pltpu.VMEM((HEAD, batch), F32),
            pltpu.VMEM((HEAD, batch), F32),
            pltpu.VMEM((per_rank, tokens), BF16),
            pltpu.VMEM((per_rank, width), BF16),
            pltpu.VMEM(w_out.shape, BF16),
            pltpu.VMEM((3, 2, width), F32),
            pltpu.VMEM((3 + F, 2, width), F32),
            pltpu.VMEM((F, 2, share), F32),
            dma((2,)),
            dma((2,)),
            dma((2,)),
            dma((288,)),
            dma((F, C, 2)),
            dma((F, C, len(PIECES))),
            dma((3 + F,)),
        ] + reduce_scratch(F, rows, width, PARTS, 2, per_rank),
        compiler_params=pltpu.CompilerParams(
            collective_id=2, has_side_effects=True, vmem_limit_bytes=60 * 1024 * 1024
        ),
    )(mixed, w_out, w_in, x, go, gains, qkv, attended, totals, place, turn, cosine, sine, hid_all, go_all, gates)


TURN_ROWS = 192


def turn_kernel(ff, src, rows_ref, out, rows_out, in_buf, out_buf, row_buf, wide_buf, in_sems, out_sems, row_sems, wide_sems):
    F, C = src.shape[0], src.shape[1]
    share = src.shape[3]
    steps = []
    base = 0
    in_order = list(range(C))
    ff_order = [cb for _, cb in sorted((ff_chunk(C, 0, cb), cb) for cb in in_order)]
    for row, size, devices in (
        (0, HEAD, in_order), (HEAD, HEAD, in_order), (2 * HEAD, HEAD, in_order),
        (3 * HEAD, ff, ff_order), (3 * HEAD + ff, ff, ff_order),
    ):
        for fb in range(F):
            steps.append((fb, row, size, base + fb * C * size, devices))
        base += F * C * size

    def fetch(i):
        fb, row, size, _, devices = steps[i]
        return [
            pltpu.make_async_copy(
                src.at[fb, cb, pl.ds(row, size)], in_buf.at[i % 2, j, pl.ds(0, size)], in_sems.at[i % 2, j]
            )
            for j, cb in enumerate(devices)
        ]

    def store(i):
        _, _, size, col, _ = steps[i]
        return pltpu.make_async_copy(
            out_buf.at[i % 2, :, pl.ds(0, C * size)], out.at[:, pl.ds(col, C * size)], out_sems.at[i % 2]
        )

    def fetch_rows(i):
        return pltpu.make_async_copy(
            rows_ref.at[pl.ds(i * TURN_ROWS, TURN_ROWS)], row_buf.at[i % 2], row_sems.at[i % 2]
        )

    def store_rows(i):
        return pltpu.make_async_copy(
            wide_buf.at[i % 2], rows_out.at[pl.ds(i * TURN_ROWS, TURN_ROWS)], wide_sems.at[i % 2]
        )

    row_steps = rows_ref.shape[0] // TURN_ROWS
    done = 0
    for copy in fetch(0):
        copy.start()
    fetch_rows(0).start()
    for i, (fb, row, size, col, _) in enumerate(steps):
        if i + 1 < len(steps):
            for copy in fetch(i + 1):
                copy.start()
        until = (i + 1) * row_steps // len(steps)
        for j in range(done, until):
            if j + 1 < row_steps:
                fetch_rows(j + 1).start()
            fetch_rows(j).wait()
            if j >= 2:
                store_rows(j - 2).wait()
            wide_buf[j % 2] = row_buf[j % 2].astype(F32)
            store_rows(j).start()
        done = until
        for copy in fetch(i):
            copy.wait()
        if i >= 2:
            store(i - 2).wait()
        block = in_buf[i % 2, :, :size, :].reshape(C * size, share).astype(F32)
        out_buf[i % 2, :, : C * size] = block.T
        store(i).start()
    store(len(steps) - 2).wait()
    store(len(steps) - 1).wait()
    store_rows(row_steps - 2).wait()
    store_rows(row_steps - 1).wait()


def turn_blocks(blocks, out_rows, ff):
    F, C, per_rank, share = blocks.shape
    count, width = out_rows.shape
    any_ = pl.BlockSpec(memory_space=pl.ANY)
    dma = pltpu.SemaphoreType.DMA
    return pl.pallas_call(
        functools.partial(turn_kernel, ff),
        out_shape=(
            jax.ShapeDtypeStruct((share, F * C * per_rank), F32),
            jax.ShapeDtypeStruct((count, width), F32),
        ),
        in_specs=[any_, any_],
        out_specs=(any_, any_),
        scratch_shapes=[
            pltpu.VMEM((2, C, ff, share), BF16),
            pltpu.VMEM((2, share, C * ff), F32),
            pltpu.VMEM((2, TURN_ROWS, width), BF16),
            pltpu.VMEM((2, TURN_ROWS, width), F32),
            dma((2, C)),
            dma((2,)),
            dma((2,)),
            dma((2,)),
        ],
        compiler_params=pltpu.CompilerParams(vmem_limit_bytes=40 * 1024 * 1024),
    )(blocks, out_rows)


def tp_body(C, F, inputs, gain, bias, in_weight, out_weight, grad_out, lengths, order):
    rows, width = inputs.shape[1:]
    T = C * F
    ff = FF // T
    x = inputs[0]
    go = grad_out[0]

    count = lengths.shape[1] + order.shape[1]
    table = jnp.pad(jnp.concatenate([lengths, order], axis=1), ((0, 0), (0, 128 - count)))

    (
        go_all, hid_all, w_in, w_out, gains, qkv, gates, mixed, attended, totals, place, turn, cosine, sine
    ) = forward_all(x, go, gain[None], bias[None], table, in_weight, out_weight, C, F)
    result, grad_in, sums, blocks, out_rows = backward_all(
        mixed, w_out, w_in, x, go, gains, qkv, attended, totals, place, turn, cosine, sine, hid_all, go_all,
        gates, out_weight.shape[0], C, F,
    )
    in_weight_grad, out_weight_grad = turn_blocks(blocks, out_rows, ff)
    return (result[None], grad_in[None], in_weight_grad, out_weight_grad, sums[0], sums[1])


def solution(mesh):
    in_specs = (
        P("fsdp", "ctx", None),
        P("fsdp"),
        P("fsdp"),
        P("fsdp", None),
        P("fsdp", None),
        P("fsdp", "ctx", None),
        P("fsdp", None),
        P("fsdp", None),
    )
    out_specs = (
        P("fsdp", "ctx", None),
        P("fsdp", "ctx", None),
        P("fsdp", None),
        P("fsdp", None),
        P("fsdp"),
        P("fsdp"),
    )
    C, F = mesh.shape["ctx"], mesh.shape["fsdp"]
    if (C, F) == (8, 4):
        work = functools.partial(tp_body, C, F)
    else:
        work = body
    return jax.shard_map(work, mesh=mesh, in_specs=in_specs, out_specs=out_specs, check_vma=False)
```
